512 devices in a mesh: dp: 8 (over y, core), expert: 64 (over x, z).
Axes of the slice: x: 4, y: 4, z: 16, core: 2. Of those that a mesh axis runs over, the one named last changes fastest.
Arguments:
- pre_query: bfloat16 [8192, 16, 576], P(('dp', 'expert')), may hold values from -25 to 25
- pre_latent: bfloat16 [8192, 576], P(('dp', 'expert')), may hold values from -5 to 5
- pre_resid: bfloat16 [8192, 2048], P(('dp', 'expert')), may hold values from -6 to 6
- dec_query: bfloat16 [512, 16, 576], P(('dp', 'expert')), may hold values from -25 to 25
- dec_latent: bfloat16 [512, 576], P(('dp', 'expert')), may hold values from -5 to 5
- dec_resid: bfloat16 [512, 2048], P(('dp', 'expert')), may hold values from -6 to 6
- cache_lengths: int32 [512], P(('dp', 'expert')), may hold values from 1 to 32768
- latent_cache: bfloat16 [512, 1024, 576], P(('dp', 'expert')), may hold values from -5 to 5
- sink_logits: float32 [16], replicated, may hold values from -1 to 3
- uv_weight: bfloat16 [16, 512, 128], P('dp', 'expert'), may hold values from -0.25 to 0.25
- out_weight: bfloat16 [16, 128, 2048], P('dp', 'expert'), may hold values from -0.125 to 0.125
- norm_gain: bfloat16 [2048], replicated, may hold values from 0.5 to 1.5
- router: bfloat16 [2048, 64], P(None, 'expert'), may hold values from -0.125 to 0.125
- routes: int32 [8704, 6], P(('dp', 'expert')), may hold values from 0 to 63, all different within a row; in each aligned block of 17 rows (0 to 16, 17 to 33, ...) at most 2 rows name the same one
- gate_weight: bfloat16 [64, 2048, 1408], P('expert', None, 'dp'), may hold values from -0.125 to 0.125
- up_weight: bfloat16 [64, 2048, 1408], P('expert', None, 'dp'), may hold values from -0.125 to 0.125
- down_weight: bfloat16 [64, 1408, 2048], P('expert', None, 'dp'), may hold values from -0.15625 to 0.15625
- shared_gate: bfloat16 [2048, 1408], P('expert', 'dp'), may hold values from -0.125 to 0.125
- shared_up: bfloat16 [2048, 1408], P('expert', 'dp'), may hold values from -0.125 to 0.125
- shared_down: bfloat16 [1408, 2048], P('expert', 'dp'), may hold values from -0.15625 to 0.15625
Outputs:
- pre_out: bfloat16 [8192, 2048], P(('dp', 'expert'))
- dec_out: bfloat16 [512, 2048], P(('dp', 'expert'))
The draws below stay inside these ranges and needn't reach their ends.
Inputs may be any that keep to these rules, and one draw needn't show every extreme that they name: `routes`: each row names 6 different experts; in each aligned block of 17 rows no expert is named by more than 2 rows.
All inputs are finite; a program needn't handle non-finite values.
Results may differ from the reference program's by a relative error of at most 0.015.
Values may be sent and summed in bfloat16 or wider, within the bound.
A program may use at most 64 MiB of HBM per device.

```python
import math
from functools import partial
import jax
import jax.numpy as jnp
import numpy as np
from jax import lax

D = 2048
HEADS = 16
LATENT = 512
ROPE = 64
QK_NOPE = 128
VDIM = 128
MOE_FF = 1408
TOPK = 6
SHARED_FF = 1408
WINDOW = 1024
SPAN = 16
MAXLEN = 32768
EXPERTS = 64
QK = 576
HEADS_GROUP = 2
ROWS_DEV = 17
CAP = 2
REQUESTS = 512
PRE_TOKENS = 8192
ROUTED_ROWS = 8704
N_DP = 8


def prefill_pair(key):
    latent = jnp.clip(jax.random.normal(jax.random.fold_in(key, 11), (PRE_TOKENS, QK), jnp.float32), -5.0, 5.0)
    query = jnp.clip(jax.random.normal(jax.random.fold_in(key, 12), (PRE_TOKENS, HEADS, QK), jnp.float32), -5.0, 5.0)
    return (query, latent)


def draw_pre_query(key, part):
    return prefill_pair(key)[0].astype(jnp.bfloat16)


def draw_pre_latent(key, part):
    return prefill_pair(key)[1].astype(jnp.bfloat16)


def decode_lengths(key):
    bits = jax.random.randint(jax.random.fold_in(key, 21), (REQUESTS,), 1, 16)
    upper = jnp.power(2, bits) + 1
    lengths = jax.random.randint(jax.random.fold_in(key, 22), (REQUESTS,), 1, upper)
    longest = jax.random.randint(jax.random.fold_in(key, 23), (), 0, REQUESTS)
    return lengths.at[longest].set(MAXLEN).astype(jnp.int32)


def decode_latent_base(key):
    return jnp.clip(jax.random.normal(jax.random.fold_in(key, 32), (REQUESTS, QK), jnp.float32), -5.0, 5.0)


def draw_cache_lengths(key, part):
    return decode_lengths(key)


def draw_dec_latent(key, part):
    return decode_latent_base(key).astype(jnp.bfloat16)


def draw_dec_query(key, part):
    query = jnp.clip(jax.random.normal(jax.random.fold_in(key, 33), (REQUESTS, HEADS, QK), jnp.float32), -5.0, 5.0)
    return query.astype(jnp.bfloat16)


def draw_latent_cache(key, part):
    return jnp.clip(jax.random.normal(jax.random.fold_in(key, 42), (REQUESTS, WINDOW, QK), jnp.float32), -5.0, 5.0).astype(jnp.bfloat16)


def block_levels(key, extent, pieces, smallest, high):
    gain = 1.0
    for axis_at, blocks in pieces:
        heights = jax.random.uniform(jax.random.fold_in(jax.random.fold_in(key, 6), axis_at), (blocks,), jnp.float32, smallest / len(pieces), high / len(pieces))
        gain = gain * jnp.repeat(jnp.exp(heights), extent[axis_at] // blocks).reshape((-1,) + (1,) * (len(extent) - 1 - axis_at))
    return gain


def routed_block(key, own, number, rows, number_of, top, bound, slope):
    sequence = jax.random.permutation(key, number_of)
    packed, ordinary = shares(number_of, rows * top, bound, slope, True), shares(number_of, rows * top, bound, slope, False)
    places = jnp.arange(number_of)

    def named(sizes, offset_by):
        used = int((sizes > 0).sum())
        fixed = max(1, used // 4)
        shifted = fixed + (places - fixed + offset_by * (used - fixed)) % max(1, number_of - fixed)
        return jnp.zeros((number_of,), jnp.int32).at[sequence[jnp.where(places < fixed, places, shifted)]].set(jnp.asarray(sizes, jnp.int32))

    sizes = jnp.where(number % 4 == 0, named(packed, number // 4), named(ordinary, number - number // 4 - 1))
    mixed = jax.random.permutation(jax.random.fold_in(own, 3), number_of)
    donor, taker = mixed[0:number_of // 2 * 2:2], mixed[1:number_of // 2 * 2:2]
    slack = jnp.minimum(sizes[donor] - 1, bound - sizes[taker]) // 2
    slack = jnp.where((donor == sequence[0]) | (taker == sequence[0]) | (sizes[taker] == 0), 0, jnp.maximum(slack, 0))
    shifted = jax.random.randint(jax.random.fold_in(own, 4), (number_of // 2,), 0, 1 << 20) % (slack + 1)
    sizes = sizes.at[donor].add(-shifted).at[taker].add(shifted)
    members = jnp.searchsorted(jnp.cumsum(sizes), jnp.arange(rows * top), side="right").astype(jnp.int32)
    listing = members.reshape(top, rows).T
    listing = listing[jax.random.permutation(jax.random.fold_in(own, 1), rows)]
    offset_by = jax.random.randint(jax.random.fold_in(own, 2), (rows, 1), 0, top)
    return jnp.take_along_axis(listing, (jnp.arange(top)[None, :] + offset_by) % top, axis=1)


def shares(count, total, bound, lean, full):
    portions = [(1 << 20) // math.isqrt(grade ** lean) + 1 for grade in range(1, count + 1)]
    largest = bound if full else min(bound, max(-(-total // count), total * portions[0] // sum(portions)))
    least = 1 if total - largest >= count - 1 else 0
    given, surplus = [largest] + [least] * (count - 1), total - largest - least * (count - 1)
    while surplus > 0:
        movable = [i for i in range(1, count) if given[i] < largest] or [i for i in range(1, count) if given[i] < bound]
        mass, left = sum([portions[i] for i in movable]), surplus
        for i in movable:
            addition = min(bound - given[i], max(1, left * portions[i] // mass), surplus)
            given[i] = given[i] + addition
            surplus = surplus - addition
    return np.array(given)


def centred(stream_key, dims, deviation, limit, shards=(), kind=jnp.bfloat16):
    level = block_levels(stream_key, dims, shards, -0.22, 0.18) if shards else 1.0
    result = jax.random.normal(stream_key, dims, jnp.float32) * deviation * level
    return jnp.minimum(jnp.maximum(result, -limit), limit).astype(kind)


def setup_inputs(seed: int = 0) -> dict:
    key_list = jax.random.split(jax.random.key(seed), 21)
    pre_query = draw_pre_query(jax.random.fold_in(key_list[20], 71), 0)
    pre_latent = draw_pre_latent(jax.random.fold_in(key_list[20], 71), 0)
    pre_resid = centred(key_list[2], (PRE_TOKENS, D), 1.0, 6.0, ((0, 512),))
    dec_query = draw_dec_query(jax.random.fold_in(key_list[20], 71), 0)
    dec_latent = draw_dec_latent(jax.random.fold_in(key_list[20], 71), 0)
    dec_resid = centred(key_list[5], (REQUESTS, D), 1.0, 6.0, ((0, 512),))
    cache_lengths = draw_cache_lengths(jax.random.fold_in(key_list[20], 71), 0)
    latent_cache = draw_latent_cache(jax.random.fold_in(key_list[20], 71), 0)
    sink_logits = jnp.clip(jax.random.uniform(key_list[8], (HEADS,), jnp.float32, -1.0, 3.0), -1.0, 3.0)
    uv_weight = centred(key_list[9], (HEADS, LATENT, VDIM), LATENT ** -0.5, 0.25, ((0, 8), (1, 64)))
    out_weight = centred(key_list[10], (HEADS, VDIM, D), (HEADS * VDIM) ** -0.5, 0.125, ((0, 8), (1, 64)))
    norm_gain = jnp.clip(1.0 + 0.1 * jax.random.normal(key_list[11], (D,), jnp.float32), 0.5, 1.5).astype(jnp.bfloat16)
    router = centred(key_list[12], (D, EXPERTS), D ** -0.5, 0.125, ((1, 64),))
    routes_keys = jax.random.split(jax.random.fold_in(key_list[13], 1), ROUTED_ROWS // ROWS_DEV)
    routes_turns = jax.random.permutation(jax.random.fold_in(key_list[13], 3), ROUTED_ROWS // ROWS_DEV)
    routes = jax.vmap(lambda own, number: routed_block(jax.random.fold_in(key_list[13], 2), own, number, ROWS_DEV, EXPERTS, TOPK, CAP, 2))(routes_keys, routes_turns).reshape((ROUTED_ROWS, TOPK))
    gate_weight = centred(key_list[14], (EXPERTS, D, MOE_FF), D ** -0.5, 0.125, ((0, 64), (2, 8)))
    up_weight = centred(key_list[15], (EXPERTS, D, MOE_FF), D ** -0.5, 0.125, ((0, 64), (2, 8)))
    down_weight = centred(key_list[16], (EXPERTS, MOE_FF, D), MOE_FF ** -0.5, 0.15625, ((0, 64), (2, 8)))
    shared_gate = centred(key_list[17], (D, SHARED_FF), D ** -0.5, 0.125, ((0, 64), (1, 8)))
    shared_up = centred(key_list[18], (D, SHARED_FF), D ** -0.5, 0.125, ((0, 64), (1, 8)))
    shared_down = centred(key_list[19], (SHARED_FF, D), SHARED_FF ** -0.5, 0.15625, ((0, 64), (1, 8)))
    return {"pre_query": pre_query, "pre_latent": pre_latent, "pre_resid": pre_resid, "dec_query": dec_query, "dec_latent": dec_latent, "dec_resid": dec_resid, "cache_lengths": cache_lengths, "latent_cache": latent_cache, "sink_logits": sink_logits, "uv_weight": uv_weight, "out_weight": out_weight, "norm_gain": norm_gain, "router": router, "routes": routes, "gate_weight": gate_weight, "up_weight": up_weight, "down_weight": down_weight, "shared_gate": shared_gate, "shared_up": shared_up, "shared_down": shared_down}


ROUTE_SCALE = 2.446
NORM_EPS = 1e-06
NEG_FILL = -1e+30
PRECISE = lax.Precision.HIGHEST

def rounded(value):
    return lax.optimization_barrier(value.astype(jnp.bfloat16)).astype(jnp.float32)

def attend_span(operands, sinks):
    query, latent = operands
    scale_qk = (QK_NOPE + ROPE) ** (-0.5)
    scores = jnp.einsum('thc,uc->thu', query.astype(jnp.float32), latent.astype(jnp.float32), precision=PRECISE) * scale_qk
    places = jnp.arange(SPAN, dtype=jnp.int32)
    allowed = (places[None, :] <= places[:, None])[:, None, :]
    masked = jnp.where(allowed, scores, NEG_FILL)
    row_max = jnp.maximum(lax.optimization_barrier(jnp.max(masked, axis=2)), sinks[None, :])
    exp_terms = jnp.where(allowed, jnp.exp(masked - row_max[:, :, None]), 0.0)
    denominator = lax.optimization_barrier(jnp.sum(exp_terms, axis=2)) + jnp.exp(sinks[None, :] - row_max)
    numerator = jnp.einsum('thu,ul->thl', rounded(exp_terms), latent[:, :LATENT].astype(jnp.float32), precision=PRECISE)
    return (numerator / denominator[:, :, None]).astype(jnp.bfloat16)

def attend_request(operands, sinks):
    query, cache_rows, own_key, length = operands
    scale_qk = (QK_NOPE + ROPE) ** (-0.5)
    slot_ids = jnp.arange(WINDOW, dtype=jnp.int32)
    newest = length - 1
    position = newest - jnp.mod(newest - slot_ids, WINDOW)
    usable = (position >= 0) & (position > length - WINDOW)
    usable = jnp.concatenate([usable, jnp.arange(1, dtype=jnp.int32) >= 0])
    keys = jnp.concatenate([cache_rows, own_key[None, :]], axis=0)
    scores = jnp.einsum('hc,uc->hu', query.astype(jnp.float32), keys.astype(jnp.float32), precision=PRECISE) * scale_qk
    masked = jnp.where(usable[None, :], scores, NEG_FILL)
    row_max = jnp.maximum(lax.optimization_barrier(jnp.max(masked, axis=1)), sinks)
    exp_terms = jnp.where(usable[None, :], jnp.exp(masked - row_max[:, None]), 0.0)
    denominator = lax.optimization_barrier(jnp.sum(exp_terms, axis=1)) + jnp.exp(sinks - row_max)
    numerator = jnp.einsum('hu,ul->hl', rounded(exp_terms), keys[:, :LATENT].astype(jnp.float32), precision=PRECISE)
    return (numerator / denominator[:, None]).astype(jnp.bfloat16)

def project(attention, uv_weight, out_weight):
    head_values = jnp.einsum('thl,hlv->thv', attention.astype(jnp.float32), uv_weight.astype(jnp.float32), precision=PRECISE).astype(jnp.bfloat16)
    summed = jnp.zeros((attention.shape[0], D), jnp.float32)
    for block in range(N_DP):
        lower = block * HEADS_GROUP
        partial_sum = jnp.einsum('thv,hvd->td', head_values[:, lower:lower + HEADS_GROUP].astype(jnp.float32), out_weight[lower:lower + HEADS_GROUP].astype(jnp.float32), precision=PRECISE)
        summed = summed + rounded(partial_sum)
    return summed

def normalize(hidden, norm_gain):
    hidden_up = hidden.astype(jnp.float32)
    mean_square = lax.optimization_barrier(jnp.mean(hidden_up * hidden_up, axis=1, keepdims=True))
    return (hidden_up * lax.rsqrt(mean_square + NORM_EPS) * norm_gain.astype(jnp.float32)[None, :]).astype(jnp.bfloat16)

def reference(pre_query, pre_latent, pre_resid, dec_query, dec_latent, dec_resid, cache_lengths, latent_cache, sink_logits, uv_weight, out_weight, norm_gain, router, routes, gate_weight, up_weight, down_weight, shared_gate, shared_up, shared_down):
    sinks = sink_logits.astype(jnp.float32)
    pre_att = lax.map(partial(attend_span, sinks=sinks), (pre_query.reshape(REQUESTS, SPAN, HEADS, QK), pre_latent.reshape(REQUESTS, SPAN, QK)))
    pre_att = pre_att.reshape(PRE_TOKENS, HEADS, LATENT)
    dec_att = lax.map(partial(attend_request, sinks=sinks), (dec_query, latent_cache, dec_latent, cache_lengths.astype(jnp.int32)))
    pre_hidden = (pre_resid.astype(jnp.float32) + project(pre_att, uv_weight, out_weight)).astype(jnp.bfloat16)
    dec_hidden = (dec_resid.astype(jnp.float32) + project(dec_att, uv_weight, out_weight)).astype(jnp.bfloat16)
    hidden_rows = jnp.concatenate([pre_hidden.reshape(REQUESTS, SPAN, D), dec_hidden.reshape(REQUESTS, 1, D)], axis=1).reshape(ROUTED_ROWS, D)
    normed_rows = normalize(hidden_rows, norm_gain)
    expert_ids = routes.reshape(-1).astype(jnp.int32)
    assignments = expert_ids.shape[0]
    order = jnp.argsort(expert_ids, stable=True).astype(jnp.int32)
    counts = lax.optimization_barrier(jnp.sum((expert_ids[:, None] == jnp.arange(EXPERTS, dtype=jnp.int32)[None, :]).astype(jnp.int32), axis=0))
    starts = jnp.cumsum(counts) - counts
    inverse = jnp.zeros((assignments,), jnp.int32).at[order].set(jnp.arange(assignments, dtype=jnp.int32))
    ranks = inverse - starts[expert_ids]
    most_rows = REQUESTS * CAP

    def run_expert(expert_index):
        picks = jnp.clip(starts[expert_index] + jnp.arange(most_rows, dtype=jnp.int32), 0, assignments - 1)
        token_index = order[picks] // TOPK
        rows = normed_rows[token_index]
        gate_proj = jnp.dot(rows, gate_weight[expert_index], preferred_element_type=jnp.float32)
        up_proj = jnp.dot(rows, up_weight[expert_index], preferred_element_type=jnp.float32)
        activation = (jax.nn.silu(gate_proj) * up_proj).astype(jnp.bfloat16)
        return jnp.dot(activation, down_weight[expert_index], preferred_element_type=jnp.float32).astype(jnp.bfloat16)
    outputs = lax.map(run_expert, jnp.arange(EXPERTS, dtype=jnp.int32))
    chosen = outputs[expert_ids, ranks].reshape(ROUTED_ROWS, TOPK, D)
    logits = jnp.dot(normed_rows, router, preferred_element_type=jnp.float32)
    scores = jax.nn.sigmoid(jnp.take_along_axis(logits, routes.astype(jnp.int32), axis=1))
    route_weight = ROUTE_SCALE * scores / lax.optimization_barrier(jnp.sum(scores, axis=1, keepdims=True))
    shared_act = (jax.nn.silu(jnp.dot(normed_rows, shared_gate, preferred_element_type=jnp.float32)) * jnp.dot(normed_rows, shared_up, preferred_element_type=jnp.float32)).astype(jnp.bfloat16)
    shared_out = jnp.dot(shared_act, shared_down, preferred_element_type=jnp.float32).astype(jnp.bfloat16)
    moe_sum = shared_out.astype(jnp.float32) + lax.optimization_barrier(jnp.sum(route_weight[:, :, None] * chosen.astype(jnp.float32), axis=1))
    final_rows = (hidden_rows.astype(jnp.float32) + moe_sum).astype(jnp.bfloat16).reshape(REQUESTS, ROWS_DEV, D)
    pre_out = final_rows[:, :SPAN].reshape(PRE_TOKENS, D)
    dec_out = final_rows[:, SPAN]
    return (pre_out, dec_out)
```

```python
from functools import partial

import jax
import jax.numpy as jnp
from jax import lax
from jax.sharding import PartitionSpec as P

D = 2048
LATENT = 512
ROPE = 64
QK_NOPE = 128
TOPK = 6


ROUTE_SCALE = 2.446
NORM_EPS = 1e-06
NEG_FILL = -1e30


def assign_slots(route_rows, experts):
    flat_routes = route_rows.reshape(-1)
    one_hot = (flat_routes[:, None] == jnp.arange(experts, dtype=jnp.int32)[None, :]).astype(
        jnp.int32
    )
    running = jnp.cumsum(one_hot, axis=0)
    slot_rank = jnp.sum(running * one_hot, axis=1) - 1
    return slot_rank.reshape(route_rows.shape)


def dispatch_matrix(route_rows, slot_rows, experts, capacity):
    target = route_rows * capacity + slot_rows
    places = jnp.arange(experts * capacity, dtype=jnp.int32)
    total = jnp.zeros((route_rows.shape[0], experts * capacity), jnp.bfloat16)
    for column in range(route_rows.shape[1]):
        total = total + (target[:, column][:, None] == places[None, :]).astype(jnp.bfloat16)
    return total


def gather_weights(members, **parts):
    names = list(parts)
    flat = jnp.concatenate([parts[n][0].reshape(-1) for n in names])
    lanes = 128
    total = flat.shape[0]
    padded = -(-total // lanes) * lanes
    flat = jnp.pad(flat, (0, padded - total)).reshape(1, padded // lanes, lanes)
    everyone = lax.all_gather(flat, "expert", axis=0, tiled=True).reshape(members, padded)
    out = {}
    start = 0
    for n in names:
        local, axis = parts[n]
        size = local.size
        piece = everyone[:, start : start + size].reshape((members,) + local.shape)
        piece = jnp.moveaxis(piece, 0, axis)
        shape = list(local.shape)
        shape[axis] *= members
        out[n] = piece.reshape(shape)
        start += size
    return out


def shards(
    pre_query,
    pre_latent,
    pre_resid,
    dec_query,
    dec_latent,
    dec_resid,
    cache_lengths,
    latent_cache,
    sink_logits,
    uv_weight,
    out_weight,
    norm_gain,
    router,
    routes,
    gate_weight,
    up_weight,
    down_weight,
    shared_gate,
    shared_up,
    shared_down,
):
    groups = lax.axis_size("dp")
    members = lax.axis_size("expert")
    pre_rows = pre_query.shape[0]
    rows_dev = pre_rows + 1
    scale_qk = (QK_NOPE + ROPE) ** (-0.5)
    weights = gather_weights(
        members,
        uv=(uv_weight, 1),
        out=(out_weight, 1),
        shared_gate=(shared_gate, 0),
        shared_up=(shared_up, 0),
        shared_down=(shared_down, 0),
    )
    pre_scores = (
        jnp.einsum("thc,uc->thu", pre_query, pre_latent, preferred_element_type=jnp.float32)
        * scale_qk
    )
    places = jnp.arange(pre_rows, dtype=jnp.int32)
    allowed = (places[None, :] <= places[:, None])[:, None, :]
    masked = jnp.where(allowed, pre_scores, NEG_FILL)
    pre_max = jnp.maximum(jnp.max(masked, axis=2), sink_logits[None, :])
    exp_terms = jnp.where(allowed, jnp.exp(masked - pre_max[:, :, None]), 0.0)
    denominator = jnp.sum(exp_terms, axis=2) + jnp.exp(sink_logits[None, :] - pre_max)
    numerator = jnp.einsum(
        "thu,ul->thl",
        exp_terms.astype(jnp.bfloat16),
        pre_latent[:, :LATENT],
        preferred_element_type=jnp.float32,
    )
    pre_att = (numerator / denominator[:, :, None]).astype(jnp.bfloat16)
    window = latent_cache.shape[1]
    slot_ids = jnp.arange(window, dtype=jnp.int32)
    newest = cache_lengths - 1
    position = newest[:, None] - jnp.mod(newest[:, None] - slot_ids[None, :], window)
    usable = ((position >= 0) & (position > cache_lengths[:, None] - window))[:, None, :]
    cache_scores = (
        jnp.einsum("rhc,rsc->rhs", dec_query, latent_cache, preferred_element_type=jnp.float32)
        * scale_qk
    )
    own_scores = (
        jnp.einsum("rhc,rc->rh", dec_query, dec_latent, preferred_element_type=jnp.float32)
        * scale_qk
    )
    cache_masked = jnp.where(usable, cache_scores, NEG_FILL)
    top_score = jnp.maximum(
        jnp.maximum(jnp.max(cache_masked, axis=2), own_scores), sink_logits[None, :]
    )
    cache_exp = jnp.where(usable, jnp.exp(cache_masked - top_score[:, :, None]), 0.0)
    own_exp = jnp.exp(own_scores - top_score)
    dec_numer = jnp.einsum(
        "rhs,rsl->rhl",
        cache_exp.astype(jnp.bfloat16),
        latent_cache[:, :, :LATENT],
        preferred_element_type=jnp.float32,
    )
    dec_numer = dec_numer + own_exp.astype(jnp.bfloat16).astype(jnp.float32)[
        :, :, None
    ] * dec_latent[:, None, :LATENT].astype(jnp.float32)
    dec_total = jnp.sum(cache_exp, axis=2) + own_exp + jnp.exp(sink_logits[None, :] - top_score)
    dec_att = (dec_numer / dec_total[:, :, None]).astype(jnp.bfloat16)
    attention = jnp.concatenate([pre_att, dec_att], axis=0)
    spread = lax.all_to_all(attention, "dp", split_axis=1, concat_axis=0, tiled=True)
    uv_full, out_full = weights["uv"], weights["out"]
    head_values = jnp.einsum(
        "thl,hlv->thv", spread, uv_full, preferred_element_type=jnp.float32
    ).astype(jnp.bfloat16)
    head_partial = jnp.einsum(
        "thv,hvd->td", head_values, out_full, preferred_element_type=jnp.float32
    )
    attn_out = lax.psum_scatter(
        head_partial.astype(jnp.bfloat16), "dp", scatter_dimension=0, tiled=True
    ).astype(jnp.float32)
    resid = jnp.concatenate([pre_resid, dec_resid], axis=0)
    hidden = (resid.astype(jnp.float32) + attn_out).astype(jnp.bfloat16)
    hidden_up = lax.optimization_barrier(hidden).astype(jnp.float32)
    mean_square = jnp.mean(hidden_up * hidden_up, axis=1, keepdims=True)
    normed = (
        hidden_up * lax.rsqrt(mean_square + NORM_EPS) * norm_gain.astype(jnp.float32)[None, :]
    ).astype(jnp.bfloat16)
    capacity = max(2, (rows_dev * TOPK + members - 1) // members)
    group_tokens = lax.all_gather(normed, "dp", axis=0, tiled=True)
    group_routes = lax.all_gather(routes, "dp", axis=0, tiled=True)
    routes_by_group = group_routes.reshape(groups, rows_dev, TOPK)
    slots_by_group = jax.vmap(partial(assign_slots, experts=members))(routes_by_group)
    tokens_by_group = group_tokens.reshape(groups, rows_dev, D)
    all_matrix = jax.vmap(partial(dispatch_matrix, experts=members, capacity=capacity))(
        routes_by_group, slots_by_group
    )
    all_matrix = all_matrix.reshape(groups, rows_dev, members, capacity)
    outgoing = jnp.einsum(
        "grxc,grd->xgcd", all_matrix, tokens_by_group, preferred_element_type=jnp.bfloat16
    )
    expert_rows = lax.all_to_all(outgoing, "expert", split_axis=0, concat_axis=0, tiled=True)
    expert_rows = expert_rows.reshape(-1, D)
    gate_score = jax.nn.sigmoid(
        jnp.dot(expert_rows, router[:, 0], preferred_element_type=jnp.float32)
    )
    gate_proj = jnp.dot(expert_rows, gate_weight[0], preferred_element_type=jnp.float32)
    up_proj = jnp.dot(expert_rows, up_weight[0], preferred_element_type=jnp.float32)
    expert_act = (jax.nn.silu(gate_proj) * up_proj).astype(jnp.bfloat16)
    shared_gate_full, shared_up_full, shared_down_full = (
        weights["shared_gate"],
        weights["shared_up"],
        weights["shared_down"],
    )
    shared_act = (
        jax.nn.silu(jnp.dot(group_tokens, shared_gate_full, preferred_element_type=jnp.float32))
        * jnp.dot(group_tokens, shared_up_full, preferred_element_type=jnp.float32)
    ).astype(jnp.bfloat16)
    down_local = down_weight[0]
    col_width = down_local.shape[1]
    routed_piece = lax.all_gather(expert_act, "dp", axis=1, tiled=True)
    shared_piece = lax.all_gather(shared_act, "dp", axis=1, tiled=True)
    routed_cols = jnp.dot(routed_piece, down_local, preferred_element_type=jnp.float32)
    shared_cols = jnp.dot(shared_piece, shared_down_full, preferred_element_type=jnp.float32)
    expert_out = routed_cols.astype(jnp.bfloat16)
    shared_out = shared_cols.astype(jnp.bfloat16)
    returned = lax.all_to_all(
        expert_out.reshape(members, groups * capacity, col_width),
        "expert",
        split_axis=0,
        concat_axis=0,
        tiled=True,
    )
    returned_scores = lax.all_to_all(
        gate_score.reshape(members, groups * capacity),
        "expert",
        split_axis=0,
        concat_axis=0,
        tiled=True,
    )
    group_offset = (jnp.arange(groups, dtype=jnp.int32) * capacity)[:, None, None]
    lookup = (routes_by_group * (groups * capacity) + group_offset + slots_by_group).reshape(
        groups * rows_dev, TOPK
    )
    picked = jnp.take(returned.reshape(-1, col_width), lookup, axis=0)
    picked_scores = jnp.take(returned_scores.reshape(-1), lookup, axis=0)
    route_weight = ROUTE_SCALE * picked_scores / jnp.sum(picked_scores, axis=1, keepdims=True)
    moe_cols = shared_out.astype(jnp.float32) + jnp.sum(
        route_weight[:, :, None] * picked.astype(jnp.float32), axis=1
    )
    moe_home = lax.all_to_all(
        moe_cols.reshape(groups, rows_dev, col_width).astype(jnp.bfloat16),
        "dp",
        split_axis=0,
        concat_axis=2,
        tiled=True,
    ).astype(jnp.float32)
    final = (hidden_up + moe_home[0]).astype(jnp.bfloat16)
    return (final[:pre_rows], final[pre_rows:])


def solution(mesh):
    in_specs = (
        P(("dp", "expert"), None, None),
        P(("dp", "expert"), None),
        P(("dp", "expert"), None),
        P(("dp", "expert"), None, None),
        P(("dp", "expert"), None),
        P(("dp", "expert"), None),
        P(("dp", "expert")),
        P(("dp", "expert"), None, None),
        P(),
        P("dp", "expert", None),
        P("dp", "expert", None),
        P(),
        P(None, "expert"),
        P(("dp", "expert"), None),
        P("expert", None, "dp"),
        P("expert", None, "dp"),
        P("expert", None, "dp"),
        P("expert", "dp"),
        P("expert", "dp"),
        P("expert", "dp"),
    )
    out_specs = (P(("dp", "expert"), None), P(("dp", "expert"), None))
    return jax.shard_map(shards, mesh=mesh, in_specs=in_specs, out_specs=out_specs, check_vma=False)
```

```python
from functools import partial

import jax
import jax.numpy as jnp
from jax import lax
from jax.sharding import PartitionSpec as P

D = 2048
LATENT = 512
ROPE = 64
QK_NOPE = 128
TOPK = 6


ROUTE_SCALE = 2.446
NORM_EPS = 1e-06
NEG_FILL = -1e30


def assign_slots(route_rows, experts):
    flat_routes = route_rows.reshape(-1)
    one_hot = (flat_routes[:, None] == jnp.arange(experts, dtype=jnp.int32)[None, :]).astype(
        jnp.int32
    )
    running = jnp.cumsum(one_hot, axis=0)
    slot_rank = jnp.sum(running * one_hot, axis=1) - 1
    return slot_rank.reshape(route_rows.shape)


def dispatch_matrix(route_rows, slot_rows, experts, capacity):
    target = route_rows * capacity + slot_rows
    places = jnp.arange(experts * capacity, dtype=jnp.int32)
    total = jnp.zeros((route_rows.shape[0], experts * capacity), jnp.bfloat16)
    for column in range(route_rows.shape[1]):
        total = total + (target[:, column][:, None] == places[None, :]).astype(jnp.bfloat16)
    return total


def gather_weights(members, **parts):
    names = list(parts)
    flat = jnp.concatenate([parts[n][0].reshape(-1) for n in names])
    lanes = 128
    total = flat.shape[0]
    padded = -(-total // lanes) * lanes
    flat = jnp.pad(flat, (0, padded - total)).reshape(1, padded // lanes, lanes)
    everyone = lax.all_gather(flat, "expert", axis=0, tiled=True).reshape(members, padded)
    out = {}
    start = 0
    for n in names:
        local, axis = parts[n]
        size = local.size
        piece = everyone[:, start : start + size].reshape((members,) + local.shape)
        piece = jnp.moveaxis(piece, 0, axis)
        shape = list(local.shape)
        shape[axis] *= members
        out[n] = piece.reshape(shape)
        start += size
    return out


def shards(
    pre_query,
    pre_latent,
    pre_resid,
    dec_query,
    dec_latent,
    dec_resid,
    cache_lengths,
    latent_cache,
    sink_logits,
    uv_weight,
    out_weight,
    norm_gain,
    router,
    routes,
    gate_weight,
    up_weight,
    down_weight,
    shared_gate,
    shared_up,
    shared_down,
):
    groups = lax.axis_size("dp")
    members = lax.axis_size("expert")
    pre_rows = pre_query.shape[0]
    rows_dev = pre_rows + 1
    scale_qk = (QK_NOPE + ROPE) ** (-0.5)
    weights = gather_weights(
        members,
        uv=(uv_weight, 1),
        out=(out_weight, 1),
        shared_gate=(shared_gate, 0),
        shared_up=(shared_up, 0),
        shared_down=(shared_down, 0),
    )
    pre_scores = (
        jnp.einsum("thc,uc->thu", pre_query, pre_latent, preferred_element_type=jnp.float32)
        * scale_qk
    )
    places = jnp.arange(pre_rows, dtype=jnp.int32)
    allowed = (places[None, :] <= places[:, None])[:, None, :]
    masked = jnp.where(allowed, pre_scores, NEG_FILL)
    pre_max = jnp.maximum(jnp.max(masked, axis=2), sink_logits[None, :])
    exp_terms = jnp.where(allowed, jnp.exp(masked - pre_max[:, :, None]), 0.0)
    denominator = jnp.sum(exp_terms, axis=2) + jnp.exp(sink_logits[None, :] - pre_max)
    numerator = jnp.einsum(
        "thu,ul->thl",
        exp_terms.astype(jnp.bfloat16),
        pre_latent[:, :LATENT],
        preferred_element_type=jnp.float32,
    )
    pre_att = (numerator / denominator[:, :, None]).astype(jnp.bfloat16)
    window = latent_cache.shape[1]
    slot_ids = jnp.arange(window, dtype=jnp.int32)
    newest = cache_lengths - 1
    position = newest[:, None] - jnp.mod(newest[:, None] - slot_ids[None, :], window)
    usable = ((position >= 0) & (position > cache_lengths[:, None] - window))[:, None, :]
    cache_scores = (
        jnp.einsum("rhc,rsc->rhs", dec_query, latent_cache, preferred_element_type=jnp.float32)
        * scale_qk
    )
    own_scores = (
        jnp.einsum("rhc,rc->rh", dec_query, dec_latent, preferred_element_type=jnp.float32)
        * scale_qk
    )
    cache_masked = jnp.where(usable, cache_scores, NEG_FILL)
    top_score = jnp.maximum(
        jnp.maximum(jnp.max(cache_masked, axis=2), own_scores), sink_logits[None, :]
    )
    cache_exp = jnp.where(usable, jnp.exp(cache_masked - top_score[:, :, None]), 0.0)
    own_exp = jnp.exp(own_scores - top_score)
    dec_numer = jnp.einsum(
        "rhs,rsl->rhl",
        cache_exp.astype(jnp.bfloat16),
        latent_cache[:, :, :LATENT],
        preferred_element_type=jnp.float32,
    )
    dec_numer = dec_numer + own_exp.astype(jnp.bfloat16).astype(jnp.float32)[
        :, :, None
    ] * dec_latent[:, None, :LATENT].astype(jnp.float32)
    dec_total = jnp.sum(cache_exp, axis=2) + own_exp + jnp.exp(sink_logits[None, :] - top_score)
    dec_att = (dec_numer / dec_total[:, :, None]).astype(jnp.bfloat16)
    attention = jnp.concatenate([pre_att, dec_att], axis=0)
    spread = lax.all_to_all(attention, "dp", split_axis=1, concat_axis=0, tiled=True)
    uv_full, out_full = weights["uv"], weights["out"]
    head_values = jnp.einsum(
        "thl,hlv->thv", spread, uv_full, preferred_element_type=jnp.float32
    ).astype(jnp.bfloat16)
    head_partial = jnp.einsum(
        "thv,hvd->td", head_values, out_full, preferred_element_type=jnp.float32
    )
    attn_out = lax.psum_scatter(
        head_partial.astype(jnp.bfloat16), "dp", scatter_dimension=0, tiled=True
    ).astype(jnp.float32)
    resid = jnp.concatenate([pre_resid, dec_resid], axis=0)
    hidden = (resid.astype(jnp.float32) + attn_out).astype(jnp.bfloat16)
    hidden_up = lax.optimization_barrier(hidden).astype(jnp.float32)
    mean_square = jnp.mean(hidden_up * hidden_up, axis=1, keepdims=True)
    normed = (
        hidden_up * lax.rsqrt(mean_square + NORM_EPS) * norm_gain.astype(jnp.float32)[None, :]
    ).astype(jnp.bfloat16)
    capacity = max(2, (rows_dev * TOPK + members - 1) // members)
    group_tokens = lax.all_gather(normed, "dp", axis=0, tiled=True)
    group_routes = lax.all_gather(routes, "dp", axis=0, tiled=True)
    routes_by_group = group_routes.reshape(groups, rows_dev, TOPK)
    slots_by_group = jax.vmap(partial(assign_slots, experts=members))(routes_by_group)
    own_slots = assign_slots(routes, members)
    own_matrix = dispatch_matrix(routes, own_slots, members, capacity).reshape(
        rows_dev, members, capacity
    )
    outgoing = jnp.einsum("rxc,rd->xcd", own_matrix, normed, preferred_element_type=jnp.bfloat16)
    arrived = lax.all_to_all(outgoing, "expert", split_axis=0, concat_axis=0, tiled=True)
    expert_rows = lax.all_gather(
        arrived.reshape(members, 1, capacity, D), "dp", axis=1, tiled=True
    )
    expert_rows = expert_rows.reshape(-1, D)
    gate_score = jax.nn.sigmoid(
        jnp.dot(expert_rows, router[:, 0], preferred_element_type=jnp.float32)
    )
    gate_proj = jnp.dot(expert_rows, gate_weight[0], preferred_element_type=jnp.float32)
    up_proj = jnp.dot(expert_rows, up_weight[0], preferred_element_type=jnp.float32)
    expert_act = (jax.nn.silu(gate_proj) * up_proj).astype(jnp.bfloat16)
    shared_gate_full, shared_up_full, shared_down_full = (
        weights["shared_gate"],
        weights["shared_up"],
        weights["shared_down"],
    )
    shared_act = (
        jax.nn.silu(jnp.dot(group_tokens, shared_gate_full, preferred_element_type=jnp.float32))
        * jnp.dot(group_tokens, shared_up_full, preferred_element_type=jnp.float32)
    ).astype(jnp.bfloat16)
    down_local = down_weight[0]
    col_width = down_local.shape[1]
    routed_piece = lax.all_gather(expert_act, "dp", axis=1, tiled=True)
    shared_piece = lax.all_gather(shared_act, "dp", axis=1, tiled=True)
    routed_cols = jnp.dot(routed_piece, down_local, preferred_element_type=jnp.float32)
    shared_cols = jnp.dot(shared_piece, shared_down_full, preferred_element_type=jnp.float32)
    expert_out = routed_cols.astype(jnp.bfloat16)
    shared_out = shared_cols.astype(jnp.bfloat16)
    returned = lax.all_to_all(
        expert_out.reshape(members, groups * capacity, col_width),
        "expert",
        split_axis=0,
        concat_axis=0,
        tiled=True,
    )
    returned_scores = lax.all_to_all(
        gate_score.reshape(members, groups * capacity),
        "expert",
        split_axis=0,
        concat_axis=0,
        tiled=True,
    )
    group_offset = (jnp.arange(groups, dtype=jnp.int32) * capacity)[:, None, None]
    lookup = (routes_by_group * (groups * capacity) + group_offset + slots_by_group).reshape(
        groups * rows_dev, TOPK
    )
    picked = jnp.take(returned.reshape(-1, col_width), lookup, axis=0)
    picked_scores = jnp.take(returned_scores.reshape(-1), lookup, axis=0)
    route_weight = ROUTE_SCALE * picked_scores / jnp.sum(picked_scores, axis=1, keepdims=True)
    moe_cols = shared_out.astype(jnp.float32) + jnp.sum(
        route_weight[:, :, None] * picked.astype(jnp.float32), axis=1
    )
    moe_home = lax.all_to_all(
        moe_cols.reshape(groups, rows_dev, col_width).astype(jnp.bfloat16),
        "dp",
        split_axis=0,
        concat_axis=2,
        tiled=True,
    ).astype(jnp.float32)
    final = (hidden_up + moe_home[0]).astype(jnp.bfloat16)
    return (final[:pre_rows], final[pre_rows:])


def solution(mesh):
    in_specs = (
        P(("dp", "expert"), None, None),
        P(("dp", "expert"), None),
        P(("dp", "expert"), None),
        P(("dp", "expert"), None, None),
        P(("dp", "expert"), None),
        P(("dp", "expert"), None),
        P(("dp", "expert")),
        P(("dp", "expert"), None, None),
        P(),
        P("dp", "expert", None),
        P("dp", "expert", None),
        P(),
        P(None, "expert"),
        P(("dp", "expert"), None),
        P("expert", None, "dp"),
        P("expert", None, "dp"),
        P("expert", None, "dp"),
        P("expert", "dp"),
        P("expert", "dp"),
        P("expert", "dp"),
    )
    out_specs = (P(("dp", "expert"), None), P(("dp", "expert"), None))
    return jax.shard_map(shards, mesh=mesh, in_specs=in_specs, out_specs=out_specs, check_vma=False)
```

```python
from functools import partial

import jax
import jax.numpy as jnp
from jax import lax
from jax.experimental import pallas as pl
from jax.experimental.pallas import tpu as pltpu
from jax.sharding import PartitionSpec as P

D = 2048
LATENT = 512
ROPE = 64
QK_NOPE = 128
TOPK = 6


ROUTE_SCALE = 2.446
NORM_EPS = 1e-06
NEG_FILL = -1e30


def assign_slots(route_rows, experts):
    flat_routes = route_rows.reshape(-1)
    one_hot = (flat_routes[:, None] == jnp.arange(experts, dtype=jnp.int32)[None, :]).astype(
        jnp.int32
    )
    running = jnp.cumsum(one_hot, axis=0)
    slot_rank = jnp.sum(running * one_hot, axis=1) - 1
    return slot_rank.reshape(route_rows.shape)


def dispatch_matrix(route_rows, slot_rows, experts, capacity):
    target = route_rows * capacity + slot_rows
    places = jnp.arange(experts * capacity, dtype=jnp.int32)
    total = jnp.zeros((route_rows.shape[0], experts * capacity), jnp.bfloat16)
    for column in range(route_rows.shape[1]):
        total = total + (target[:, column][:, None] == places[None, :]).astype(jnp.bfloat16)
    return total


MESH_ID = pl.DeviceIdType.MESH


def gather_kernel(nx, nz, shard_ref, out_ref, xs_sem, xr_sem, own_sem, rs_sem, ls_sem, rr_sem):
    d = lax.axis_index("dp")
    e = lax.axis_index("expert")
    x = e // nz
    z = e % nz
    right = x * nz + (z + 1) % nz
    left = x * nz + (z + nz - 1) % nz
    steps_r = nz // 2
    steps_l = nz - 1 - steps_r

    barrier = pltpu.get_barrier_semaphore()
    for k in range(1, nx):
        peer = ((x + k) % nx) * nz + z
        pl.semaphore_signal(barrier, 1, device_id=(d, peer), device_id_type=MESH_ID)
    greeted = nx - 1
    if nz > 1:
        pl.semaphore_signal(barrier, 1, device_id=(d, right), device_id_type=MESH_ID)
        greeted += 1
    if nz > 2:
        pl.semaphore_signal(barrier, 1, device_id=(d, left), device_id_type=MESH_ID)
        greeted += 1
    if greeted:
        pl.semaphore_wait(barrier, greeted)

    own = pltpu.make_async_copy(shard_ref, out_ref.at[z, x], own_sem)
    own.start()
    x_copies = []
    for k in range(1, nx):
        px = (x + k) % nx
        send = pltpu.make_async_remote_copy(
            src_ref=shard_ref,
            dst_ref=out_ref.at[z, x],
            send_sem=xs_sem.at[k],
            recv_sem=xr_sem.at[x],
            device_id=(d, px * nz + z),
            device_id_type=MESH_ID,
        )
        send.start()
        x_copies.append(send)
    own.wait()
    for k in range(1, nx):
        px = (x + k) % nx
        incoming = pltpu.make_async_remote_copy(
            src_ref=shard_ref,
            dst_ref=out_ref.at[z, px],
            send_sem=xs_sem.at[k],
            recv_sem=xr_sem.at[px],
            device_id=(d, px * nz + z),
            device_id_type=MESH_ID,
        )
        incoming.wait_recv()

    def ring_copy(group, sems, step, target):
        return pltpu.make_async_remote_copy(
            src_ref=out_ref.at[group],
            dst_ref=out_ref.at[group],
            send_sem=sems.at[step],
            recv_sem=rr_sem.at[group],
            device_id=(d, target),
            device_id_type=MESH_ID,
        )

    sent = []
    for s in range(max(steps_r, steps_l)):
        if s < steps_r:
            group = (z - s + nz) % nz
            if s > 0:
                ring_copy(group, rs_sem, s, right).wait_recv()
            c = ring_copy(group, rs_sem, s, right)
            c.start()
            sent.append(c)
        if s < steps_l:
            group = (z + s) % nz
            if s > 0:
                ring_copy(group, ls_sem, s, left).wait_recv()
            c = ring_copy(group, ls_sem, s, left)
            c.start()
            sent.append(c)
    if steps_r > 0:
        ring_copy((z - steps_r + nz) % nz, rs_sem, 0, right).wait_recv()
    if steps_l > 0:
        ring_copy((z + steps_l) % nz, ls_sem, 0, left).wait_recv()
    for c in sent:
        c.wait_send()
    for c in x_copies:
        c.wait_send()


def expert_gather(flat, members):
    nz = 16 if members % 16 == 0 else members
    nx = members // nz
    rows, lanes = flat.shape
    steps = max(nz // 2, 1)
    out = pl.pallas_call(
        partial(gather_kernel, nx, nz),
        out_shape=jax.ShapeDtypeStruct((nz, nx, rows, lanes), flat.dtype),
        in_specs=[pl.BlockSpec(memory_space=pltpu.VMEM)],
        out_specs=pl.BlockSpec(memory_space=pltpu.VMEM),
        scratch_shapes=[
            pltpu.SemaphoreType.DMA((max(nx, 1),)),
            pltpu.SemaphoreType.DMA((max(nx, 1),)),
            pltpu.SemaphoreType.DMA(()),
            pltpu.SemaphoreType.DMA((steps,)),
            pltpu.SemaphoreType.DMA((steps,)),
            pltpu.SemaphoreType.DMA((nz,)),
        ],
        compiler_params=pltpu.CompilerParams(collective_id=0, has_side_effects=True),
    )(flat)
    return jnp.swapaxes(out, 0, 1).reshape(members, rows * lanes)


def gather_weights(members, **parts):
    names = list(parts)
    flat = jnp.concatenate([parts[n][0].reshape(-1) for n in names])
    lanes = 128
    total = flat.shape[0]
    padded = -(-total // (lanes * 8)) * lanes * 8
    flat = jnp.pad(flat, (0, padded - total)).reshape(padded // lanes, lanes)
    everyone = expert_gather(flat, members)
    out = {}
    start = 0
    for n in names:
        local, axis = parts[n]
        size = local.size
        piece = everyone[:, start : start + size].reshape((members,) + local.shape)
        piece = jnp.moveaxis(piece, 0, axis)
        shape = list(local.shape)
        shape[axis] *= members
        out[n] = piece.reshape(shape)
        start += size
    return out


def shards(
    pre_query,
    pre_latent,
    pre_resid,
    dec_query,
    dec_latent,
    dec_resid,
    cache_lengths,
    latent_cache,
    sink_logits,
    uv_weight,
    out_weight,
    norm_gain,
    router,
    routes,
    gate_weight,
    up_weight,
    down_weight,
    shared_gate,
    shared_up,
    shared_down,
):
    groups = lax.axis_size("dp")
    members = lax.axis_size("expert")
    pre_rows = pre_query.shape[0]
    rows_dev = pre_rows + 1
    scale_qk = (QK_NOPE + ROPE) ** (-0.5)
    weights = gather_weights(
        members,
        uv=(uv_weight, 1),
        out=(out_weight, 1),
        shared_gate=(shared_gate, 0),
        shared_up=(shared_up, 0),
        shared_down=(shared_down, 0),
    )
    pre_scores = (
        jnp.einsum("thc,uc->thu", pre_query, pre_latent, preferred_element_type=jnp.float32)
        * scale_qk
    )
    places = jnp.arange(pre_rows, dtype=jnp.int32)
    allowed = (places[None, :] <= places[:, None])[:, None, :]
    masked = jnp.where(allowed, pre_scores, NEG_FILL)
    pre_max = jnp.maximum(jnp.max(masked, axis=2), sink_logits[None, :])
    exp_terms = jnp.where(allowed, jnp.exp(masked - pre_max[:, :, None]), 0.0)
    denominator = jnp.sum(exp_terms, axis=2) + jnp.exp(sink_logits[None, :] - pre_max)
    numerator = jnp.einsum(
        "thu,ul->thl",
        exp_terms.astype(jnp.bfloat16),
        pre_latent[:, :LATENT],
        preferred_element_type=jnp.float32,
    )
    pre_att = (numerator / denominator[:, :, None]).astype(jnp.bfloat16)
    window = latent_cache.shape[1]
    slot_ids = jnp.arange(window, dtype=jnp.int32)
    newest = cache_lengths - 1
    position = newest[:, None] - jnp.mod(newest[:, None] - slot_ids[None, :], window)
    usable = ((position >= 0) & (position > cache_lengths[:, None] - window))[:, None, :]
    cache_scores = (
        jnp.einsum("rhc,rsc->rhs", dec_query, latent_cache, preferred_element_type=jnp.float32)
        * scale_qk
    )
    own_scores = (
        jnp.einsum("rhc,rc->rh", dec_query, dec_latent, preferred_element_type=jnp.float32)
        * scale_qk
    )
    cache_masked = jnp.where(usable, cache_scores, NEG_FILL)
    top_score = jnp.maximum(
        jnp.maximum(jnp.max(cache_masked, axis=2), own_scores), sink_logits[None, :]
    )
    cache_exp = jnp.where(usable, jnp.exp(cache_masked - top_score[:, :, None]), 0.0)
    own_exp = jnp.exp(own_scores - top_score)
    dec_numer = jnp.einsum(
        "rhs,rsl->rhl",
        cache_exp.astype(jnp.bfloat16),
        latent_cache[:, :, :LATENT],
        preferred_element_type=jnp.float32,
    )
    dec_numer = dec_numer + own_exp.astype(jnp.bfloat16).astype(jnp.float32)[
        :, :, None
    ] * dec_latent[:, None, :LATENT].astype(jnp.float32)
    dec_total = jnp.sum(cache_exp, axis=2) + own_exp + jnp.exp(sink_logits[None, :] - top_score)
    dec_att = (dec_numer / dec_total[:, :, None]).astype(jnp.bfloat16)
    attention = jnp.concatenate([pre_att, dec_att], axis=0)
    spread = lax.all_to_all(attention, "dp", split_axis=1, concat_axis=0, tiled=True)
    uv_full, out_full = weights["uv"], weights["out"]
    head_values = jnp.einsum(
        "thl,hlv->thv", spread, uv_full, preferred_element_type=jnp.float32
    ).astype(jnp.bfloat16)
    head_partial = jnp.einsum(
        "thv,hvd->td", head_values, out_full, preferred_element_type=jnp.float32
    )
    attn_out = lax.psum_scatter(
        head_partial.astype(jnp.bfloat16), "dp", scatter_dimension=0, tiled=True
    ).astype(jnp.float32)
    resid = jnp.concatenate([pre_resid, dec_resid], axis=0)
    hidden = (resid.astype(jnp.float32) + attn_out).astype(jnp.bfloat16)
    hidden_up = lax.optimization_barrier(hidden).astype(jnp.float32)
    mean_square = jnp.mean(hidden_up * hidden_up, axis=1, keepdims=True)
    normed = (
        hidden_up * lax.rsqrt(mean_square + NORM_EPS) * norm_gain.astype(jnp.float32)[None, :]
    ).astype(jnp.bfloat16)
    capacity = max(2, (rows_dev * TOPK + members - 1) // members)
    group_tokens = lax.all_gather(normed, "dp", axis=0, tiled=True)
    group_routes = lax.all_gather(routes, "dp", axis=0, tiled=True)
    routes_by_group = group_routes.reshape(groups, rows_dev, TOPK)
    slots_by_group = jax.vmap(partial(assign_slots, experts=members))(routes_by_group)
    own_slots = assign_slots(routes, members)
    own_matrix = dispatch_matrix(routes, own_slots, members, capacity).reshape(
        rows_dev, members, capacity
    )
    outgoing = jnp.einsum("rxc,rd->xcd", own_matrix, normed, preferred_element_type=jnp.bfloat16)
    arrived = lax.all_to_all(outgoing, "expert", split_axis=0, concat_axis=0, tiled=True)
    expert_rows = lax.all_gather(
        arrived.reshape(members, 1, capacity, D), "dp", axis=1, tiled=True
    )
    expert_rows = expert_rows.reshape(-1, D)
    gate_score = jax.nn.sigmoid(
        jnp.dot(expert_rows, router[:, 0], preferred_element_type=jnp.float32)
    )
    gate_proj = jnp.dot(expert_rows, gate_weight[0], preferred_element_type=jnp.float32)
    up_proj = jnp.dot(expert_rows, up_weight[0], preferred_element_type=jnp.float32)
    expert_act = (jax.nn.silu(gate_proj) * up_proj).astype(jnp.bfloat16)
    shared_gate_full, shared_up_full, shared_down_full = (
        weights["shared_gate"],
        weights["shared_up"],
        weights["shared_down"],
    )
    shared_act = (
        jax.nn.silu(jnp.dot(group_tokens, shared_gate_full, preferred_element_type=jnp.float32))
        * jnp.dot(group_tokens, shared_up_full, preferred_element_type=jnp.float32)
    ).astype(jnp.bfloat16)
    down_local = down_weight[0]
    col_width = down_local.shape[1]
    routed_piece = lax.all_gather(expert_act, "dp", axis=1, tiled=True)
    shared_piece = lax.all_gather(shared_act, "dp", axis=1, tiled=True)
    routed_cols = jnp.dot(routed_piece, down_local, preferred_element_type=jnp.float32)
    shared_cols = jnp.dot(shared_piece, shared_down_full, preferred_element_type=jnp.float32)
    expert_out = routed_cols.astype(jnp.bfloat16)
    shared_out = shared_cols.astype(jnp.bfloat16)
    returned = lax.all_to_all(
        expert_out.reshape(members, groups * capacity, col_width),
        "expert",
        split_axis=0,
        concat_axis=0,
        tiled=True,
    )
    returned_scores = lax.all_to_all(
        gate_score.reshape(members, groups * capacity),
        "expert",
        split_axis=0,
        concat_axis=0,
        tiled=True,
    )
    group_offset = (jnp.arange(groups, dtype=jnp.int32) * capacity)[:, None, None]
    lookup = (routes_by_group * (groups * capacity) + group_offset + slots_by_group).reshape(
        groups * rows_dev, TOPK
    )
    picked = jnp.take(returned.reshape(-1, col_width), lookup, axis=0)
    picked_scores = jnp.take(returned_scores.reshape(-1), lookup, axis=0)
    route_weight = ROUTE_SCALE * picked_scores / jnp.sum(picked_scores, axis=1, keepdims=True)
    moe_cols = shared_out.astype(jnp.float32) + jnp.sum(
        route_weight[:, :, None] * picked.astype(jnp.float32), axis=1
    )
    moe_home = lax.all_to_all(
        moe_cols.reshape(groups, rows_dev, col_width).astype(jnp.bfloat16),
        "dp",
        split_axis=0,
        concat_axis=2,
        tiled=True,
    ).astype(jnp.float32)
    final = (hidden_up + moe_home[0]).astype(jnp.bfloat16)
    return (final[:pre_rows], final[pre_rows:])


def solution(mesh):
    in_specs = (
        P(("dp", "expert"), None, None),
        P(("dp", "expert"), None),
        P(("dp", "expert"), None),
        P(("dp", "expert"), None, None),
        P(("dp", "expert"), None),
        P(("dp", "expert"), None),
        P(("dp", "expert")),
        P(("dp", "expert"), None, None),
        P(),
        P("dp", "expert", None),
        P("dp", "expert", None),
        P(),
        P(None, "expert"),
        P(("dp", "expert"), None),
        P("expert", None, "dp"),
        P("expert", None, "dp"),
        P("expert", None, "dp"),
        P("expert", "dp"),
        P("expert", "dp"),
        P("expert", "dp"),
    )
    out_specs = (P(("dp", "expert"), None), P(("dp", "expert"), None))
    return jax.shard_map(shards, mesh=mesh, in_specs=in_specs, out_specs=out_specs, check_vma=False)
```

```python
from functools import partial

import jax
import jax.numpy as jnp
from jax import lax
from jax.experimental import pallas as pl
from jax.experimental.pallas import tpu as pltpu
from jax.sharding import PartitionSpec as P

D = 2048
LATENT = 512
ROPE = 64
QK_NOPE = 128
TOPK = 6


ROUTE_SCALE = 2.446
NORM_EPS = 1e-06
NEG_FILL = -1e30


def assign_slots(route_rows, experts):
    flat_routes = route_rows.reshape(-1)
    one_hot = (flat_routes[:, None] == jnp.arange(experts, dtype=jnp.int32)[None, :]).astype(
        jnp.int32
    )
    running = jnp.cumsum(one_hot, axis=0)
    slot_rank = jnp.sum(running * one_hot, axis=1) - 1
    return slot_rank.reshape(route_rows.shape)


def dispatch_matrix(route_rows, slot_rows, experts, capacity):
    target = route_rows * capacity + slot_rows
    places = jnp.arange(experts * capacity, dtype=jnp.int32)
    total = jnp.zeros((route_rows.shape[0], experts * capacity), jnp.bfloat16)
    for column in range(route_rows.shape[1]):
        total = total + (target[:, column][:, None] == places[None, :]).astype(jnp.bfloat16)
    return total


MESH_ID = pl.DeviceIdType.MESH


def gather_kernel(nx, nz, shard_ref, out_ref, xs_sem, xr_sem, own_sem, rs_sem, ls_sem, rr_sem):
    d = lax.axis_index("dp")
    e = lax.axis_index("expert")
    x = e // nz
    z = e % nz
    right = x * nz + (z + 1) % nz
    left = x * nz + (z + nz - 1) % nz
    steps_r = nz // 2
    steps_l = nz - 1 - steps_r

    barrier = pltpu.get_barrier_semaphore()
    for k in range(1, nx):
        peer = ((x + k) % nx) * nz + z
        pl.semaphore_signal(barrier, 1, device_id=(d, peer), device_id_type=MESH_ID)
    greeted = nx - 1
    if nz > 1:
        pl.semaphore_signal(barrier, 1, device_id=(d, right), device_id_type=MESH_ID)
        greeted += 1
    if nz > 2:
        pl.semaphore_signal(barrier, 1, device_id=(d, left), device_id_type=MESH_ID)
        greeted += 1
    if greeted:
        pl.semaphore_wait(barrier, greeted)

    own = pltpu.make_async_copy(shard_ref, out_ref.at[z, x], own_sem)
    own.start()
    x_copies = []
    for k in range(1, nx):
        px = (x + k) % nx
        send = pltpu.make_async_remote_copy(
            src_ref=shard_ref,
            dst_ref=out_ref.at[z, x],
            send_sem=xs_sem.at[k],
            recv_sem=xr_sem.at[x],
            device_id=(d, px * nz + z),
            device_id_type=MESH_ID,
        )
        send.start()
        x_copies.append(send)
    own.wait()
    for k in range(1, nx):
        px = (x + k) % nx
        incoming = pltpu.make_async_remote_copy(
            src_ref=shard_ref,
            dst_ref=out_ref.at[z, px],
            send_sem=xs_sem.at[k],
            recv_sem=xr_sem.at[px],
            device_id=(d, px * nz + z),
            device_id_type=MESH_ID,
        )
        incoming.wait_recv()

    def ring_copy(group, sems, step, target):
        return pltpu.make_async_remote_copy(
            src_ref=out_ref.at[group],
            dst_ref=out_ref.at[group],
            send_sem=sems.at[step],
            recv_sem=rr_sem.at[group],
            device_id=(d, target),
            device_id_type=MESH_ID,
        )

    sent = []
    for s in range(max(steps_r, steps_l)):
        if s < steps_r:
            group = (z - s + nz) % nz
            if s > 0:
                ring_copy(group, rs_sem, s, right).wait_recv()
            c = ring_copy(group, rs_sem, s, right)
            c.start()
            sent.append(c)
        if s < steps_l:
            group = (z + s) % nz
            if s > 0:
                ring_copy(group, ls_sem, s, left).wait_recv()
            c = ring_copy(group, ls_sem, s, left)
            c.start()
            sent.append(c)
    if steps_r > 0:
        ring_copy((z - steps_r + nz) % nz, rs_sem, 0, right).wait_recv()
    if steps_l > 0:
        ring_copy((z + steps_l) % nz, ls_sem, 0, left).wait_recv()
    for c in sent:
        c.wait_send()
    for c in x_copies:
        c.wait_send()


def expert_gather(flat, members):
    nz = 16 if members % 16 == 0 else members
    nx = members // nz
    rows, lanes = flat.shape
    steps = max(nz // 2, 1)
    out = pl.pallas_call(
        partial(gather_kernel, nx, nz),
        out_shape=jax.ShapeDtypeStruct((nz, nx, rows, lanes), flat.dtype),
        in_specs=[pl.BlockSpec(memory_space=pltpu.VMEM)],
        out_specs=pl.BlockSpec(memory_space=pltpu.VMEM),
        scratch_shapes=[
            pltpu.SemaphoreType.DMA((max(nx, 1),)),
            pltpu.SemaphoreType.DMA((max(nx, 1),)),
            pltpu.SemaphoreType.DMA(()),
            pltpu.SemaphoreType.DMA((steps,)),
            pltpu.SemaphoreType.DMA((steps,)),
            pltpu.SemaphoreType.DMA((nz,)),
        ],
        compiler_params=pltpu.CompilerParams(collective_id=0, has_side_effects=True),
    )(flat)
    return jnp.swapaxes(out, 0, 1).reshape(members, rows * lanes)


def gather_weights(members, by_kernel, **parts):
    names = list(parts)
    flat = jnp.concatenate([parts[n][0].reshape(-1) for n in names])
    lanes = 128
    total = flat.shape[0]
    padded = -(-total // (lanes * 8)) * lanes * 8
    flat = jnp.pad(flat, (0, padded - total)).reshape(padded // lanes, lanes)
    if by_kernel:
        everyone = expert_gather(flat, members)
    else:
        everyone = lax.all_gather(flat[None], "expert", axis=0, tiled=True)
        everyone = everyone.reshape(members, padded)
    out = {}
    start = 0
    for n in names:
        local, axis = parts[n]
        size = local.size
        piece = everyone[:, start : start + size].reshape((members,) + local.shape)
        piece = jnp.moveaxis(piece, 0, axis)
        shape = list(local.shape)
        shape[axis] *= members
        out[n] = piece.reshape(shape)
        start += size
    return out


def shards(
    pre_query,
    pre_latent,
    pre_resid,
    dec_query,
    dec_latent,
    dec_resid,
    cache_lengths,
    latent_cache,
    sink_logits,
    uv_weight,
    out_weight,
    norm_gain,
    router,
    routes,
    gate_weight,
    up_weight,
    down_weight,
    shared_gate,
    shared_up,
    shared_down,
):
    groups = lax.axis_size("dp")
    members = lax.axis_size("expert")
    pre_rows = pre_query.shape[0]
    rows_dev = pre_rows + 1
    scale_qk = (QK_NOPE + ROPE) ** (-0.5)
    weights = gather_weights(
        members,
        True,
        uv=(uv_weight, 1),
        out=(out_weight, 1),
    )
    weights.update(
        gather_weights(
            members,
            False,
            shared_gate=(shared_gate, 0),
            shared_up=(shared_up, 0),
            shared_down=(shared_down, 0),
        )
    )
    pre_scores = (
        jnp.einsum("thc,uc->thu", pre_query, pre_latent, preferred_element_type=jnp.float32)
        * scale_qk
    )
    places = jnp.arange(pre_rows, dtype=jnp.int32)
    allowed = (places[None, :] <= places[:, None])[:, None, :]
    masked = jnp.where(allowed, pre_scores, NEG_FILL)
    pre_max = jnp.maximum(jnp.max(masked, axis=2), sink_logits[None, :])
    exp_terms = jnp.where(allowed, jnp.exp(masked - pre_max[:, :, None]), 0.0)
    denominator = jnp.sum(exp_terms, axis=2) + jnp.exp(sink_logits[None, :] - pre_max)
    numerator = jnp.einsum(
        "thu,ul->thl",
        exp_terms.astype(jnp.bfloat16),
        pre_latent[:, :LATENT],
        preferred_element_type=jnp.float32,
    )
    pre_att = (numerator / denominator[:, :, None]).astype(jnp.bfloat16)
    window = latent_cache.shape[1]
    slot_ids = jnp.arange(window, dtype=jnp.int32)
    newest = cache_lengths - 1
    position = newest[:, None] - jnp.mod(newest[:, None] - slot_ids[None, :], window)
    usable = ((position >= 0) & (position > cache_lengths[:, None] - window))[:, None, :]
    cache_scores = (
        jnp.einsum("rhc,rsc->rhs", dec_query, latent_cache, preferred_element_type=jnp.float32)
        * scale_qk
    )
    own_scores = (
        jnp.einsum("rhc,rc->rh", dec_query, dec_latent, preferred_element_type=jnp.float32)
        * scale_qk
    )
    cache_masked = jnp.where(usable, cache_scores, NEG_FILL)
    top_score = jnp.maximum(
        jnp.maximum(jnp.max(cache_masked, axis=2), own_scores), sink_logits[None, :]
    )
    cache_exp = jnp.where(usable, jnp.exp(cache_masked - top_score[:, :, None]), 0.0)
    own_exp = jnp.exp(own_scores - top_score)
    dec_numer = jnp.einsum(
        "rhs,rsl->rhl",
        cache_exp.astype(jnp.bfloat16),
        latent_cache[:, :, :LATENT],
        preferred_element_type=jnp.float32,
    )
    dec_numer = dec_numer + own_exp.astype(jnp.bfloat16).astype(jnp.float32)[
        :, :, None
    ] * dec_latent[:, None, :LATENT].astype(jnp.float32)
    dec_total = jnp.sum(cache_exp, axis=2) + own_exp + jnp.exp(sink_logits[None, :] - top_score)
    dec_att = (dec_numer / dec_total[:, :, None]).astype(jnp.bfloat16)
    attention = jnp.concatenate([pre_att, dec_att], axis=0)
    spread = lax.all_to_all(attention, "dp", split_axis=1, concat_axis=0, tiled=True)
    uv_full, out_full = weights["uv"], weights["out"]
    head_values = jnp.einsum(
        "thl,hlv->thv", spread, uv_full, preferred_element_type=jnp.float32
    ).astype(jnp.bfloat16)
    head_partial = jnp.einsum(
        "thv,hvd->td", head_values, out_full, preferred_element_type=jnp.float32
    )
    attn_out = lax.psum_scatter(
        head_partial.astype(jnp.bfloat16), "dp", scatter_dimension=0, tiled=True
    ).astype(jnp.float32)
    resid = jnp.concatenate([pre_resid, dec_resid], axis=0)
    hidden = (resid.astype(jnp.float32) + attn_out).astype(jnp.bfloat16)
    hidden_up = lax.optimization_barrier(hidden).astype(jnp.float32)
    mean_square = jnp.mean(hidden_up * hidden_up, axis=1, keepdims=True)
    normed = (
        hidden_up * lax.rsqrt(mean_square + NORM_EPS) * norm_gain.astype(jnp.float32)[None, :]
    ).astype(jnp.bfloat16)
    capacity = max(2, (rows_dev * TOPK + members - 1) // members)
    group_tokens = lax.all_gather(normed, "dp", axis=0, tiled=True)
    group_routes = lax.all_gather(routes, "dp", axis=0, tiled=True)
    routes_by_group = group_routes.reshape(groups, rows_dev, TOPK)
    slots_by_group = jax.vmap(partial(assign_slots, experts=members))(routes_by_group)
    own_slots = assign_slots(routes, members)
    own_matrix = dispatch_matrix(routes, own_slots, members, capacity).reshape(
        rows_dev, members, capacity
    )
    outgoing = jnp.einsum("rxc,rd->xcd", own_matrix, normed, preferred_element_type=jnp.bfloat16)
    arrived = lax.all_to_all(outgoing, "expert", split_axis=0, concat_axis=0, tiled=True)
    shared_ready = (weights["shared_gate"], weights["shared_up"], weights["shared_down"])
    arrived, shared_ready = lax.optimization_barrier((arrived, shared_ready))
    expert_rows = lax.all_gather(
        arrived.reshape(members, 1, capacity, D), "dp", axis=1, tiled=True
    )
    expert_rows = expert_rows.reshape(-1, D)
    gate_score = jax.nn.sigmoid(
        jnp.dot(expert_rows, router[:, 0], preferred_element_type=jnp.float32)
    )
    gate_proj = jnp.dot(expert_rows, gate_weight[0], preferred_element_type=jnp.float32)
    up_proj = jnp.dot(expert_rows, up_weight[0], preferred_element_type=jnp.float32)
    expert_act = (jax.nn.silu(gate_proj) * up_proj).astype(jnp.bfloat16)
    shared_gate_full, shared_up_full, shared_down_full = shared_ready
    shared_act = (
        jax.nn.silu(jnp.dot(group_tokens, shared_gate_full, preferred_element_type=jnp.float32))
        * jnp.dot(group_tokens, shared_up_full, preferred_element_type=jnp.float32)
    ).astype(jnp.bfloat16)
    down_local = down_weight[0]
    col_width = down_local.shape[1]
    routed_piece = lax.all_gather(expert_act, "dp", axis=1, tiled=True)
    shared_piece = lax.all_gather(shared_act, "dp", axis=1, tiled=True)
    routed_cols = jnp.dot(routed_piece, down_local, preferred_element_type=jnp.float32)
    shared_cols = jnp.dot(shared_piece, shared_down_full, preferred_element_type=jnp.float32)
    expert_out = routed_cols.astype(jnp.bfloat16)
    shared_out = shared_cols.astype(jnp.bfloat16)
    returned = lax.all_to_all(
        expert_out.reshape(members, groups * capacity, col_width),
        "expert",
        split_axis=0,
        concat_axis=0,
        tiled=True,
    )
    returned_scores = lax.all_to_all(
        gate_score.reshape(members, groups * capacity),
        "expert",
        split_axis=0,
        concat_axis=0,
        tiled=True,
    )
    group_offset = (jnp.arange(groups, dtype=jnp.int32) * capacity)[:, None, None]
    lookup = (routes_by_group * (groups * capacity) + group_offset + slots_by_group).reshape(
        groups * rows_dev, TOPK
    )
    picked = jnp.take(returned.reshape(-1, col_width), lookup, axis=0)
    picked_scores = jnp.take(returned_scores.reshape(-1), lookup, axis=0)
    route_weight = ROUTE_SCALE * picked_scores / jnp.sum(picked_scores, axis=1, keepdims=True)
    moe_cols = shared_out.astype(jnp.float32) + jnp.sum(
        route_weight[:, :, None] * picked.astype(jnp.float32), axis=1
    )
    moe_home = lax.all_to_all(
        moe_cols.reshape(groups, rows_dev, col_width).astype(jnp.bfloat16),
        "dp",
        split_axis=0,
        concat_axis=2,
        tiled=True,
    ).astype(jnp.float32)
    final = (hidden_up + moe_home[0]).astype(jnp.bfloat16)
    return (final[:pre_rows], final[pre_rows:])


def solution(mesh):
    in_specs = (
        P(("dp", "expert"), None, None),
        P(("dp", "expert"), None),
        P(("dp", "expert"), None),
        P(("dp", "expert"), None, None),
        P(("dp", "expert"), None),
        P(("dp", "expert"), None),
        P(("dp", "expert")),
        P(("dp", "expert"), None, None),
        P(),
        P("dp", "expert", None),
        P("dp", "expert", None),
        P(),
        P(None, "expert"),
        P(("dp", "expert"), None),
        P("expert", None, "dp"),
        P("expert", None, "dp"),
        P("expert", None, "dp"),
        P("expert", "dp"),
        P("expert", "dp"),
        P("expert", "dp"),
    )
    out_specs = (P(("dp", "expert"), None), P(("dp", "expert"), None))
    return jax.shard_map(shards, mesh=mesh, in_specs=in_specs, out_specs=out_specs, check_vma=False)
```

```python
from functools import partial

import jax
import jax.numpy as jnp
from jax import lax
from jax.experimental import pallas as pl
from jax.experimental.pallas import tpu as pltpu
from jax.sharding import PartitionSpec as P

D = 2048
LATENT = 512
ROPE = 64
QK_NOPE = 128
TOPK = 6


ROUTE_SCALE = 2.446
NORM_EPS = 1e-06
NEG_FILL = -1e30


def assign_slots(route_rows, experts):
    flat_routes = route_rows.reshape(-1)
    one_hot = (flat_routes[:, None] == jnp.arange(experts, dtype=jnp.int32)[None, :]).astype(
        jnp.int32
    )
    running = jnp.cumsum(one_hot, axis=0)
    slot_rank = jnp.sum(running * one_hot, axis=1) - 1
    return slot_rank.reshape(route_rows.shape)


def dispatch_matrix(route_rows, slot_rows, experts, capacity):
    target = route_rows * capacity + slot_rows
    places = jnp.arange(experts * capacity, dtype=jnp.int32)
    total = jnp.zeros((route_rows.shape[0], experts * capacity), jnp.bfloat16)
    for column in range(route_rows.shape[1]):
        total = total + (target[:, column][:, None] == places[None, :]).astype(jnp.bfloat16)
    return total


MESH_ID = pl.DeviceIdType.MESH


def gather_kernel(nx, nz, shard_ref, out_ref, xs_sem, xr_sem, own_sem, rs_sem, ls_sem, rr_sem):
    d = lax.axis_index("dp")
    e = lax.axis_index("expert")
    x = e // nz
    z = e % nz
    right = x * nz + (z + 1) % nz
    left = x * nz + (z + nz - 1) % nz
    steps_r = nz // 2
    steps_l = nz - 1 - steps_r

    barrier = pltpu.get_barrier_semaphore()
    for k in range(1, nx):
        peer = ((x + k) % nx) * nz + z
        pl.semaphore_signal(barrier, 1, device_id=(d, peer), device_id_type=MESH_ID)
    greeted = nx - 1
    if nz > 1:
        pl.semaphore_signal(barrier, 1, device_id=(d, right), device_id_type=MESH_ID)
        greeted += 1
    if nz > 2:
        pl.semaphore_signal(barrier, 1, device_id=(d, left), device_id_type=MESH_ID)
        greeted += 1
    if greeted:
        pl.semaphore_wait(barrier, greeted)

    own = pltpu.make_async_copy(shard_ref, out_ref.at[z, x], own_sem)
    own.start()
    x_copies = []
    for k in range(1, nx):
        px = (x + k) % nx
        send = pltpu.make_async_remote_copy(
            src_ref=shard_ref,
            dst_ref=out_ref.at[z, x],
            send_sem=xs_sem.at[k],
            recv_sem=xr_sem.at[x],
            device_id=(d, px * nz + z),
            device_id_type=MESH_ID,
        )
        send.start()
        x_copies.append(send)
    own.wait()
    for k in range(1, nx):
        px = (x + k) % nx
        incoming = pltpu.make_async_remote_copy(
            src_ref=shard_ref,
            dst_ref=out_ref.at[z, px],
            send_sem=xs_sem.at[k],
            recv_sem=xr_sem.at[px],
            device_id=(d, px * nz + z),
            device_id_type=MESH_ID,
        )
        incoming.wait_recv()

    def ring_copy(group, sems, step, target):
        return pltpu.make_async_remote_copy(
            src_ref=out_ref.at[group],
            dst_ref=out_ref.at[group],
            send_sem=sems.at[step],
            recv_sem=rr_sem.at[group],
            device_id=(d, target),
            device_id_type=MESH_ID,
        )

    sent = []
    for s in range(max(steps_r, steps_l)):
        if s < steps_r:
            group = (z - s + nz) % nz
            if s > 0:
                ring_copy(group, rs_sem, s, right).wait_recv()
            c = ring_copy(group, rs_sem, s, right)
            c.start()
            sent.append(c)
        if s < steps_l:
            group = (z + s) % nz
            if s > 0:
                ring_copy(group, ls_sem, s, left).wait_recv()
            c = ring_copy(group, ls_sem, s, left)
            c.start()
            sent.append(c)
    if steps_r > 0:
        ring_copy((z - steps_r + nz) % nz, rs_sem, 0, right).wait_recv()
    if steps_l > 0:
        ring_copy((z + steps_l) % nz, ls_sem, 0, left).wait_recv()
    for c in sent:
        c.wait_send()
    for c in x_copies:
        c.wait_send()


def expert_gather(flat, members):
    nz = 16 if members % 16 == 0 else members
    nx = members // nz
    rows, lanes = flat.shape
    steps = max(nz // 2, 1)
    out = pl.pallas_call(
        partial(gather_kernel, nx, nz),
        out_shape=jax.ShapeDtypeStruct((nz, nx, rows, lanes), flat.dtype),
        in_specs=[pl.BlockSpec(memory_space=pltpu.VMEM)],
        out_specs=pl.BlockSpec(memory_space=pltpu.VMEM),
        scratch_shapes=[
            pltpu.SemaphoreType.DMA((max(nx, 1),)),
            pltpu.SemaphoreType.DMA((max(nx, 1),)),
            pltpu.SemaphoreType.DMA(()),
            pltpu.SemaphoreType.DMA((steps,)),
            pltpu.SemaphoreType.DMA((steps,)),
            pltpu.SemaphoreType.DMA((nz,)),
        ],
        compiler_params=pltpu.CompilerParams(collective_id=0, has_side_effects=True),
    )(flat)
    return jnp.swapaxes(out, 0, 1).reshape(members, rows * lanes)


def gather_weights(members, by_kernel, **parts):
    names = list(parts)
    flat = jnp.concatenate([parts[n][0].reshape(-1) for n in names])
    lanes = 128
    total = flat.shape[0]
    padded = -(-total // (lanes * 8)) * lanes * 8
    flat = jnp.pad(flat, (0, padded - total)).reshape(padded // lanes, lanes)
    if by_kernel:
        everyone = expert_gather(flat, members)
    else:
        everyone = lax.all_gather(flat[None], "expert", axis=0, tiled=True)
        everyone = everyone.reshape(members, padded)
    out = {}
    start = 0
    for n in names:
        local, axis = parts[n]
        size = local.size
        piece = everyone[:, start : start + size].reshape((members,) + local.shape)
        piece = jnp.moveaxis(piece, 0, axis)
        shape = list(local.shape)
        shape[axis] *= members
        out[n] = piece.reshape(shape)
        start += size
    return out


def shards(
    pre_query,
    pre_latent,
    pre_resid,
    dec_query,
    dec_latent,
    dec_resid,
    cache_lengths,
    latent_cache,
    sink_logits,
    uv_weight,
    out_weight,
    norm_gain,
    router,
    routes,
    gate_weight,
    up_weight,
    down_weight,
    shared_gate,
    shared_up,
    shared_down,
):
    groups = lax.axis_size("dp")
    members = lax.axis_size("expert")
    pre_rows = pre_query.shape[0]
    rows_dev = pre_rows + 1
    scale_qk = (QK_NOPE + ROPE) ** (-0.5)
    weights = gather_weights(
        members,
        True,
        uv=(uv_weight, 1),
        out=(out_weight, 1),
    )
    weights.update(
        gather_weights(
            members,
            False,
            shared_gate=(shared_gate, 0),
            shared_up=(shared_up, 0),
            shared_down=(shared_down, 0),
            router=(router, 1),
        )
    )
    pre_scores = (
        jnp.einsum("thc,uc->thu", pre_query, pre_latent, preferred_element_type=jnp.float32)
        * scale_qk
    )
    places = jnp.arange(pre_rows, dtype=jnp.int32)
    allowed = (places[None, :] <= places[:, None])[:, None, :]
    masked = jnp.where(allowed, pre_scores, NEG_FILL)
    pre_max = jnp.maximum(jnp.max(masked, axis=2), sink_logits[None, :])
    exp_terms = jnp.where(allowed, jnp.exp(masked - pre_max[:, :, None]), 0.0)
    denominator = jnp.sum(exp_terms, axis=2) + jnp.exp(sink_logits[None, :] - pre_max)
    numerator = jnp.einsum(
        "thu,ul->thl",
        exp_terms.astype(jnp.bfloat16),
        pre_latent[:, :LATENT],
        preferred_element_type=jnp.float32,
    )
    pre_att = (numerator / denominator[:, :, None]).astype(jnp.bfloat16)
    window = latent_cache.shape[1]
    slot_ids = jnp.arange(window, dtype=jnp.int32)
    newest = cache_lengths - 1
    position = newest[:, None] - jnp.mod(newest[:, None] - slot_ids[None, :], window)
    usable = ((position >= 0) & (position > cache_lengths[:, None] - window))[:, None, :]
    cache_scores = (
        jnp.einsum("rhc,rsc->rhs", dec_query, latent_cache, preferred_element_type=jnp.float32)
        * scale_qk
    )
    own_scores = (
        jnp.einsum("rhc,rc->rh", dec_query, dec_latent, preferred_element_type=jnp.float32)
        * scale_qk
    )
    cache_masked = jnp.where(usable, cache_scores, NEG_FILL)
    top_score = jnp.maximum(
        jnp.maximum(jnp.max(cache_masked, axis=2), own_scores), sink_logits[None, :]
    )
    cache_exp = jnp.where(usable, jnp.exp(cache_masked - top_score[:, :, None]), 0.0)
    own_exp = jnp.exp(own_scores - top_score)
    dec_numer = jnp.einsum(
        "rhs,rsl->rhl",
        cache_exp.astype(jnp.bfloat16),
        latent_cache[:, :, :LATENT],
        preferred_element_type=jnp.float32,
    )
    dec_numer = dec_numer + own_exp.astype(jnp.bfloat16).astype(jnp.float32)[
        :, :, None
    ] * dec_latent[:, None, :LATENT].astype(jnp.float32)
    dec_total = jnp.sum(cache_exp, axis=2) + own_exp + jnp.exp(sink_logits[None, :] - top_score)
    dec_att = (dec_numer / dec_total[:, :, None]).astype(jnp.bfloat16)
    attention = jnp.concatenate([pre_att, dec_att], axis=0)
    spread = lax.all_to_all(attention, "dp", split_axis=1, concat_axis=0, tiled=True)
    uv_full, out_full = weights["uv"], weights["out"]
    head_values = jnp.einsum(
        "thl,hlv->thv", spread, uv_full, preferred_element_type=jnp.float32
    ).astype(jnp.bfloat16)
    head_partial = jnp.einsum(
        "thv,hvd->td", head_values, out_full, preferred_element_type=jnp.float32
    )
    attn_out = lax.psum_scatter(
        head_partial.astype(jnp.bfloat16), "dp", scatter_dimension=0, tiled=True
    ).astype(jnp.float32)
    resid = jnp.concatenate([pre_resid, dec_resid], axis=0)
    hidden = (resid.astype(jnp.float32) + attn_out).astype(jnp.bfloat16)
    hidden_up = lax.optimization_barrier(hidden).astype(jnp.float32)
    mean_square = jnp.mean(hidden_up * hidden_up, axis=1, keepdims=True)
    normed = (
        hidden_up * lax.rsqrt(mean_square + NORM_EPS) * norm_gain.astype(jnp.float32)[None, :]
    ).astype(jnp.bfloat16)
    capacity = max(2, (rows_dev * TOPK + members - 1) // members)
    route_row = routes.astype(jnp.bfloat16).reshape(1, rows_dev * TOPK)
    route_row = jnp.pad(route_row, ((0, 0), (0, D - rows_dev * TOPK)))
    group_both = lax.all_gather(
        jnp.concatenate([normed, route_row], axis=0)[None], "dp", axis=0, tiled=True
    )
    group_tokens = group_both[:, :rows_dev].reshape(groups * rows_dev, D)
    group_routes = (
        group_both[:, rows_dev, : rows_dev * TOPK].astype(jnp.int32).reshape(-1, TOPK)
    )
    routes_by_group = group_routes.reshape(groups, rows_dev, TOPK)
    slots_by_group = jax.vmap(partial(assign_slots, experts=members))(routes_by_group)
    own_slots = assign_slots(routes, members)
    own_matrix = dispatch_matrix(routes, own_slots, members, capacity).reshape(
        rows_dev, members, capacity
    )
    outgoing = jnp.einsum("rxc,rd->xcd", own_matrix, normed, preferred_element_type=jnp.bfloat16)
    arrived = lax.all_to_all(outgoing, "expert", split_axis=0, concat_axis=0, tiled=True)
    shared_ready = (
        weights["shared_gate"],
        weights["shared_up"],
        weights["shared_down"],
        weights["router"],
    )
    arrived, shared_ready = lax.optimization_barrier((arrived, shared_ready))
    expert_rows = lax.all_gather(
        arrived.reshape(members, 1, capacity, D), "dp", axis=1, tiled=True
    )
    expert_rows = expert_rows.reshape(-1, D)
    gate_proj = jnp.dot(expert_rows, gate_weight[0], preferred_element_type=jnp.float32)
    up_proj = jnp.dot(expert_rows, up_weight[0], preferred_element_type=jnp.float32)
    expert_act = (jax.nn.silu(gate_proj) * up_proj).astype(jnp.bfloat16)
    shared_gate_full, shared_up_full, shared_down_full, router_full = shared_ready
    shared_act = (
        jax.nn.silu(jnp.dot(group_tokens, shared_gate_full, preferred_element_type=jnp.float32))
        * jnp.dot(group_tokens, shared_up_full, preferred_element_type=jnp.float32)
    ).astype(jnp.bfloat16)
    down_local = down_weight[0]
    col_width = down_local.shape[1]
    routed_piece = lax.all_gather(expert_act, "dp", axis=1, tiled=True)
    shared_piece = lax.all_gather(shared_act, "dp", axis=1, tiled=True)
    routed_cols = jnp.dot(routed_piece, down_local, preferred_element_type=jnp.float32)
    shared_cols = jnp.dot(shared_piece, shared_down_full, preferred_element_type=jnp.float32)
    expert_out = routed_cols.astype(jnp.bfloat16)
    shared_out = shared_cols.astype(jnp.bfloat16)
    returned = lax.all_to_all(
        expert_out.reshape(members, groups * capacity, col_width),
        "expert",
        split_axis=0,
        concat_axis=0,
        tiled=True,
    )
    group_offset = (jnp.arange(groups, dtype=jnp.int32) * capacity)[:, None, None]
    lookup = (routes_by_group * (groups * capacity) + group_offset + slots_by_group).reshape(
        groups * rows_dev, TOPK
    )
    picked = jnp.take(returned.reshape(-1, col_width), lookup, axis=0)
    group_logits = jnp.dot(group_tokens, router_full, preferred_element_type=jnp.float32)
    picked_scores = jax.nn.sigmoid(
        jnp.take_along_axis(group_logits, group_routes.reshape(-1, TOPK), axis=1)
    )
    route_weight = ROUTE_SCALE * picked_scores / jnp.sum(picked_scores, axis=1, keepdims=True)
    moe_cols = shared_out.astype(jnp.float32) + jnp.sum(
        route_weight[:, :, None] * picked.astype(jnp.float32), axis=1
    )
    moe_home = lax.all_to_all(
        moe_cols.reshape(groups, rows_dev, col_width).astype(jnp.bfloat16),
        "dp",
        split_axis=0,
        concat_axis=2,
        tiled=True,
    ).astype(jnp.float32)
    final = (hidden_up + moe_home[0]).astype(jnp.bfloat16)
    return (final[:pre_rows], final[pre_rows:])


def solution(mesh):
    in_specs = (
        P(("dp", "expert"), None, None),
        P(("dp", "expert"), None),
        P(("dp", "expert"), None),
        P(("dp", "expert"), None, None),
        P(("dp", "expert"), None),
        P(("dp", "expert"), None),
        P(("dp", "expert")),
        P(("dp", "expert"), None, None),
        P(),
        P("dp", "expert", None),
        P("dp", "expert", None),
        P(),
        P(None, "expert"),
        P(("dp", "expert"), None),
        P("expert", None, "dp"),
        P("expert", None, "dp"),
        P("expert", None, "dp"),
        P("expert", "dp"),
        P("expert", "dp"),
        P("expert", "dp"),
    )
    out_specs = (P(("dp", "expert"), None), P(("dp", "expert"), None))
    return jax.shard_map(shards, mesh=mesh, in_specs=in_specs, out_specs=out_specs, check_vma=False)
```

```python
from functools import partial

import jax
import jax.numpy as jnp
from jax import lax
from jax.experimental import pallas as pl
from jax.experimental.pallas import tpu as pltpu
from jax.sharding import PartitionSpec as P

D = 2048
LATENT = 512
ROPE = 64
QK_NOPE = 128
TOPK = 6


ROUTE_SCALE = 2.446
NORM_EPS = 1e-06
NEG_FILL = -1e30


def assign_slots(route_rows, experts):
    flat_routes = route_rows.reshape(-1)
    one_hot = (flat_routes[:, None] == jnp.arange(experts, dtype=jnp.int32)[None, :]).astype(
        jnp.int32
    )
    running = jnp.cumsum(one_hot, axis=0)
    slot_rank = jnp.sum(running * one_hot, axis=1) - 1
    return slot_rank.reshape(route_rows.shape)


def dispatch_matrix(route_rows, slot_rows, experts, capacity):
    target = route_rows * capacity + slot_rows
    places = jnp.arange(experts * capacity, dtype=jnp.int32)
    total = jnp.zeros((route_rows.shape[0], experts * capacity), jnp.bfloat16)
    for column in range(route_rows.shape[1]):
        total = total + (target[:, column][:, None] == places[None, :]).astype(jnp.bfloat16)
    return total


MESH_ID = pl.DeviceIdType.MESH


def gather_kernel(nx, nz, shard_ref, out_ref, xs_sem, xr_sem, own_sem, rs_sem, ls_sem, rr_sem):
    d = lax.axis_index("dp")
    e = lax.axis_index("expert")
    x = e // nz
    z = e % nz
    right = x * nz + (z + 1) % nz
    left = x * nz + (z + nz - 1) % nz
    steps_r = nz // 2
    steps_l = nz - 1 - steps_r

    barrier = pltpu.get_barrier_semaphore()
    for k in range(1, nx):
        peer = ((x + k) % nx) * nz + z
        pl.semaphore_signal(barrier, 1, device_id=(d, peer), device_id_type=MESH_ID)
    greeted = nx - 1
    if nz > 1:
        pl.semaphore_signal(barrier, 1, device_id=(d, right), device_id_type=MESH_ID)
        greeted += 1
    if nz > 2:
        pl.semaphore_signal(barrier, 1, device_id=(d, left), device_id_type=MESH_ID)
        greeted += 1
    if greeted:
        pl.semaphore_wait(barrier, greeted)

    own = pltpu.make_async_copy(shard_ref, out_ref.at[z, x], own_sem)
    own.start()
    x_copies = []
    for k in range(1, nx):
        px = (x + k) % nx
        send = pltpu.make_async_remote_copy(
            src_ref=shard_ref,
            dst_ref=out_ref.at[z, x],
            send_sem=xs_sem.at[k],
            recv_sem=xr_sem.at[x],
            device_id=(d, px * nz + z),
            device_id_type=MESH_ID,
        )
        send.start()
        x_copies.append(send)
    own.wait()
    for k in range(1, nx):
        px = (x + k) % nx
        incoming = pltpu.make_async_remote_copy(
            src_ref=shard_ref,
            dst_ref=out_ref.at[z, px],
            send_sem=xs_sem.at[k],
            recv_sem=xr_sem.at[px],
            device_id=(d, px * nz + z),
            device_id_type=MESH_ID,
        )
        incoming.wait_recv()

    def ring_copy(group, sems, step, target):
        return pltpu.make_async_remote_copy(
            src_ref=out_ref.at[group],
            dst_ref=out_ref.at[group],
            send_sem=sems.at[step],
            recv_sem=rr_sem.at[group],
            device_id=(d, target),
            device_id_type=MESH_ID,
        )

    sent = []
    for s in range(max(steps_r, steps_l)):
        if s < steps_r:
            group = (z - s + nz) % nz
            if s > 0:
                ring_copy(group, rs_sem, s, right).wait_recv()
            c = ring_copy(group, rs_sem, s, right)
            c.start()
            sent.append(c)
        if s < steps_l:
            group = (z + s) % nz
            if s > 0:
                ring_copy(group, ls_sem, s, left).wait_recv()
            c = ring_copy(group, ls_sem, s, left)
            c.start()
            sent.append(c)
    if steps_r > 0:
        ring_copy((z - steps_r + nz) % nz, rs_sem, 0, right).wait_recv()
    if steps_l > 0:
        ring_copy((z + steps_l) % nz, ls_sem, 0, left).wait_recv()
    for c in sent:
        c.wait_send()
    for c in x_copies:
        c.wait_send()


def expert_gather(flat, members):
    nz = 16 if members % 16 == 0 else members
    nx = members // nz
    rows, lanes = flat.shape
    steps = max(nz // 2, 1)
    out = pl.pallas_call(
        partial(gather_kernel, nx, nz),
        out_shape=jax.ShapeDtypeStruct((nz, nx, rows, lanes), flat.dtype),
        in_specs=[pl.BlockSpec(memory_space=pltpu.VMEM)],
        out_specs=pl.BlockSpec(memory_space=pltpu.VMEM),
        scratch_shapes=[
            pltpu.SemaphoreType.DMA((max(nx, 1),)),
            pltpu.SemaphoreType.DMA((max(nx, 1),)),
            pltpu.SemaphoreType.DMA(()),
            pltpu.SemaphoreType.DMA((steps,)),
            pltpu.SemaphoreType.DMA((steps,)),
            pltpu.SemaphoreType.DMA((nz,)),
        ],
        compiler_params=pltpu.CompilerParams(collective_id=0, has_side_effects=True),
    )(flat)
    return jnp.swapaxes(out, 0, 1).reshape(members, rows * lanes)


def gather_weights(members, by_kernel, **parts):
    names = list(parts)
    flat = jnp.concatenate([parts[n][0].reshape(-1) for n in names])
    lanes = 128
    total = flat.shape[0]
    padded = -(-total // (lanes * 8)) * lanes * 8
    flat = jnp.pad(flat, (0, padded - total)).reshape(padded // lanes, lanes)
    if by_kernel:
        everyone = expert_gather(flat, members)
    else:
        everyone = lax.all_gather(flat[None], "expert", axis=0, tiled=True)
        everyone = everyone.reshape(members, padded)
    out = {}
    start = 0
    for n in names:
        local, axis = parts[n]
        size = local.size
        piece = everyone[:, start : start + size].reshape((members,) + local.shape)
        piece = jnp.moveaxis(piece, 0, axis)
        shape = list(local.shape)
        shape[axis] *= members
        out[n] = piece.reshape(shape)
        start += size
    return out


def shards(
    pre_query,
    pre_latent,
    pre_resid,
    dec_query,
    dec_latent,
    dec_resid,
    cache_lengths,
    latent_cache,
    sink_logits,
    uv_weight,
    out_weight,
    norm_gain,
    router,
    routes,
    gate_weight,
    up_weight,
    down_weight,
    shared_gate,
    shared_up,
    shared_down,
):
    groups = lax.axis_size("dp")
    members = lax.axis_size("expert")
    pre_rows = pre_query.shape[0]
    rows_dev = pre_rows + 1
    scale_qk = (QK_NOPE + ROPE) ** (-0.5)
    weights = gather_weights(
        members,
        True,
        uv=(uv_weight, 1),
        out=(out_weight, 1),
        shared_gate=(shared_gate, 0),
        shared_up=(shared_up, 0),
        shared_down=(shared_down, 0),
        router=(router, 1),
    )
    pre_scores = (
        jnp.einsum("thc,uc->thu", pre_query, pre_latent, preferred_element_type=jnp.float32)
        * scale_qk
    )
    places = jnp.arange(pre_rows, dtype=jnp.int32)
    allowed = (places[None, :] <= places[:, None])[:, None, :]
    masked = jnp.where(allowed, pre_scores, NEG_FILL)
    pre_max = jnp.maximum(jnp.max(masked, axis=2), sink_logits[None, :])
    exp_terms = jnp.where(allowed, jnp.exp(masked - pre_max[:, :, None]), 0.0)
    denominator = jnp.sum(exp_terms, axis=2) + jnp.exp(sink_logits[None, :] - pre_max)
    numerator = jnp.einsum(
        "thu,ul->thl",
        exp_terms.astype(jnp.bfloat16),
        pre_latent[:, :LATENT],
        preferred_element_type=jnp.float32,
    )
    pre_att = (numerator / denominator[:, :, None]).astype(jnp.bfloat16)
    window = latent_cache.shape[1]
    slot_ids = jnp.arange(window, dtype=jnp.int32)
    newest = cache_lengths - 1
    position = newest[:, None] - jnp.mod(newest[:, None] - slot_ids[None, :], window)
    usable = ((position >= 0) & (position > cache_lengths[:, None] - window))[:, None, :]
    cache_scores = (
        jnp.einsum("rhc,rsc->rhs", dec_query, latent_cache, preferred_element_type=jnp.float32)
        * scale_qk
    )
    own_scores = (
        jnp.einsum("rhc,rc->rh", dec_query, dec_latent, preferred_element_type=jnp.float32)
        * scale_qk
    )
    cache_masked = jnp.where(usable, cache_scores, NEG_FILL)
    top_score = jnp.maximum(
        jnp.maximum(jnp.max(cache_masked, axis=2), own_scores), sink_logits[None, :]
    )
    cache_exp = jnp.where(usable, jnp.exp(cache_masked - top_score[:, :, None]), 0.0)
    own_exp = jnp.exp(own_scores - top_score)
    dec_numer = jnp.einsum(
        "rhs,rsl->rhl",
        cache_exp.astype(jnp.bfloat16),
        latent_cache[:, :, :LATENT],
        preferred_element_type=jnp.float32,
    )
    dec_numer = dec_numer + own_exp.astype(jnp.bfloat16).astype(jnp.float32)[
        :, :, None
    ] * dec_latent[:, None, :LATENT].astype(jnp.float32)
    dec_total = jnp.sum(cache_exp, axis=2) + own_exp + jnp.exp(sink_logits[None, :] - top_score)
    dec_att = (dec_numer / dec_total[:, :, None]).astype(jnp.bfloat16)
    attention = jnp.concatenate([pre_att, dec_att], axis=0)
    spread = lax.all_to_all(attention, "dp", split_axis=1, concat_axis=0, tiled=True)
    uv_full, out_full = weights["uv"], weights["out"]
    head_values = jnp.einsum(
        "thl,hlv->thv", spread, uv_full, preferred_element_type=jnp.float32
    ).astype(jnp.bfloat16)
    head_partial = jnp.einsum(
        "thv,hvd->td", head_values, out_full, preferred_element_type=jnp.float32
    )
    attn_out = lax.psum_scatter(
        head_partial.astype(jnp.bfloat16), "dp", scatter_dimension=0, tiled=True
    ).astype(jnp.float32)
    resid = jnp.concatenate([pre_resid, dec_resid], axis=0)
    hidden = (resid.astype(jnp.float32) + attn_out).astype(jnp.bfloat16)
    hidden_up = lax.optimization_barrier(hidden).astype(jnp.float32)
    mean_square = jnp.mean(hidden_up * hidden_up, axis=1, keepdims=True)
    normed = (
        hidden_up * lax.rsqrt(mean_square + NORM_EPS) * norm_gain.astype(jnp.float32)[None, :]
    ).astype(jnp.bfloat16)
    capacity = max(2, (rows_dev * TOPK + members - 1) // members)
    route_row = routes.astype(jnp.bfloat16).reshape(1, rows_dev * TOPK)
    route_row = jnp.pad(route_row, ((0, 0), (0, D - rows_dev * TOPK)))
    group_both = lax.all_gather(
        jnp.concatenate([normed, route_row], axis=0)[None], "dp", axis=0, tiled=True
    )
    group_tokens = group_both[:, :rows_dev].reshape(groups * rows_dev, D)
    group_routes = (
        group_both[:, rows_dev, : rows_dev * TOPK].astype(jnp.int32).reshape(-1, TOPK)
    )
    routes_by_group = group_routes.reshape(groups, rows_dev, TOPK)
    slots_by_group = jax.vmap(partial(assign_slots, experts=members))(routes_by_group)
    own_slots = assign_slots(routes, members)
    own_matrix = dispatch_matrix(routes, own_slots, members, capacity).reshape(
        rows_dev, members, capacity
    )
    outgoing = jnp.einsum("rxc,rd->xcd", own_matrix, normed, preferred_element_type=jnp.bfloat16)
    arrived = lax.all_to_all(outgoing, "expert", split_axis=0, concat_axis=0, tiled=True)
    shared_ready = (
        weights["shared_gate"],
        weights["shared_up"],
        weights["shared_down"],
        weights["router"],
    )
    expert_rows = lax.all_gather(
        arrived.reshape(members, 1, capacity, D), "dp", axis=1, tiled=True
    )
    expert_rows = expert_rows.reshape(-1, D)
    gate_proj = jnp.dot(expert_rows, gate_weight[0], preferred_element_type=jnp.float32)
    up_proj = jnp.dot(expert_rows, up_weight[0], preferred_element_type=jnp.float32)
    expert_act = (jax.nn.silu(gate_proj) * up_proj).astype(jnp.bfloat16)
    shared_gate_full, shared_up_full, shared_down_full, router_full = shared_ready
    shared_act = (
        jax.nn.silu(jnp.dot(group_tokens, shared_gate_full, preferred_element_type=jnp.float32))
        * jnp.dot(group_tokens, shared_up_full, preferred_element_type=jnp.float32)
    ).astype(jnp.bfloat16)
    down_local = down_weight[0]
    col_width = down_local.shape[1]
    routed_piece = lax.all_gather(expert_act, "dp", axis=1, tiled=True)
    shared_piece = lax.all_gather(shared_act, "dp", axis=1, tiled=True)
    routed_cols = jnp.dot(routed_piece, down_local, preferred_element_type=jnp.float32)
    shared_cols = jnp.dot(shared_piece, shared_down_full, preferred_element_type=jnp.float32)
    expert_out = routed_cols.astype(jnp.bfloat16)
    shared_out = shared_cols.astype(jnp.bfloat16)
    returned = lax.all_to_all(
        expert_out.reshape(members, groups * capacity, col_width),
        "expert",
        split_axis=0,
        concat_axis=0,
        tiled=True,
    )
    group_offset = (jnp.arange(groups, dtype=jnp.int32) * capacity)[:, None, None]
    lookup = (routes_by_group * (groups * capacity) + group_offset + slots_by_group).reshape(
        groups * rows_dev, TOPK
    )
    picked = jnp.take(returned.reshape(-1, col_width), lookup, axis=0)
    group_logits = jnp.dot(group_tokens, router_full, preferred_element_type=jnp.float32)
    picked_scores = jax.nn.sigmoid(
        jnp.take_along_axis(group_logits, group_routes.reshape(-1, TOPK), axis=1)
    )
    route_weight = ROUTE_SCALE * picked_scores / jnp.sum(picked_scores, axis=1, keepdims=True)
    moe_cols = shared_out.astype(jnp.float32) + jnp.sum(
        route_weight[:, :, None] * picked.astype(jnp.float32), axis=1
    )
    moe_home = lax.all_to_all(
        moe_cols.reshape(groups, rows_dev, col_width).astype(jnp.bfloat16),
        "dp",
        split_axis=0,
        concat_axis=2,
        tiled=True,
    ).astype(jnp.float32)
    final = (hidden_up + moe_home[0]).astype(jnp.bfloat16)
    return (final[:pre_rows], final[pre_rows:])


def solution(mesh):
    in_specs = (
        P(("dp", "expert"), None, None),
        P(("dp", "expert"), None),
        P(("dp", "expert"), None),
        P(("dp", "expert"), None, None),
        P(("dp", "expert"), None),
        P(("dp", "expert"), None),
        P(("dp", "expert")),
        P(("dp", "expert"), None, None),
        P(),
        P("dp", "expert", None),
        P("dp", "expert", None),
        P(),
        P(None, "expert"),
        P(("dp", "expert"), None),
        P("expert", None, "dp"),
        P("expert", None, "dp"),
        P("expert", None, "dp"),
        P("expert", "dp"),
        P("expert", "dp"),
        P("expert", "dp"),
    )
    out_specs = (P(("dp", "expert"), None), P(("dp", "expert"), None))
    return jax.shard_map(shards, mesh=mesh, in_specs=in_specs, out_specs=out_specs, check_vma=False)
```

```python
from functools import partial

import jax
import jax.numpy as jnp
from jax import lax
from jax.experimental import pallas as pl
from jax.experimental.pallas import tpu as pltpu
from jax.sharding import PartitionSpec as P

D = 2048
LATENT = 512
ROPE = 64
QK_NOPE = 128
TOPK = 6


ROUTE_SCALE = 2.446
NORM_EPS = 1e-06
NEG_FILL = -1e30


def assign_slots(route_rows, experts):
    flat_routes = route_rows.reshape(-1)
    one_hot = (flat_routes[:, None] == jnp.arange(experts, dtype=jnp.int32)[None, :]).astype(
        jnp.int32
    )
    running = jnp.cumsum(one_hot, axis=0)
    slot_rank = jnp.sum(running * one_hot, axis=1) - 1
    return slot_rank.reshape(route_rows.shape)


def dispatch_matrix(route_rows, slot_rows, experts, capacity):
    target = route_rows * capacity + slot_rows
    places = jnp.arange(experts * capacity, dtype=jnp.int32)
    total = jnp.zeros((route_rows.shape[0], experts * capacity), jnp.bfloat16)
    for column in range(route_rows.shape[1]):
        total = total + (target[:, column][:, None] == places[None, :]).astype(jnp.bfloat16)
    return total


MESH_ID = pl.DeviceIdType.MESH


def gather_kernel(nx, nz, shard_ref, out_ref, xs_sem, xr_sem, own_sem, rs_sem, ls_sem, rr_sem):
    d = lax.axis_index("dp")
    e = lax.axis_index("expert")
    x = e // nz
    z = e % nz
    right = x * nz + (z + 1) % nz
    left = x * nz + (z + nz - 1) % nz
    steps_r = nz // 2
    steps_l = nz - 1 - steps_r

    barrier = pltpu.get_barrier_semaphore()
    for k in range(1, nx):
        peer = ((x + k) % nx) * nz + z
        pl.semaphore_signal(barrier, 1, device_id=(d, peer), device_id_type=MESH_ID)
    greeted = nx - 1
    if nz > 1:
        pl.semaphore_signal(barrier, 1, device_id=(d, right), device_id_type=MESH_ID)
        greeted += 1
    if nz > 2:
        pl.semaphore_signal(barrier, 1, device_id=(d, left), device_id_type=MESH_ID)
        greeted += 1
    if greeted:
        pl.semaphore_wait(barrier, greeted)

    own = pltpu.make_async_copy(shard_ref, out_ref.at[z, x], own_sem)
    own.start()
    x_copies = []
    for k in range(1, nx):
        px = (x + k) % nx
        send = pltpu.make_async_remote_copy(
            src_ref=shard_ref,
            dst_ref=out_ref.at[z, x],
            send_sem=xs_sem.at[k],
            recv_sem=xr_sem.at[x],
            device_id=(d, px * nz + z),
            device_id_type=MESH_ID,
        )
        send.start()
        x_copies.append(send)
    own.wait()
    for k in range(1, nx):
        px = (x + k) % nx
        incoming = pltpu.make_async_remote_copy(
            src_ref=shard_ref,
            dst_ref=out_ref.at[z, px],
            send_sem=xs_sem.at[k],
            recv_sem=xr_sem.at[px],
            device_id=(d, px * nz + z),
            device_id_type=MESH_ID,
        )
        incoming.wait_recv()

    def ring_copy(group, sems, step, target):
        return pltpu.make_async_remote_copy(
            src_ref=out_ref.at[group],
            dst_ref=out_ref.at[group],
            send_sem=sems.at[step],
            recv_sem=rr_sem.at[group],
            device_id=(d, target),
            device_id_type=MESH_ID,
        )

    sent = []
    for s in range(max(steps_r, steps_l)):
        if s < steps_r:
            group = (z - s + nz) % nz
            if s > 0:
                ring_copy(group, rs_sem, s, right).wait_recv()
            c = ring_copy(group, rs_sem, s, right)
            c.start()
            sent.append(c)
        if s < steps_l:
            group = (z + s) % nz
            if s > 0:
                ring_copy(group, ls_sem, s, left).wait_recv()
            c = ring_copy(group, ls_sem, s, left)
            c.start()
            sent.append(c)
    if steps_r > 0:
        ring_copy((z - steps_r + nz) % nz, rs_sem, 0, right).wait_recv()
    if steps_l > 0:
        ring_copy((z + steps_l) % nz, ls_sem, 0, left).wait_recv()
    for c in sent:
        c.wait_send()
    for c in x_copies:
        c.wait_send()


def expert_gather(flat, members):
    nz = 16 if members % 16 == 0 else members
    nx = members // nz
    rows, lanes = flat.shape
    steps = max(nz // 2, 1)
    out = pl.pallas_call(
        partial(gather_kernel, nx, nz),
        out_shape=jax.ShapeDtypeStruct((nz, nx, rows, lanes), flat.dtype),
        in_specs=[pl.BlockSpec(memory_space=pltpu.VMEM)],
        out_specs=pl.BlockSpec(memory_space=pltpu.VMEM),
        scratch_shapes=[
            pltpu.SemaphoreType.DMA((max(nx, 1),)),
            pltpu.SemaphoreType.DMA((max(nx, 1),)),
            pltpu.SemaphoreType.DMA(()),
            pltpu.SemaphoreType.DMA((steps,)),
            pltpu.SemaphoreType.DMA((steps,)),
            pltpu.SemaphoreType.DMA((nz,)),
        ],
        compiler_params=pltpu.CompilerParams(collective_id=0, has_side_effects=True),
    )(flat)
    return jnp.swapaxes(out, 0, 1).reshape(members, rows * lanes)


def gather_weights(members, by_kernel, **parts):
    names = list(parts)
    flat = jnp.concatenate([parts[n][0].reshape(-1) for n in names])
    lanes = 128
    total = flat.shape[0]
    padded = -(-total // (lanes * 8)) * lanes * 8
    flat = jnp.pad(flat, (0, padded - total)).reshape(padded // lanes, lanes)
    if by_kernel:
        everyone = expert_gather(flat, members)
    else:
        everyone = lax.all_gather(flat[None], "expert", axis=0, tiled=True)
        everyone = everyone.reshape(members, padded)
    out = {}
    start = 0
    for n in names:
        local, axis = parts[n]
        size = local.size
        piece = everyone[:, start : start + size].reshape((members,) + local.shape)
        piece = jnp.moveaxis(piece, 0, axis)
        shape = list(local.shape)
        shape[axis] *= members
        out[n] = piece.reshape(shape)
        start += size
    return out


def shards(
    pre_query,
    pre_latent,
    pre_resid,
    dec_query,
    dec_latent,
    dec_resid,
    cache_lengths,
    latent_cache,
    sink_logits,
    uv_weight,
    out_weight,
    norm_gain,
    router,
    routes,
    gate_weight,
    up_weight,
    down_weight,
    shared_gate,
    shared_up,
    shared_down,
):
    groups = lax.axis_size("dp")
    members = lax.axis_size("expert")
    pre_rows = pre_query.shape[0]
    rows_dev = pre_rows + 1
    scale_qk = (QK_NOPE + ROPE) ** (-0.5)
    weights = gather_weights(
        members,
        True,
        uv=(uv_weight, 1),
        out=(out_weight, 1),
        shared_gate=(shared_gate, 0),
        shared_up=(shared_up, 0),
        shared_down=(shared_down, 0),
        router=(router, 1),
    )
    pre_scores = (
        jnp.einsum("thc,uc->thu", pre_query, pre_latent, preferred_element_type=jnp.float32)
        * scale_qk
    )
    places = jnp.arange(pre_rows, dtype=jnp.int32)
    allowed = (places[None, :] <= places[:, None])[:, None, :]
    masked = jnp.where(allowed, pre_scores, NEG_FILL)
    pre_max = jnp.maximum(jnp.max(masked, axis=2), sink_logits[None, :])
    exp_terms = jnp.where(allowed, jnp.exp(masked - pre_max[:, :, None]), 0.0)
    denominator = jnp.sum(exp_terms, axis=2) + jnp.exp(sink_logits[None, :] - pre_max)
    numerator = jnp.einsum(
        "thu,ul->thl",
        exp_terms.astype(jnp.bfloat16),
        pre_latent[:, :LATENT],
        preferred_element_type=jnp.float32,
    )
    pre_att = (numerator / denominator[:, :, None]).astype(jnp.bfloat16)
    window = latent_cache.shape[1]
    slot_ids = jnp.arange(window, dtype=jnp.int32)
    newest = cache_lengths - 1
    position = newest[:, None] - jnp.mod(newest[:, None] - slot_ids[None, :], window)
    usable = ((position >= 0) & (position > cache_lengths[:, None] - window))[:, None, :]
    cache_scores = (
        jnp.einsum("rhc,rsc->rhs", dec_query, latent_cache, preferred_element_type=jnp.float32)
        * scale_qk
    )
    own_scores = (
        jnp.einsum("rhc,rc->rh", dec_query, dec_latent, preferred_element_type=jnp.float32)
        * scale_qk
    )
    cache_masked = jnp.where(usable, cache_scores, NEG_FILL)
    top_score = jnp.maximum(
        jnp.maximum(jnp.max(cache_masked, axis=2), own_scores), sink_logits[None, :]
    )
    cache_exp = jnp.where(usable, jnp.exp(cache_masked - top_score[:, :, None]), 0.0)
    own_exp = jnp.exp(own_scores - top_score)
    dec_numer = jnp.einsum(
        "rhs,rsl->rhl",
        cache_exp.astype(jnp.bfloat16),
        latent_cache[:, :, :LATENT],
        preferred_element_type=jnp.float32,
    )
    dec_numer = dec_numer + own_exp.astype(jnp.bfloat16).astype(jnp.float32)[
        :, :, None
    ] * dec_latent[:, None, :LATENT].astype(jnp.float32)
    dec_total = jnp.sum(cache_exp, axis=2) + own_exp + jnp.exp(sink_logits[None, :] - top_score)
    dec_att = (dec_numer / dec_total[:, :, None]).astype(jnp.bfloat16)
    attention = jnp.concatenate([pre_att, dec_att], axis=0)
    spread = lax.all_to_all(attention, "dp", split_axis=1, concat_axis=0, tiled=True)
    uv_full, out_full = weights["uv"], weights["out"]
    head_values = jnp.einsum(
        "thl,hlv->thv", spread, uv_full, preferred_element_type=jnp.float32
    ).astype(jnp.bfloat16)
    head_partial = jnp.einsum(
        "thv,hvd->td", head_values, out_full, preferred_element_type=jnp.float32
    )
    attn_out = lax.psum_scatter(
        head_partial.astype(jnp.bfloat16), "dp", scatter_dimension=0, tiled=True
    ).astype(jnp.float32)
    resid = jnp.concatenate([pre_resid, dec_resid], axis=0)
    hidden = (resid.astype(jnp.float32) + attn_out).astype(jnp.bfloat16)
    hidden_up = lax.optimization_barrier(hidden).astype(jnp.float32)
    mean_square = jnp.mean(hidden_up * hidden_up, axis=1, keepdims=True)
    normed = (
        hidden_up * lax.rsqrt(mean_square + NORM_EPS) * norm_gain.astype(jnp.float32)[None, :]
    ).astype(jnp.bfloat16)
    capacity = max(2, (rows_dev * TOPK + members - 1) // members)
    route_row = routes.astype(jnp.bfloat16).reshape(1, rows_dev * TOPK)
    route_row = jnp.pad(route_row, ((0, 0), (0, D - rows_dev * TOPK)))
    group_both = lax.all_gather(
        jnp.concatenate([normed, route_row], axis=0)[None], "dp", axis=0, tiled=True
    )
    group_tokens = group_both[:, :rows_dev].reshape(groups * rows_dev, D)
    group_routes = (
        group_both[:, rows_dev, : rows_dev * TOPK].astype(jnp.int32).reshape(-1, TOPK)
    )
    routes_by_group = group_routes.reshape(groups, rows_dev, TOPK)
    slots_by_group = jax.vmap(partial(assign_slots, experts=members))(routes_by_group)
    own_slots = assign_slots(routes, members)
    own_matrix = dispatch_matrix(routes, own_slots, members, capacity).reshape(
        rows_dev, members, capacity
    )
    outgoing = jnp.einsum("rxc,rd->xcd", own_matrix, normed, preferred_element_type=jnp.bfloat16)
    shared_gate_full, shared_up_full = weights["shared_gate"], weights["shared_up"]
    shared_down_full, router_full = weights["shared_down"], weights["router"]
    shared_act = (
        jax.nn.silu(jnp.dot(group_tokens, shared_gate_full, preferred_element_type=jnp.float32))
        * jnp.dot(group_tokens, shared_up_full, preferred_element_type=jnp.float32)
    ).astype(jnp.bfloat16)
    shared_piece = lax.all_gather(shared_act, "dp", axis=1, tiled=True)
    arrived = lax.all_to_all(outgoing, "expert", split_axis=0, concat_axis=0, tiled=True)
    arrived, shared_piece = lax.optimization_barrier((arrived, shared_piece))
    expert_rows = lax.all_gather(
        arrived.reshape(members, 1, capacity, D), "dp", axis=1, tiled=True
    )
    expert_rows = expert_rows.reshape(-1, D)
    gate_proj = jnp.dot(expert_rows, gate_weight[0], preferred_element_type=jnp.float32)
    up_proj = jnp.dot(expert_rows, up_weight[0], preferred_element_type=jnp.float32)
    expert_act = (jax.nn.silu(gate_proj) * up_proj).astype(jnp.bfloat16)
    down_local = down_weight[0]
    col_width = down_local.shape[1]
    routed_piece = lax.all_gather(expert_act, "dp", axis=1, tiled=True)
    routed_cols = jnp.dot(routed_piece, down_local, preferred_element_type=jnp.float32)
    shared_cols = jnp.dot(shared_piece, shared_down_full, preferred_element_type=jnp.float32)
    expert_out = routed_cols.astype(jnp.bfloat16)
    shared_out = shared_cols.astype(jnp.bfloat16)
    returned = lax.all_to_all(
        expert_out.reshape(members, groups * capacity, col_width),
        "expert",
        split_axis=0,
        concat_axis=0,
        tiled=True,
    )
    group_offset = (jnp.arange(groups, dtype=jnp.int32) * capacity)[:, None, None]
    lookup = (routes_by_group * (groups * capacity) + group_offset + slots_by_group).reshape(
        groups * rows_dev, TOPK
    )
    picked = jnp.take(returned.reshape(-1, col_width), lookup, axis=0)
    group_logits = jnp.dot(group_tokens, router_full, preferred_element_type=jnp.float32)
    picked_scores = jax.nn.sigmoid(
        jnp.take_along_axis(group_logits, group_routes.reshape(-1, TOPK), axis=1)
    )
    route_weight = ROUTE_SCALE * picked_scores / jnp.sum(picked_scores, axis=1, keepdims=True)
    moe_cols = shared_out.astype(jnp.float32) + jnp.sum(
        route_weight[:, :, None] * picked.astype(jnp.float32), axis=1
    )
    moe_home = lax.all_to_all(
        moe_cols.reshape(groups, rows_dev, col_width).astype(jnp.bfloat16),
        "dp",
        split_axis=0,
        concat_axis=2,
        tiled=True,
    ).astype(jnp.float32)
    final = (hidden_up + moe_home[0]).astype(jnp.bfloat16)
    return (final[:pre_rows], final[pre_rows:])


def solution(mesh):
    in_specs = (
        P(("dp", "expert"), None, None),
        P(("dp", "expert"), None),
        P(("dp", "expert"), None),
        P(("dp", "expert"), None, None),
        P(("dp", "expert"), None),
        P(("dp", "expert"), None),
        P(("dp", "expert")),
        P(("dp", "expert"), None, None),
        P(),
        P("dp", "expert", None),
        P("dp", "expert", None),
        P(),
        P(None, "expert"),
        P(("dp", "expert"), None),
        P("expert", None, "dp"),
        P("expert", None, "dp"),
        P("expert", None, "dp"),
        P("expert", "dp"),
        P("expert", "dp"),
        P("expert", "dp"),
    )
    out_specs = (P(("dp", "expert"), None), P(("dp", "expert"), None))
    return jax.shard_map(shards, mesh=mesh, in_specs=in_specs, out_specs=out_specs, check_vma=False)
```

```python
from functools import partial

import jax
import jax.numpy as jnp
from jax import lax
from jax.experimental import pallas as pl
from jax.experimental.pallas import tpu as pltpu
from jax.sharding import PartitionSpec as P

D = 2048
LATENT = 512
ROPE = 64
QK_NOPE = 128
TOPK = 6


ROUTE_SCALE = 2.446
NORM_EPS = 1e-06
NEG_FILL = -1e30


def assign_slots(route_rows, experts):
    flat_routes = route_rows.reshape(-1)
    one_hot = (flat_routes[:, None] == jnp.arange(experts, dtype=jnp.int32)[None, :]).astype(
        jnp.int32
    )
    running = jnp.cumsum(one_hot, axis=0)
    slot_rank = jnp.sum(running * one_hot, axis=1) - 1
    return slot_rank.reshape(route_rows.shape)


def dispatch_matrix(route_rows, slot_rows, experts, capacity):
    target = route_rows * capacity + slot_rows
    places = jnp.arange(experts * capacity, dtype=jnp.int32)
    total = jnp.zeros((route_rows.shape[0], experts * capacity), jnp.bfloat16)
    for column in range(route_rows.shape[1]):
        total = total + (target[:, column][:, None] == places[None, :]).astype(jnp.bfloat16)
    return total


MESH_ID = pl.DeviceIdType.MESH


def gather_kernel(nx, nz, shard_ref, out_ref, xs_sem, xr_sem, own_sem, rs_sem, ls_sem, rr_sem):
    d = lax.axis_index("dp")
    e = lax.axis_index("expert")
    x = e // nz
    z = e % nz
    right = x * nz + (z + 1) % nz
    left = x * nz + (z + nz - 1) % nz
    steps_r = nz // 2
    steps_l = nz - 1 - steps_r

    barrier = pltpu.get_barrier_semaphore()
    for k in range(1, nx):
        peer = ((x + k) % nx) * nz + z
        pl.semaphore_signal(barrier, 1, device_id=(d, peer), device_id_type=MESH_ID)
    greeted = nx - 1
    if nz > 1:
        pl.semaphore_signal(barrier, 1, device_id=(d, right), device_id_type=MESH_ID)
        greeted += 1
    if nz > 2:
        pl.semaphore_signal(barrier, 1, device_id=(d, left), device_id_type=MESH_ID)
        greeted += 1
    if greeted:
        pl.semaphore_wait(barrier, greeted)

    own = pltpu.make_async_copy(shard_ref, out_ref.at[z, x], own_sem)
    own.start()
    x_copies = []
    for k in range(1, nx):
        px = (x + k) % nx
        send = pltpu.make_async_remote_copy(
            src_ref=shard_ref,
            dst_ref=out_ref.at[z, x],
            send_sem=xs_sem.at[k],
            recv_sem=xr_sem.at[x],
            device_id=(d, px * nz + z),
            device_id_type=MESH_ID,
        )
        send.start()
        x_copies.append(send)
    own.wait()
    for k in range(1, nx):
        px = (x + k) % nx
        incoming = pltpu.make_async_remote_copy(
            src_ref=shard_ref,
            dst_ref=out_ref.at[z, px],
            send_sem=xs_sem.at[k],
            recv_sem=xr_sem.at[px],
            device_id=(d, px * nz + z),
            device_id_type=MESH_ID,
        )
        incoming.wait_recv()

    def ring_copy(group, sems, step, target):
        return pltpu.make_async_remote_copy(
            src_ref=out_ref.at[group],
            dst_ref=out_ref.at[group],
            send_sem=sems.at[step],
            recv_sem=rr_sem.at[group],
            device_id=(d, target),
            device_id_type=MESH_ID,
        )

    sent = []
    for s in range(max(steps_r, steps_l)):
        if s < steps_r:
            group = (z - s + nz) % nz
            if s > 0:
                ring_copy(group, rs_sem, s, right).wait_recv()
            c = ring_copy(group, rs_sem, s, right)
            c.start()
            sent.append(c)
        if s < steps_l:
            group = (z + s) % nz
            if s > 0:
                ring_copy(group, ls_sem, s, left).wait_recv()
            c = ring_copy(group, ls_sem, s, left)
            c.start()
            sent.append(c)
    if steps_r > 0:
        ring_copy((z - steps_r + nz) % nz, rs_sem, 0, right).wait_recv()
    if steps_l > 0:
        ring_copy((z + steps_l) % nz, ls_sem, 0, left).wait_recv()
    for c in sent:
        c.wait_send()
    for c in x_copies:
        c.wait_send()


def expert_gather(flat, members):
    nz = 16 if members % 16 == 0 else members
    nx = members // nz
    rows, lanes = flat.shape
    steps = max(nz // 2, 1)
    out = pl.pallas_call(
        partial(gather_kernel, nx, nz),
        out_shape=jax.ShapeDtypeStruct((nz, nx, rows, lanes), flat.dtype),
        in_specs=[pl.BlockSpec(memory_space=pltpu.VMEM)],
        out_specs=pl.BlockSpec(memory_space=pltpu.VMEM),
        scratch_shapes=[
            pltpu.SemaphoreType.DMA((max(nx, 1),)),
            pltpu.SemaphoreType.DMA((max(nx, 1),)),
            pltpu.SemaphoreType.DMA(()),
            pltpu.SemaphoreType.DMA((steps,)),
            pltpu.SemaphoreType.DMA((steps,)),
            pltpu.SemaphoreType.DMA((nz,)),
        ],
        compiler_params=pltpu.CompilerParams(collective_id=0, has_side_effects=True),
    )(flat)
    return jnp.swapaxes(out, 0, 1).reshape(members, rows * lanes)


def gather_weights(members, by_kernel, **parts):
    names = list(parts)
    flat = jnp.concatenate([parts[n][0].reshape(-1) for n in names])
    lanes = 128
    total = flat.shape[0]
    padded = -(-total // (lanes * 8)) * lanes * 8
    flat = jnp.pad(flat, (0, padded - total)).reshape(padded // lanes, lanes)
    if by_kernel:
        everyone = expert_gather(flat, members)
    else:
        everyone = lax.all_gather(flat[None], "expert", axis=0, tiled=True)
        everyone = everyone.reshape(members, padded)
    out = {}
    start = 0
    for n in names:
        local, axis = parts[n]
        size = local.size
        piece = everyone[:, start : start + size].reshape((members,) + local.shape)
        piece = jnp.moveaxis(piece, 0, axis)
        shape = list(local.shape)
        shape[axis] *= members
        out[n] = piece.reshape(shape)
        start += size
    return out


def shards(
    pre_query,
    pre_latent,
    pre_resid,
    dec_query,
    dec_latent,
    dec_resid,
    cache_lengths,
    latent_cache,
    sink_logits,
    uv_weight,
    out_weight,
    norm_gain,
    router,
    routes,
    gate_weight,
    up_weight,
    down_weight,
    shared_gate,
    shared_up,
    shared_down,
):
    groups = lax.axis_size("dp")
    members = lax.axis_size("expert")
    pre_rows = pre_query.shape[0]
    rows_dev = pre_rows + 1
    scale_qk = (QK_NOPE + ROPE) ** (-0.5)
    weights = gather_weights(
        members,
        True,
        uv=(uv_weight, 1),
        out=(out_weight, 1),
        shared_gate=(shared_gate, 0),
        shared_up=(shared_up, 0),
        shared_down=(shared_down, 0),
        router=(router, 1),
    )
    pre_scores = (
        jnp.einsum("thc,uc->thu", pre_query, pre_latent, preferred_element_type=jnp.float32)
        * scale_qk
    )
    places = jnp.arange(pre_rows, dtype=jnp.int32)
    allowed = (places[None, :] <= places[:, None])[:, None, :]
    masked = jnp.where(allowed, pre_scores, NEG_FILL)
    pre_max = jnp.maximum(jnp.max(masked, axis=2), sink_logits[None, :])
    exp_terms = jnp.where(allowed, jnp.exp(masked - pre_max[:, :, None]), 0.0)
    denominator = jnp.sum(exp_terms, axis=2) + jnp.exp(sink_logits[None, :] - pre_max)
    numerator = jnp.einsum(
        "thu,ul->thl",
        exp_terms.astype(jnp.bfloat16),
        pre_latent[:, :LATENT],
        preferred_element_type=jnp.float32,
    )
    pre_att = (numerator / denominator[:, :, None]).astype(jnp.bfloat16)
    window = latent_cache.shape[1]
    slot_ids = jnp.arange(window, dtype=jnp.int32)
    newest = cache_lengths - 1
    position = newest[:, None] - jnp.mod(newest[:, None] - slot_ids[None, :], window)
    usable = ((position >= 0) & (position > cache_lengths[:, None] - window))[:, None, :]
    cache_scores = (
        jnp.einsum("rhc,rsc->rhs", dec_query, latent_cache, preferred_element_type=jnp.float32)
        * scale_qk
    )
    own_scores = (
        jnp.einsum("rhc,rc->rh", dec_query, dec_latent, preferred_element_type=jnp.float32)
        * scale_qk
    )
    cache_masked = jnp.where(usable, cache_scores, NEG_FILL)
    top_score = jnp.maximum(
        jnp.maximum(jnp.max(cache_masked, axis=2), own_scores), sink_logits[None, :]
    )
    cache_exp = jnp.where(usable, jnp.exp(cache_masked - top_score[:, :, None]), 0.0)
    own_exp = jnp.exp(own_scores - top_score)
    dec_numer = jnp.einsum(
        "rhs,rsl->rhl",
        cache_exp.astype(jnp.bfloat16),
        latent_cache[:, :, :LATENT],
        preferred_element_type=jnp.float32,
    )
    dec_numer = dec_numer + own_exp.astype(jnp.bfloat16).astype(jnp.float32)[
        :, :, None
    ] * dec_latent[:, None, :LATENT].astype(jnp.float32)
    dec_total = jnp.sum(cache_exp, axis=2) + own_exp + jnp.exp(sink_logits[None, :] - top_score)
    dec_att = (dec_numer / dec_total[:, :, None]).astype(jnp.bfloat16)
    attention = jnp.concatenate([pre_att, dec_att], axis=0)
    spread = lax.all_to_all(attention, "dp", split_axis=1, concat_axis=0, tiled=True)
    uv_full, out_full = weights["uv"], weights["out"]
    head_values = jnp.einsum(
        "thl,hlv->thv", spread, uv_full, preferred_element_type=jnp.float32
    ).astype(jnp.bfloat16)
    head_partial = jnp.einsum(
        "thv,hvd->td", head_values, out_full, preferred_element_type=jnp.float32
    )
    attn_out = lax.psum_scatter(
        head_partial.astype(jnp.bfloat16), "dp", scatter_dimension=0, tiled=True
    ).astype(jnp.float32)
    resid = jnp.concatenate([pre_resid, dec_resid], axis=0)
    hidden = (resid.astype(jnp.float32) + attn_out).astype(jnp.bfloat16)
    hidden_up = lax.optimization_barrier(hidden).astype(jnp.float32)
    mean_square = jnp.mean(hidden_up * hidden_up, axis=1, keepdims=True)
    normed = (
        hidden_up * lax.rsqrt(mean_square + NORM_EPS) * norm_gain.astype(jnp.float32)[None, :]
    ).astype(jnp.bfloat16)
    capacity = max(2, (rows_dev * TOPK + members - 1) // members)
    route_row = routes.astype(jnp.bfloat16).reshape(1, rows_dev * TOPK)
    route_row = jnp.pad(route_row, ((0, 0), (0, D - rows_dev * TOPK)))
    own_slots = assign_slots(routes, members)
    own_matrix = dispatch_matrix(routes, own_slots, members, capacity).reshape(
        rows_dev, members, capacity
    )
    outgoing = jnp.einsum("rxc,rd->xcd", own_matrix, normed, preferred_element_type=jnp.bfloat16)
    arrived = lax.all_to_all(outgoing, "expert", split_axis=0, concat_axis=0, tiled=True)
    slots_in = members * capacity
    combined = jnp.concatenate([arrived.reshape(slots_in, D), normed, route_row], axis=0)
    group_all = lax.all_gather(combined[None], "dp", axis=0, tiled=True)
    expert_rows = group_all[:, :slots_in].reshape(-1, D)
    group_tokens = group_all[:, slots_in : slots_in + rows_dev].reshape(groups * rows_dev, D)
    group_routes = (
        group_all[:, slots_in + rows_dev, : rows_dev * TOPK].astype(jnp.int32).reshape(-1, TOPK)
    )
    routes_by_group = group_routes.reshape(groups, rows_dev, TOPK)
    slots_by_group = jax.vmap(partial(assign_slots, experts=members))(routes_by_group)
    shared_ready = (
        weights["shared_gate"],
        weights["shared_up"],
        weights["shared_down"],
        weights["router"],
    )
    gate_proj = jnp.dot(expert_rows, gate_weight[0], preferred_element_type=jnp.float32)
    up_proj = jnp.dot(expert_rows, up_weight[0], preferred_element_type=jnp.float32)
    expert_act = (jax.nn.silu(gate_proj) * up_proj).astype(jnp.bfloat16)
    shared_gate_full, shared_up_full, shared_down_full, router_full = shared_ready
    shared_act = (
        jax.nn.silu(jnp.dot(group_tokens, shared_gate_full, preferred_element_type=jnp.float32))
        * jnp.dot(group_tokens, shared_up_full, preferred_element_type=jnp.float32)
    ).astype(jnp.bfloat16)
    down_local = down_weight[0]
    col_width = down_local.shape[1]
    both_acts = jnp.concatenate([expert_act, shared_act], axis=0)
    both_pieces = lax.all_gather(both_acts, "dp", axis=1, tiled=True)
    routed_piece = both_pieces[: expert_act.shape[0]]
    shared_piece = both_pieces[expert_act.shape[0] :]
    routed_cols = jnp.dot(routed_piece, down_local, preferred_element_type=jnp.float32)
    shared_cols = jnp.dot(shared_piece, shared_down_full, preferred_element_type=jnp.float32)
    expert_out = routed_cols.astype(jnp.bfloat16)
    shared_out = shared_cols.astype(jnp.bfloat16)
    expert_out = jnp.swapaxes(expert_out.reshape(groups, members, capacity, col_width), 0, 1)
    returned = lax.all_to_all(
        expert_out.reshape(members, groups * capacity, col_width),
        "expert",
        split_axis=0,
        concat_axis=0,
        tiled=True,
    )
    group_offset = (jnp.arange(groups, dtype=jnp.int32) * capacity)[:, None, None]
    lookup = (routes_by_group * (groups * capacity) + group_offset + slots_by_group).reshape(
        groups * rows_dev, TOPK
    )
    picked = jnp.take(returned.reshape(-1, col_width), lookup, axis=0)
    group_logits = jnp.dot(group_tokens, router_full, preferred_element_type=jnp.float32)
    picked_scores = jax.nn.sigmoid(
        jnp.take_along_axis(group_logits, group_routes.reshape(-1, TOPK), axis=1)
    )
    route_weight = ROUTE_SCALE * picked_scores / jnp.sum(picked_scores, axis=1, keepdims=True)
    moe_cols = shared_out.astype(jnp.float32) + jnp.sum(
        route_weight[:, :, None] * picked.astype(jnp.float32), axis=1
    )
    moe_home = lax.all_to_all(
        moe_cols.reshape(groups, rows_dev, col_width).astype(jnp.bfloat16),
        "dp",
        split_axis=0,
        concat_axis=2,
        tiled=True,
    ).astype(jnp.float32)
    final = (hidden_up + moe_home[0]).astype(jnp.bfloat16)
    return (final[:pre_rows], final[pre_rows:])


def solution(mesh):
    in_specs = (
        P(("dp", "expert"), None, None),
        P(("dp", "expert"), None),
        P(("dp", "expert"), None),
        P(("dp", "expert"), None, None),
        P(("dp", "expert"), None),
        P(("dp", "expert"), None),
        P(("dp", "expert")),
        P(("dp", "expert"), None, None),
        P(),
        P("dp", "expert", None),
        P("dp", "expert", None),
        P(),
        P(None, "expert"),
        P(("dp", "expert"), None),
        P("expert", None, "dp"),
        P("expert", None, "dp"),
        P("expert", None, "dp"),
        P("expert", "dp"),
        P("expert", "dp"),
        P("expert", "dp"),
    )
    out_specs = (P(("dp", "expert"), None), P(("dp", "expert"), None))
    return jax.shard_map(shards, mesh=mesh, in_specs=in_specs, out_specs=out_specs, check_vma=False)
```

```python
from functools import partial

import jax
import jax.numpy as jnp
from jax import lax
from jax.experimental import pallas as pl
from jax.experimental.pallas import tpu as pltpu
from jax.sharding import PartitionSpec as P

D = 2048
LATENT = 512
ROPE = 64
QK_NOPE = 128
TOPK = 6


ROUTE_SCALE = 2.446
NORM_EPS = 1e-06
NEG_FILL = -1e30


def assign_slots(route_rows, experts):
    flat_routes = route_rows.reshape(-1)
    one_hot = (flat_routes[:, None] == jnp.arange(experts, dtype=jnp.int32)[None, :]).astype(
        jnp.int32
    )
    running = jnp.cumsum(one_hot, axis=0)
    slot_rank = jnp.sum(running * one_hot, axis=1) - 1
    return slot_rank.reshape(route_rows.shape)


def dispatch_matrix(route_rows, slot_rows, experts, capacity):
    target = route_rows * capacity + slot_rows
    places = jnp.arange(experts * capacity, dtype=jnp.int32)
    total = jnp.zeros((route_rows.shape[0], experts * capacity), jnp.bfloat16)
    for column in range(route_rows.shape[1]):
        total = total + (target[:, column][:, None] == places[None, :]).astype(jnp.bfloat16)
    return total


MESH_ID = pl.DeviceIdType.MESH


def gather_kernel(nx, nz, shard_ref, out_ref, xs_sem, xr_sem, own_sem, rs_sem, ls_sem, rr_sem):
    d = lax.axis_index("dp")
    e = lax.axis_index("expert")
    x = e // nz
    z = e % nz
    right = x * nz + (z + 1) % nz
    left = x * nz + (z + nz - 1) % nz
    steps_r = nz // 2
    steps_l = nz - 1 - steps_r

    barrier = pltpu.get_barrier_semaphore()
    for k in range(1, nx):
        peer = ((x + k) % nx) * nz + z
        pl.semaphore_signal(barrier, 1, device_id=(d, peer), device_id_type=MESH_ID)
    greeted = nx - 1
    if nz > 1:
        pl.semaphore_signal(barrier, 1, device_id=(d, right), device_id_type=MESH_ID)
        greeted += 1
    if nz > 2:
        pl.semaphore_signal(barrier, 1, device_id=(d, left), device_id_type=MESH_ID)
        greeted += 1
    if greeted:
        pl.semaphore_wait(barrier, greeted)

    own = pltpu.make_async_copy(shard_ref, out_ref.at[z, x], own_sem)
    own.start()
    x_copies = []
    for k in range(1, nx):
        px = (x + k) % nx
        send = pltpu.make_async_remote_copy(
            src_ref=shard_ref,
            dst_ref=out_ref.at[z, x],
            send_sem=xs_sem.at[k],
            recv_sem=xr_sem.at[x],
            device_id=(d, px * nz + z),
            device_id_type=MESH_ID,
        )
        send.start()
        x_copies.append(send)
    own.wait()
    for k in range(1, nx):
        px = (x + k) % nx
        incoming = pltpu.make_async_remote_copy(
            src_ref=shard_ref,
            dst_ref=out_ref.at[z, px],
            send_sem=xs_sem.at[k],
            recv_sem=xr_sem.at[px],
            device_id=(d, px * nz + z),
            device_id_type=MESH_ID,
        )
        incoming.wait_recv()

    def ring_copy(group, sems, step, target):
        return pltpu.make_async_remote_copy(
            src_ref=out_ref.at[group],
            dst_ref=out_ref.at[group],
            send_sem=sems.at[step],
            recv_sem=rr_sem.at[group],
            device_id=(d, target),
            device_id_type=MESH_ID,
        )

    sent = []
    for s in range(max(steps_r, steps_l)):
        if s < steps_r:
            group = (z - s + nz) % nz
            if s > 0:
                ring_copy(group, rs_sem, s, right).wait_recv()
            c = ring_copy(group, rs_sem, s, right)
            c.start()
            sent.append(c)
        if s < steps_l:
            group = (z + s) % nz
            if s > 0:
                ring_copy(group, ls_sem, s, left).wait_recv()
            c = ring_copy(group, ls_sem, s, left)
            c.start()
            sent.append(c)
    if steps_r > 0:
        ring_copy((z - steps_r + nz) % nz, rs_sem, 0, right).wait_recv()
    if steps_l > 0:
        ring_copy((z + steps_l) % nz, ls_sem, 0, left).wait_recv()
    for c in sent:
        c.wait_send()
    for c in x_copies:
        c.wait_send()


def expert_gather(flat, members):
    nz = 16 if members % 16 == 0 else members
    nx = members // nz
    rows, lanes = flat.shape
    steps = max(nz // 2, 1)
    out = pl.pallas_call(
        partial(gather_kernel, nx, nz),
        out_shape=jax.ShapeDtypeStruct((nz, nx, rows, lanes), flat.dtype),
        in_specs=[pl.BlockSpec(memory_space=pltpu.VMEM)],
        out_specs=pl.BlockSpec(memory_space=pltpu.VMEM),
        scratch_shapes=[
            pltpu.SemaphoreType.DMA((max(nx, 1),)),
            pltpu.SemaphoreType.DMA((max(nx, 1),)),
            pltpu.SemaphoreType.DMA(()),
            pltpu.SemaphoreType.DMA((steps,)),
            pltpu.SemaphoreType.DMA((steps,)),
            pltpu.SemaphoreType.DMA((nz,)),
        ],
        compiler_params=pltpu.CompilerParams(collective_id=0, has_side_effects=True),
    )(flat)
    return jnp.swapaxes(out, 0, 1).reshape(members, rows * lanes)


def gather_weights(members, by_kernel, **parts):
    names = list(parts)
    flat = jnp.concatenate([parts[n][0].reshape(-1) for n in names])
    lanes = 128
    total = flat.shape[0]
    padded = -(-total // (lanes * 8)) * lanes * 8
    flat = jnp.pad(flat, (0, padded - total)).reshape(padded // lanes, lanes)
    if by_kernel:
        everyone = expert_gather(flat, members)
    else:
        everyone = lax.all_gather(flat[None], "expert", axis=0, tiled=True)
        everyone = everyone.reshape(members, padded)
    out = {}
    start = 0
    for n in names:
        local, axis = parts[n]
        size = local.size
        piece = everyone[:, start : start + size].reshape((members,) + local.shape)
        piece = jnp.moveaxis(piece, 0, axis)
        shape = list(local.shape)
        shape[axis] *= members
        out[n] = piece.reshape(shape)
        start += size
    return out


def shards(
    pre_query,
    pre_latent,
    pre_resid,
    dec_query,
    dec_latent,
    dec_resid,
    cache_lengths,
    latent_cache,
    sink_logits,
    uv_weight,
    out_weight,
    norm_gain,
    router,
    routes,
    gate_weight,
    up_weight,
    down_weight,
    shared_gate,
    shared_up,
    shared_down,
):
    groups = lax.axis_size("dp")
    members = lax.axis_size("expert")
    pre_rows = pre_query.shape[0]
    rows_dev = pre_rows + 1
    scale_qk = (QK_NOPE + ROPE) ** (-0.5)
    weights = gather_weights(
        members,
        True,
        uv=(uv_weight, 1),
        out=(out_weight, 1),
        shared_gate=(shared_gate, 0),
        shared_up=(shared_up, 0),
        shared_down=(shared_down, 0),
        router=(router, 1),
    )
    pre_scores = (
        jnp.einsum("thc,uc->thu", pre_query, pre_latent, preferred_element_type=jnp.float32)
        * scale_qk
    )
    places = jnp.arange(pre_rows, dtype=jnp.int32)
    allowed = (places[None, :] <= places[:, None])[:, None, :]
    masked = jnp.where(allowed, pre_scores, NEG_FILL)
    pre_max = jnp.maximum(jnp.max(masked, axis=2), sink_logits[None, :])
    exp_terms = jnp.where(allowed, jnp.exp(masked - pre_max[:, :, None]), 0.0)
    denominator = jnp.sum(exp_terms, axis=2) + jnp.exp(sink_logits[None, :] - pre_max)
    numerator = jnp.einsum(
        "thu,ul->thl",
        exp_terms.astype(jnp.bfloat16),
        pre_latent[:, :LATENT],
        preferred_element_type=jnp.float32,
    )
    pre_att = (numerator / denominator[:, :, None]).astype(jnp.bfloat16)
    window = latent_cache.shape[1]
    slot_ids = jnp.arange(window, dtype=jnp.int32)
    newest = cache_lengths - 1
    position = newest[:, None] - jnp.mod(newest[:, None] - slot_ids[None, :], window)
    usable = ((position >= 0) & (position > cache_lengths[:, None] - window))[:, None, :]
    cache_scores = (
        jnp.einsum("rhc,rsc->rhs", dec_query, latent_cache, preferred_element_type=jnp.float32)
        * scale_qk
    )
    own_scores = (
        jnp.einsum("rhc,rc->rh", dec_query, dec_latent, preferred_element_type=jnp.float32)
        * scale_qk
    )
    cache_masked = jnp.where(usable, cache_scores, NEG_FILL)
    top_score = jnp.maximum(
        jnp.maximum(jnp.max(cache_masked, axis=2), own_scores), sink_logits[None, :]
    )
    cache_exp = jnp.where(usable, jnp.exp(cache_masked - top_score[:, :, None]), 0.0)
    own_exp = jnp.exp(own_scores - top_score)
    dec_numer = jnp.einsum(
        "rhs,rsl->rhl",
        cache_exp.astype(jnp.bfloat16),
        latent_cache[:, :, :LATENT],
        preferred_element_type=jnp.float32,
    )
    dec_numer = dec_numer + own_exp.astype(jnp.bfloat16).astype(jnp.float32)[
        :, :, None
    ] * dec_latent[:, None, :LATENT].astype(jnp.float32)
    dec_total = jnp.sum(cache_exp, axis=2) + own_exp + jnp.exp(sink_logits[None, :] - top_score)
    dec_att = (dec_numer / dec_total[:, :, None]).astype(jnp.bfloat16)
    attention = jnp.concatenate([pre_att, dec_att], axis=0)
    spread = lax.all_to_all(attention, "dp", split_axis=1, concat_axis=0, tiled=True)
    uv_full, out_full = weights["uv"], weights["out"]
    head_values = jnp.einsum(
        "thl,hlv->thv", spread, uv_full, preferred_element_type=jnp.float32
    ).astype(jnp.bfloat16)
    head_partial = jnp.einsum(
        "thv,hvd->td", head_values, out_full, preferred_element_type=jnp.float32
    )
    aligned = 32
    padded_partial = jnp.pad(
        head_partial.astype(jnp.bfloat16).reshape(groups, rows_dev, D),
        ((0, 0), (0, aligned - rows_dev), (0, 0)),
    ).reshape(groups * aligned, D)
    attn_out = lax.psum_scatter(padded_partial, "dp", scatter_dimension=0, tiled=True)
    attn_out = attn_out[:rows_dev].astype(jnp.float32)
    resid = jnp.concatenate([pre_resid, dec_resid], axis=0)
    hidden = (resid.astype(jnp.float32) + attn_out).astype(jnp.bfloat16)
    hidden_up = lax.optimization_barrier(hidden).astype(jnp.float32)
    mean_square = jnp.mean(hidden_up * hidden_up, axis=1, keepdims=True)
    normed = (
        hidden_up * lax.rsqrt(mean_square + NORM_EPS) * norm_gain.astype(jnp.float32)[None, :]
    ).astype(jnp.bfloat16)
    capacity = max(2, (rows_dev * TOPK + members - 1) // members)
    route_row = routes.astype(jnp.bfloat16).reshape(1, rows_dev * TOPK)
    route_row = jnp.pad(route_row, ((0, 0), (0, D - rows_dev * TOPK)))
    group_both = lax.all_gather(
        jnp.concatenate([normed, route_row], axis=0)[None], "dp", axis=0, tiled=True
    )
    group_tokens = group_both[:, :rows_dev].reshape(groups * rows_dev, D)
    group_routes = (
        group_both[:, rows_dev, : rows_dev * TOPK].astype(jnp.int32).reshape(-1, TOPK)
    )
    routes_by_group = group_routes.reshape(groups, rows_dev, TOPK)
    slots_by_group = jax.vmap(partial(assign_slots, experts=members))(routes_by_group)
    own_slots = assign_slots(routes, members)
    own_matrix = dispatch_matrix(routes, own_slots, members, capacity).reshape(
        rows_dev, members, capacity
    )
    outgoing = jnp.einsum("rxc,rd->xcd", own_matrix, normed, preferred_element_type=jnp.bfloat16)
    arrived = lax.all_to_all(outgoing, "expert", split_axis=0, concat_axis=0, tiled=True)
    shared_ready = (
        weights["shared_gate"],
        weights["shared_up"],
        weights["shared_down"],
        weights["router"],
    )
    expert_rows = lax.all_gather(
        arrived.reshape(members, 1, capacity, D), "dp", axis=1, tiled=True
    )
    expert_rows = expert_rows.reshape(-1, D)
    gate_proj = jnp.dot(expert_rows, gate_weight[0], preferred_element_type=jnp.float32)
    up_proj = jnp.dot(expert_rows, up_weight[0], preferred_element_type=jnp.float32)
    expert_act = (jax.nn.silu(gate_proj) * up_proj).astype(jnp.bfloat16)
    shared_gate_full, shared_up_full, shared_down_full, router_full = shared_ready
    shared_act = (
        jax.nn.silu(jnp.dot(group_tokens, shared_gate_full, preferred_element_type=jnp.float32))
        * jnp.dot(group_tokens, shared_up_full, preferred_element_type=jnp.float32)
    ).astype(jnp.bfloat16)
    down_local = down_weight[0]
    col_width = down_local.shape[1]
    routed_piece = lax.all_gather(expert_act, "dp", axis=1, tiled=True)
    shared_piece = lax.all_gather(shared_act, "dp", axis=1, tiled=True)
    routed_cols = jnp.dot(routed_piece, down_local, preferred_element_type=jnp.float32)
    shared_cols = jnp.dot(shared_piece, shared_down_full, preferred_element_type=jnp.float32)
    expert_out = routed_cols.astype(jnp.bfloat16)
    shared_out = shared_cols.astype(jnp.bfloat16)
    returned = lax.all_to_all(
        expert_out.reshape(members, groups * capacity, col_width),
        "expert",
        split_axis=0,
        concat_axis=0,
        tiled=True,
    )
    group_offset = (jnp.arange(groups, dtype=jnp.int32) * capacity)[:, None, None]
    lookup = (routes_by_group * (groups * capacity) + group_offset + slots_by_group).reshape(
        groups * rows_dev, TOPK
    )
    picked = jnp.take(returned.reshape(-1, col_width), lookup, axis=0)
    group_logits = jnp.dot(group_tokens, router_full, preferred_element_type=jnp.float32)
    picked_scores = jax.nn.sigmoid(
        jnp.take_along_axis(group_logits, group_routes.reshape(-1, TOPK), axis=1)
    )
    route_weight = ROUTE_SCALE * picked_scores / jnp.sum(picked_scores, axis=1, keepdims=True)
    moe_cols = shared_out.astype(jnp.float32) + jnp.sum(
        route_weight[:, :, None] * picked.astype(jnp.float32), axis=1
    )
    moe_home = lax.all_to_all(
        moe_cols.reshape(groups, rows_dev, col_width).astype(jnp.bfloat16),
        "dp",
        split_axis=0,
        concat_axis=2,
        tiled=True,
    ).astype(jnp.float32)
    final = (hidden_up + moe_home[0]).astype(jnp.bfloat16)
    return (final[:pre_rows], final[pre_rows:])


def solution(mesh):
    in_specs = (
        P(("dp", "expert"), None, None),
        P(("dp", "expert"), None),
        P(("dp", "expert"), None),
        P(("dp", "expert"), None, None),
        P(("dp", "expert"), None),
        P(("dp", "expert"), None),
        P(("dp", "expert")),
        P(("dp", "expert"), None, None),
        P(),
        P("dp", "expert", None),
        P("dp", "expert", None),
        P(),
        P(None, "expert"),
        P(("dp", "expert"), None),
        P("expert", None, "dp"),
        P("expert", None, "dp"),
        P("expert", None, "dp"),
        P("expert", "dp"),
        P("expert", "dp"),
        P("expert", "dp"),
    )
    out_specs = (P(("dp", "expert"), None), P(("dp", "expert"), None))
    return jax.shard_map(shards, mesh=mesh, in_specs=in_specs, out_specs=out_specs, check_vma=False)
```

```python
from functools import partial

import jax
import jax.numpy as jnp
from jax import lax
from jax.experimental import pallas as pl
from jax.experimental.pallas import tpu as pltpu
from jax.sharding import PartitionSpec as P

D = 2048
LATENT = 512
ROPE = 64
QK_NOPE = 128
TOPK = 6


ROUTE_SCALE = 2.446
NORM_EPS = 1e-06
NEG_FILL = -1e30


def assign_slots(route_rows, experts):
    flat_routes = route_rows.reshape(-1)
    one_hot = (flat_routes[:, None] == jnp.arange(experts, dtype=jnp.int32)[None, :]).astype(
        jnp.int32
    )
    running = jnp.cumsum(one_hot, axis=0)
    slot_rank = jnp.sum(running * one_hot, axis=1) - 1
    return slot_rank.reshape(route_rows.shape)


def dispatch_matrix(route_rows, slot_rows, experts, capacity):
    target = route_rows * capacity + slot_rows
    places = jnp.arange(experts * capacity, dtype=jnp.int32)
    total = jnp.zeros((route_rows.shape[0], experts * capacity), jnp.bfloat16)
    for column in range(route_rows.shape[1]):
        total = total + (target[:, column][:, None] == places[None, :]).astype(jnp.bfloat16)
    return total


MESH_ID = pl.DeviceIdType.MESH


def gather_kernel(nx, nz, shard_ref, out_ref, xs_sem, xr_sem, own_sem, rs_sem, ls_sem, rr_sem):
    d = lax.axis_index("dp")
    e = lax.axis_index("expert")
    x = e // nz
    z = e % nz
    right = x * nz + (z + 1) % nz
    left = x * nz + (z + nz - 1) % nz
    steps_r = nz // 2
    steps_l = nz - 1 - steps_r

    barrier = pltpu.get_barrier_semaphore()
    for k in range(1, nx):
        peer = ((x + k) % nx) * nz + z
        pl.semaphore_signal(barrier, 1, device_id=(d, peer), device_id_type=MESH_ID)
    greeted = nx - 1
    if nz > 1:
        pl.semaphore_signal(barrier, 1, device_id=(d, right), device_id_type=MESH_ID)
        greeted += 1
    if nz > 2:
        pl.semaphore_signal(barrier, 1, device_id=(d, left), device_id_type=MESH_ID)
        greeted += 1
    if greeted:
        pl.semaphore_wait(barrier, greeted)

    own = pltpu.make_async_copy(shard_ref, out_ref.at[z, x], own_sem)
    own.start()
    x_copies = []
    for k in range(1, nx):
        px = (x + k) % nx
        send = pltpu.make_async_remote_copy(
            src_ref=shard_ref,
            dst_ref=out_ref.at[z, x],
            send_sem=xs_sem.at[k],
            recv_sem=xr_sem.at[x],
            device_id=(d, px * nz + z),
            device_id_type=MESH_ID,
        )
        send.start()
        x_copies.append(send)
    own.wait()
    for k in range(1, nx):
        px = (x + k) % nx
        incoming = pltpu.make_async_remote_copy(
            src_ref=shard_ref,
            dst_ref=out_ref.at[z, px],
            send_sem=xs_sem.at[k],
            recv_sem=xr_sem.at[px],
            device_id=(d, px * nz + z),
            device_id_type=MESH_ID,
        )
        incoming.wait_recv()

    def ring_copy(group, sems, step, target):
        return pltpu.make_async_remote_copy(
            src_ref=out_ref.at[group],
            dst_ref=out_ref.at[group],
            send_sem=sems.at[step],
            recv_sem=rr_sem.at[group],
            device_id=(d, target),
            device_id_type=MESH_ID,
        )

    sent = []
    for s in range(max(steps_r, steps_l)):
        if s < steps_r:
            group = (z - s + nz) % nz
            if s > 0:
                ring_copy(group, rs_sem, s, right).wait_recv()
            c = ring_copy(group, rs_sem, s, right)
            c.start()
            sent.append(c)
        if s < steps_l:
            group = (z + s) % nz
            if s > 0:
                ring_copy(group, ls_sem, s, left).wait_recv()
            c = ring_copy(group, ls_sem, s, left)
            c.start()
            sent.append(c)
    if steps_r > 0:
        ring_copy((z - steps_r + nz) % nz, rs_sem, 0, right).wait_recv()
    if steps_l > 0:
        ring_copy((z + steps_l) % nz, ls_sem, 0, left).wait_recv()
    for c in sent:
        c.wait_send()
    for c in x_copies:
        c.wait_send()


def expert_gather(flat, members):
    nz = 16 if members % 16 == 0 else members
    nx = members // nz
    rows, lanes = flat.shape
    steps = max(nz // 2, 1)
    out = pl.pallas_call(
        partial(gather_kernel, nx, nz),
        out_shape=jax.ShapeDtypeStruct((nz, nx, rows, lanes), flat.dtype),
        in_specs=[pl.BlockSpec(memory_space=pltpu.VMEM)],
        out_specs=pl.BlockSpec(memory_space=pltpu.VMEM),
        scratch_shapes=[
            pltpu.SemaphoreType.DMA((max(nx, 1),)),
            pltpu.SemaphoreType.DMA((max(nx, 1),)),
            pltpu.SemaphoreType.DMA(()),
            pltpu.SemaphoreType.DMA((steps,)),
            pltpu.SemaphoreType.DMA((steps,)),
            pltpu.SemaphoreType.DMA((nz,)),
        ],
        compiler_params=pltpu.CompilerParams(collective_id=0, has_side_effects=True),
    )(flat)
    return jnp.swapaxes(out, 0, 1).reshape(members, rows * lanes)


def gather_weights(members, by_kernel, **parts):
    names = list(parts)
    flat = jnp.concatenate([parts[n][0].reshape(-1) for n in names])
    lanes = 128
    total = flat.shape[0]
    padded = -(-total // (lanes * 8)) * lanes * 8
    flat = jnp.pad(flat, (0, padded - total)).reshape(padded // lanes, lanes)
    if by_kernel:
        everyone = expert_gather(flat, members)
    else:
        everyone = lax.all_gather(flat[None], "expert", axis=0, tiled=True)
        everyone = everyone.reshape(members, padded)
    out = {}
    start = 0
    for n in names:
        local, axis = parts[n]
        size = local.size
        piece = everyone[:, start : start + size].reshape((members,) + local.shape)
        piece = jnp.moveaxis(piece, 0, axis)
        shape = list(local.shape)
        shape[axis] *= members
        out[n] = piece.reshape(shape)
        start += size
    return out


def shards(
    pre_query,
    pre_latent,
    pre_resid,
    dec_query,
    dec_latent,
    dec_resid,
    cache_lengths,
    latent_cache,
    sink_logits,
    uv_weight,
    out_weight,
    norm_gain,
    router,
    routes,
    gate_weight,
    up_weight,
    down_weight,
    shared_gate,
    shared_up,
    shared_down,
):
    groups = lax.axis_size("dp")
    members = lax.axis_size("expert")
    pre_rows = pre_query.shape[0]
    rows_dev = pre_rows + 1
    scale_qk = (QK_NOPE + ROPE) ** (-0.5)
    weights = gather_weights(
        members,
        True,
        uv=(uv_weight, 1),
        out=(out_weight, 1),
        shared_gate=(shared_gate, 0),
        shared_up=(shared_up, 0),
        shared_down=(shared_down, 0),
        router=(router, 1),
    )
    pre_scores = (
        jnp.einsum("thc,uc->thu", pre_query, pre_latent, preferred_element_type=jnp.float32)
        * scale_qk
    )
    places = jnp.arange(pre_rows, dtype=jnp.int32)
    allowed = (places[None, :] <= places[:, None])[:, None, :]
    masked = jnp.where(allowed, pre_scores, NEG_FILL)
    pre_max = jnp.maximum(jnp.max(masked, axis=2), sink_logits[None, :])
    exp_terms = jnp.where(allowed, jnp.exp(masked - pre_max[:, :, None]), 0.0)
    denominator = jnp.sum(exp_terms, axis=2) + jnp.exp(sink_logits[None, :] - pre_max)
    numerator = jnp.einsum(
        "thu,ul->thl",
        exp_terms.astype(jnp.bfloat16),
        pre_latent[:, :LATENT],
        preferred_element_type=jnp.float32,
    )
    pre_att = (numerator / denominator[:, :, None]).astype(jnp.bfloat16)
    window = latent_cache.shape[1]
    slot_ids = jnp.arange(window, dtype=jnp.int32)
    newest = cache_lengths - 1
    position = newest[:, None] - jnp.mod(newest[:, None] - slot_ids[None, :], window)
    usable = ((position >= 0) & (position > cache_lengths[:, None] - window))[:, None, :]
    cache_scores = (
        jnp.einsum("rhc,rsc->rhs", dec_query, latent_cache, preferred_element_type=jnp.float32)
        * scale_qk
    )
    own_scores = (
        jnp.einsum("rhc,rc->rh", dec_query, dec_latent, preferred_element_type=jnp.float32)
        * scale_qk
    )
    cache_masked = jnp.where(usable, cache_scores, NEG_FILL)
    top_score = jnp.maximum(
        jnp.maximum(jnp.max(cache_masked, axis=2), own_scores), sink_logits[None, :]
    )
    cache_exp = jnp.where(usable, jnp.exp(cache_masked - top_score[:, :, None]), 0.0)
    own_exp = jnp.exp(own_scores - top_score)
    dec_numer = jnp.einsum(
        "rhs,rsl->rhl",
        cache_exp.astype(jnp.bfloat16),
        latent_cache[:, :, :LATENT],
        preferred_element_type=jnp.float32,
    )
    dec_numer = dec_numer + own_exp.astype(jnp.bfloat16).astype(jnp.float32)[
        :, :, None
    ] * dec_latent[:, None, :LATENT].astype(jnp.float32)
    dec_total = jnp.sum(cache_exp, axis=2) + own_exp + jnp.exp(sink_logits[None, :] - top_score)
    dec_att = (dec_numer / dec_total[:, :, None]).astype(jnp.bfloat16)
    attention = jnp.concatenate([pre_att, dec_att], axis=0)
    spread = lax.all_to_all(attention, "dp", split_axis=1, concat_axis=0, tiled=True)
    uv_full, out_full = weights["uv"], weights["out"]
    head_values = jnp.einsum(
        "thl,hlv->thv", spread, uv_full, preferred_element_type=jnp.float32
    ).astype(jnp.bfloat16)
    head_partial = jnp.einsum(
        "thv,hvd->td", head_values, out_full, preferred_element_type=jnp.float32
    )
    attn_out = lax.psum_scatter(
        head_partial.astype(jnp.bfloat16), "dp", scatter_dimension=0, tiled=True
    ).astype(jnp.float32)
    resid = jnp.concatenate([pre_resid, dec_resid], axis=0)
    hidden = (resid.astype(jnp.float32) + attn_out).astype(jnp.bfloat16)
    hidden_up = lax.optimization_barrier(hidden).astype(jnp.float32)
    mean_square = jnp.mean(hidden_up * hidden_up, axis=1, keepdims=True)
    normed = (
        hidden_up * lax.rsqrt(mean_square + NORM_EPS) * norm_gain.astype(jnp.float32)[None, :]
    ).astype(jnp.bfloat16)
    capacity = max(2, (rows_dev * TOPK + members - 1) // members)
    route_row = routes.astype(jnp.bfloat16).reshape(1, rows_dev * TOPK)
    route_row = jnp.pad(route_row, ((0, 0), (0, D - rows_dev * TOPK)))
    own_slots = assign_slots(routes, members)
    own_matrix = dispatch_matrix(routes, own_slots, members, capacity).reshape(
        rows_dev, members, capacity
    )
    outgoing = jnp.einsum("rxc,rd->xcd", own_matrix, normed, preferred_element_type=jnp.bfloat16)
    arrived = lax.all_to_all(outgoing, "expert", split_axis=0, concat_axis=0, tiled=True)
    shared_ready = (
        weights["shared_gate"],
        weights["shared_up"],
        weights["shared_down"],
        weights["router"],
    )
    expert_rows = lax.all_gather(
        arrived.reshape(members, 1, capacity, D), "dp", axis=1, tiled=True
    )
    expert_rows = expert_rows.reshape(-1, D)
    own_both, _ = lax.optimization_barrier(
        (jnp.concatenate([normed, route_row], axis=0), arrived)
    )
    group_both = lax.all_gather(own_both[None], "dp", axis=0, tiled=True)
    expert_rows, group_both = lax.optimization_barrier((expert_rows, group_both))
    group_tokens = group_both[:, :rows_dev].reshape(groups * rows_dev, D)
    group_routes = (
        group_both[:, rows_dev, : rows_dev * TOPK].astype(jnp.int32).reshape(-1, TOPK)
    )
    routes_by_group = group_routes.reshape(groups, rows_dev, TOPK)
    slots_by_group = jax.vmap(partial(assign_slots, experts=members))(routes_by_group)
    gate_proj = jnp.dot(expert_rows, gate_weight[0], preferred_element_type=jnp.float32)
    up_proj = jnp.dot(expert_rows, up_weight[0], preferred_element_type=jnp.float32)
    expert_act = (jax.nn.silu(gate_proj) * up_proj).astype(jnp.bfloat16)
    shared_gate_full, shared_up_full, shared_down_full, router_full = shared_ready
    shared_act = (
        jax.nn.silu(jnp.dot(group_tokens, shared_gate_full, preferred_element_type=jnp.float32))
        * jnp.dot(group_tokens, shared_up_full, preferred_element_type=jnp.float32)
    ).astype(jnp.bfloat16)
    down_local = down_weight[0]
    col_width = down_local.shape[1]
    routed_piece = lax.all_gather(expert_act, "dp", axis=1, tiled=True)
    shared_piece = lax.all_gather(shared_act, "dp", axis=1, tiled=True)
    routed_cols = jnp.dot(routed_piece, down_local, preferred_element_type=jnp.float32)
    shared_cols = jnp.dot(shared_piece, shared_down_full, preferred_element_type=jnp.float32)
    expert_out = routed_cols.astype(jnp.bfloat16)
    shared_out = shared_cols.astype(jnp.bfloat16)
    returned = lax.all_to_all(
        expert_out.reshape(members, groups * capacity, col_width),
        "expert",
        split_axis=0,
        concat_axis=0,
        tiled=True,
    )
    group_offset = (jnp.arange(groups, dtype=jnp.int32) * capacity)[:, None, None]
    lookup = (routes_by_group * (groups * capacity) + group_offset + slots_by_group).reshape(
        groups * rows_dev, TOPK
    )
    picked = jnp.take(returned.reshape(-1, col_width), lookup, axis=0)
    group_logits = jnp.dot(group_tokens, router_full, preferred_element_type=jnp.float32)
    picked_scores = jax.nn.sigmoid(
        jnp.take_along_axis(group_logits, group_routes.reshape(-1, TOPK), axis=1)
    )
    route_weight = ROUTE_SCALE * picked_scores / jnp.sum(picked_scores, axis=1, keepdims=True)
    moe_cols = shared_out.astype(jnp.float32) + jnp.sum(
        route_weight[:, :, None] * picked.astype(jnp.float32), axis=1
    )
    moe_home = lax.all_to_all(
        moe_cols.reshape(groups, rows_dev, col_width).astype(jnp.bfloat16),
        "dp",
        split_axis=0,
        concat_axis=2,
        tiled=True,
    ).astype(jnp.float32)
    final = (hidden_up + moe_home[0]).astype(jnp.bfloat16)
    return (final[:pre_rows], final[pre_rows:])


def solution(mesh):
    in_specs = (
        P(("dp", "expert"), None, None),
        P(("dp", "expert"), None),
        P(("dp", "expert"), None),
        P(("dp", "expert"), None, None),
        P(("dp", "expert"), None),
        P(("dp", "expert"), None),
        P(("dp", "expert")),
        P(("dp", "expert"), None, None),
        P(),
        P("dp", "expert", None),
        P("dp", "expert", None),
        P(),
        P(None, "expert"),
        P(("dp", "expert"), None),
        P("expert", None, "dp"),
        P("expert", None, "dp"),
        P("expert", None, "dp"),
        P("expert", "dp"),
        P("expert", "dp"),
        P("expert", "dp"),
    )
    out_specs = (P(("dp", "expert"), None), P(("dp", "expert"), None))
    return jax.shard_map(shards, mesh=mesh, in_specs=in_specs, out_specs=out_specs, check_vma=False)
```

```python
from functools import partial

import jax
import jax.numpy as jnp
from jax import lax
from jax.experimental import pallas as pl
from jax.experimental.pallas import tpu as pltpu
from jax.sharding import PartitionSpec as P

D = 2048
LATENT = 512
ROPE = 64
QK_NOPE = 128
TOPK = 6


ROUTE_SCALE = 2.446
NORM_EPS = 1e-06
NEG_FILL = -1e30


def assign_slots(route_rows, experts):
    flat_routes = route_rows.reshape(-1)
    one_hot = (flat_routes[:, None] == jnp.arange(experts, dtype=jnp.int32)[None, :]).astype(
        jnp.int32
    )
    running = jnp.cumsum(one_hot, axis=0)
    slot_rank = jnp.sum(running * one_hot, axis=1) - 1
    return slot_rank.reshape(route_rows.shape)


def dispatch_matrix(route_rows, slot_rows, experts, capacity):
    target = route_rows * capacity + slot_rows
    places = jnp.arange(experts * capacity, dtype=jnp.int32)
    total = jnp.zeros((route_rows.shape[0], experts * capacity), jnp.bfloat16)
    for column in range(route_rows.shape[1]):
        total = total + (target[:, column][:, None] == places[None, :]).astype(jnp.bfloat16)
    return total


MESH_ID = pl.DeviceIdType.MESH


def gather_kernel(nx, nz, shard_ref, out_ref, xs_sem, xr_sem, own_sem, rs_sem, ls_sem, rr_sem):
    d = lax.axis_index("dp")
    e = lax.axis_index("expert")
    x = e // nz
    z = e % nz
    right = x * nz + (z + 1) % nz
    left = x * nz + (z + nz - 1) % nz
    steps_r = nz // 2
    steps_l = nz - 1 - steps_r

    barrier = pltpu.get_barrier_semaphore()
    for k in range(1, nx):
        peer = ((x + k) % nx) * nz + z
        pl.semaphore_signal(barrier, 1, device_id=(d, peer), device_id_type=MESH_ID)
    greeted = nx - 1
    if nz > 1:
        pl.semaphore_signal(barrier, 1, device_id=(d, right), device_id_type=MESH_ID)
        greeted += 1
    if nz > 2:
        pl.semaphore_signal(barrier, 1, device_id=(d, left), device_id_type=MESH_ID)
        greeted += 1
    if greeted:
        pl.semaphore_wait(barrier, greeted)

    own = pltpu.make_async_copy(shard_ref, out_ref.at[z, x], own_sem)
    own.start()
    x_copies = []
    for k in range(1, nx):
        px = (x + k) % nx
        send = pltpu.make_async_remote_copy(
            src_ref=shard_ref,
            dst_ref=out_ref.at[z, x],
            send_sem=xs_sem.at[k],
            recv_sem=xr_sem.at[x],
            device_id=(d, px * nz + z),
            device_id_type=MESH_ID,
        )
        send.start()
        x_copies.append(send)
    own.wait()
    for k in range(1, nx):
        px = (x + k) % nx
        incoming = pltpu.make_async_remote_copy(
            src_ref=shard_ref,
            dst_ref=out_ref.at[z, px],
            send_sem=xs_sem.at[k],
            recv_sem=xr_sem.at[px],
            device_id=(d, px * nz + z),
            device_id_type=MESH_ID,
        )
        incoming.wait_recv()

    def ring_copy(group, sems, step, target):
        return pltpu.make_async_remote_copy(
            src_ref=out_ref.at[group],
            dst_ref=out_ref.at[group],
            send_sem=sems.at[step],
            recv_sem=rr_sem.at[group],
            device_id=(d, target),
            device_id_type=MESH_ID,
        )

    sent = []
    for s in range(max(steps_r, steps_l)):
        if s < steps_r:
            group = (z - s + nz) % nz
            if s > 0:
                ring_copy(group, rs_sem, s, right).wait_recv()
            c = ring_copy(group, rs_sem, s, right)
            c.start()
            sent.append(c)
        if s < steps_l:
            group = (z + s) % nz
            if s > 0:
                ring_copy(group, ls_sem, s, left).wait_recv()
            c = ring_copy(group, ls_sem, s, left)
            c.start()
            sent.append(c)
    if steps_r > 0:
        ring_copy((z - steps_r + nz) % nz, rs_sem, 0, right).wait_recv()
    if steps_l > 0:
        ring_copy((z + steps_l) % nz, ls_sem, 0, left).wait_recv()
    for c in sent:
        c.wait_send()
    for c in x_copies:
        c.wait_send()


def exchange_kernel(members, send_ref, recv_ref, send_sem, recv_sem, own_sem):
    d = lax.axis_index("dp")
    e = lax.axis_index("expert")
    barrier = pltpu.get_barrier_semaphore()
    for k in range(1, members):
        peer = (e + k) % members
        pl.semaphore_signal(barrier, 1, device_id=(d, peer), device_id_type=MESH_ID)
    pl.semaphore_wait(barrier, members - 1)

    def remote(peer, slot):
        return pltpu.make_async_remote_copy(
            src_ref=send_ref.at[peer],
            dst_ref=recv_ref.at[slot],
            send_sem=send_sem.at[peer],
            recv_sem=recv_sem.at[slot],
            device_id=(d, peer),
            device_id_type=MESH_ID,
        )

    own = pltpu.make_async_copy(send_ref.at[e], recv_ref.at[e], own_sem)
    own.start()

    def start(k, carry):
        remote((e + k) % members, e).start()
        return carry

    lax.fori_loop(1, members, start, 0)
    own.wait()

    def finish(k, carry):
        remote((e + members - k) % members, (e + members - k) % members).wait_recv()
        remote((e + k) % members, e).wait_send()
        return carry

    lax.fori_loop(1, members, finish, 0)


def expert_exchange(outgoing, members):
    return pl.pallas_call(
        partial(exchange_kernel, members),
        out_shape=jax.ShapeDtypeStruct(outgoing.shape, outgoing.dtype),
        in_specs=[pl.BlockSpec(memory_space=pltpu.VMEM)],
        out_specs=pl.BlockSpec(memory_space=pltpu.VMEM),
        scratch_shapes=[
            pltpu.SemaphoreType.DMA((members,)),
            pltpu.SemaphoreType.DMA((members,)),
            pltpu.SemaphoreType.DMA(()),
        ],
        compiler_params=pltpu.CompilerParams(collective_id=1, has_side_effects=True),
    )(outgoing)


def expert_gather(flat, members):
    nz = 16 if members % 16 == 0 else members
    nx = members // nz
    rows, lanes = flat.shape
    steps = max(nz // 2, 1)
    out = pl.pallas_call(
        partial(gather_kernel, nx, nz),
        out_shape=jax.ShapeDtypeStruct((nz, nx, rows, lanes), flat.dtype),
        in_specs=[pl.BlockSpec(memory_space=pltpu.VMEM)],
        out_specs=pl.BlockSpec(memory_space=pltpu.VMEM),
        scratch_shapes=[
            pltpu.SemaphoreType.DMA((max(nx, 1),)),
            pltpu.SemaphoreType.DMA((max(nx, 1),)),
            pltpu.SemaphoreType.DMA(()),
            pltpu.SemaphoreType.DMA((steps,)),
            pltpu.SemaphoreType.DMA((steps,)),
            pltpu.SemaphoreType.DMA((nz,)),
        ],
        compiler_params=pltpu.CompilerParams(collective_id=0, has_side_effects=True),
    )(flat)
    return jnp.swapaxes(out, 0, 1).reshape(members, rows * lanes)


def gather_weights(members, by_kernel, **parts):
    names = list(parts)
    flat = jnp.concatenate([parts[n][0].reshape(-1) for n in names])
    lanes = 128
    total = flat.shape[0]
    padded = -(-total // (lanes * 8)) * lanes * 8
    flat = jnp.pad(flat, (0, padded - total)).reshape(padded // lanes, lanes)
    if by_kernel:
        everyone = expert_gather(flat, members)
    else:
        everyone = lax.all_gather(flat[None], "expert", axis=0, tiled=True)
        everyone = everyone.reshape(members, padded)
    out = {}
    start = 0
    for n in names:
        local, axis = parts[n]
        size = local.size
        piece = everyone[:, start : start + size].reshape((members,) + local.shape)
        piece = jnp.moveaxis(piece, 0, axis)
        shape = list(local.shape)
        shape[axis] *= members
        out[n] = piece.reshape(shape)
        start += size
    return out


def shards(
    pre_query,
    pre_latent,
    pre_resid,
    dec_query,
    dec_latent,
    dec_resid,
    cache_lengths,
    latent_cache,
    sink_logits,
    uv_weight,
    out_weight,
    norm_gain,
    router,
    routes,
    gate_weight,
    up_weight,
    down_weight,
    shared_gate,
    shared_up,
    shared_down,
):
    groups = lax.axis_size("dp")
    members = lax.axis_size("expert")
    pre_rows = pre_query.shape[0]
    rows_dev = pre_rows + 1
    scale_qk = (QK_NOPE + ROPE) ** (-0.5)
    weights = gather_weights(
        members,
        True,
        uv=(uv_weight, 1),
        out=(out_weight, 1),
        shared_gate=(shared_gate, 0),
        shared_up=(shared_up, 0),
        shared_down=(shared_down, 0),
        router=(router, 1),
    )
    pre_scores = (
        jnp.einsum("thc,uc->thu", pre_query, pre_latent, preferred_element_type=jnp.float32)
        * scale_qk
    )
    places = jnp.arange(pre_rows, dtype=jnp.int32)
    allowed = (places[None, :] <= places[:, None])[:, None, :]
    masked = jnp.where(allowed, pre_scores, NEG_FILL)
    pre_max = jnp.maximum(jnp.max(masked, axis=2), sink_logits[None, :])
    exp_terms = jnp.where(allowed, jnp.exp(masked - pre_max[:, :, None]), 0.0)
    denominator = jnp.sum(exp_terms, axis=2) + jnp.exp(sink_logits[None, :] - pre_max)
    numerator = jnp.einsum(
        "thu,ul->thl",
        exp_terms.astype(jnp.bfloat16),
        pre_latent[:, :LATENT],
        preferred_element_type=jnp.float32,
    )
    pre_att = (numerator / denominator[:, :, None]).astype(jnp.bfloat16)
    window = latent_cache.shape[1]
    slot_ids = jnp.arange(window, dtype=jnp.int32)
    newest = cache_lengths - 1
    position = newest[:, None] - jnp.mod(newest[:, None] - slot_ids[None, :], window)
    usable = ((position >= 0) & (position > cache_lengths[:, None] - window))[:, None, :]
    cache_scores = (
        jnp.einsum("rhc,rsc->rhs", dec_query, latent_cache, preferred_element_type=jnp.float32)
        * scale_qk
    )
    own_scores = (
        jnp.einsum("rhc,rc->rh", dec_query, dec_latent, preferred_element_type=jnp.float32)
        * scale_qk
    )
    cache_masked = jnp.where(usable, cache_scores, NEG_FILL)
    top_score = jnp.maximum(
        jnp.maximum(jnp.max(cache_masked, axis=2), own_scores), sink_logits[None, :]
    )
    cache_exp = jnp.where(usable, jnp.exp(cache_masked - top_score[:, :, None]), 0.0)
    own_exp = jnp.exp(own_scores - top_score)
    dec_numer = jnp.einsum(
        "rhs,rsl->rhl",
        cache_exp.astype(jnp.bfloat16),
        latent_cache[:, :, :LATENT],
        preferred_element_type=jnp.float32,
    )
    dec_numer = dec_numer + own_exp.astype(jnp.bfloat16).astype(jnp.float32)[
        :, :, None
    ] * dec_latent[:, None, :LATENT].astype(jnp.float32)
    dec_total = jnp.sum(cache_exp, axis=2) + own_exp + jnp.exp(sink_logits[None, :] - top_score)
    dec_att = (dec_numer / dec_total[:, :, None]).astype(jnp.bfloat16)
    attention = jnp.concatenate([pre_att, dec_att], axis=0)
    spread = lax.all_to_all(attention, "dp", split_axis=1, concat_axis=0, tiled=True)
    uv_full, out_full = weights["uv"], weights["out"]
    head_values = jnp.einsum(
        "thl,hlv->thv", spread, uv_full, preferred_element_type=jnp.float32
    ).astype(jnp.bfloat16)
    head_partial = jnp.einsum(
        "thv,hvd->td", head_values, out_full, preferred_element_type=jnp.float32
    )
    attn_out = lax.psum_scatter(
        head_partial.astype(jnp.bfloat16), "dp", scatter_dimension=0, tiled=True
    ).astype(jnp.float32)
    resid = jnp.concatenate([pre_resid, dec_resid], axis=0)
    hidden = (resid.astype(jnp.float32) + attn_out).astype(jnp.bfloat16)
    hidden_up = lax.optimization_barrier(hidden).astype(jnp.float32)
    mean_square = jnp.mean(hidden_up * hidden_up, axis=1, keepdims=True)
    normed = (
        hidden_up * lax.rsqrt(mean_square + NORM_EPS) * norm_gain.astype(jnp.float32)[None, :]
    ).astype(jnp.bfloat16)
    capacity = max(2, (rows_dev * TOPK + members - 1) // members)
    route_row = routes.astype(jnp.bfloat16).reshape(1, rows_dev * TOPK)
    route_row = jnp.pad(route_row, ((0, 0), (0, D - rows_dev * TOPK)))
    own_slots = assign_slots(routes, members)
    own_matrix = dispatch_matrix(routes, own_slots, members, capacity).reshape(
        rows_dev, members, capacity
    )
    outgoing = jnp.einsum("rxc,rd->xcd", own_matrix, normed, preferred_element_type=jnp.bfloat16)
    arrived = expert_exchange(outgoing, members)
    shared_ready = (
        weights["shared_gate"],
        weights["shared_up"],
        weights["shared_down"],
        weights["router"],
    )
    expert_rows = lax.all_gather(
        arrived.reshape(members, 1, capacity, D), "dp", axis=1, tiled=True
    )
    expert_rows = expert_rows.reshape(-1, D)
    own_both, _ = lax.optimization_barrier(
        (jnp.concatenate([normed, route_row], axis=0), arrived)
    )
    group_both = lax.all_gather(own_both[None], "dp", axis=0, tiled=True)
    expert_rows, group_both = lax.optimization_barrier((expert_rows, group_both))
    group_tokens = group_both[:, :rows_dev].reshape(groups * rows_dev, D)
    group_routes = (
        group_both[:, rows_dev, : rows_dev * TOPK].astype(jnp.int32).reshape(-1, TOPK)
    )
    routes_by_group = group_routes.reshape(groups, rows_dev, TOPK)
    slots_by_group = jax.vmap(partial(assign_slots, experts=members))(routes_by_group)
    gate_proj = jnp.dot(expert_rows, gate_weight[0], preferred_element_type=jnp.float32)
    up_proj = jnp.dot(expert_rows, up_weight[0], preferred_element_type=jnp.float32)
    expert_act = (jax.nn.silu(gate_proj) * up_proj).astype(jnp.bfloat16)
    shared_gate_full, shared_up_full, shared_down_full, router_full = shared_ready
    shared_act = (
        jax.nn.silu(jnp.dot(group_tokens, shared_gate_full, preferred_element_type=jnp.float32))
        * jnp.dot(group_tokens, shared_up_full, preferred_element_type=jnp.float32)
    ).astype(jnp.bfloat16)
    down_local = down_weight[0]
    col_width = down_local.shape[1]
    routed_piece = lax.all_gather(expert_act, "dp", axis=1, tiled=True)
    shared_piece = lax.all_gather(shared_act, "dp", axis=1, tiled=True)
    routed_cols = jnp.dot(routed_piece, down_local, preferred_element_type=jnp.float32)
    shared_cols = jnp.dot(shared_piece, shared_down_full, preferred_element_type=jnp.float32)
    expert_out = routed_cols.astype(jnp.bfloat16)
    shared_out = shared_cols.astype(jnp.bfloat16)
    returned = lax.all_to_all(
        expert_out.reshape(members, groups * capacity, col_width),
        "expert",
        split_axis=0,
        concat_axis=0,
        tiled=True,
    )
    group_offset = (jnp.arange(groups, dtype=jnp.int32) * capacity)[:, None, None]
    lookup = (routes_by_group * (groups * capacity) + group_offset + slots_by_group).reshape(
        groups * rows_dev, TOPK
    )
    picked = jnp.take(returned.reshape(-1, col_width), lookup, axis=0)
    group_logits = jnp.dot(group_tokens, router_full, preferred_element_type=jnp.float32)
    picked_scores = jax.nn.sigmoid(
        jnp.take_along_axis(group_logits, group_routes.reshape(-1, TOPK), axis=1)
    )
    route_weight = ROUTE_SCALE * picked_scores / jnp.sum(picked_scores, axis=1, keepdims=True)
    moe_cols = shared_out.astype(jnp.float32) + jnp.sum(
        route_weight[:, :, None] * picked.astype(jnp.float32), axis=1
    )
    moe_home = lax.all_to_all(
        moe_cols.reshape(groups, rows_dev, col_width).astype(jnp.bfloat16),
        "dp",
        split_axis=0,
        concat_axis=2,
        tiled=True,
    ).astype(jnp.float32)
    final = (hidden_up + moe_home[0]).astype(jnp.bfloat16)
    return (final[:pre_rows], final[pre_rows:])


def solution(mesh):
    in_specs = (
        P(("dp", "expert"), None, None),
        P(("dp", "expert"), None),
        P(("dp", "expert"), None),
        P(("dp", "expert"), None, None),
        P(("dp", "expert"), None),
        P(("dp", "expert"), None),
        P(("dp", "expert")),
        P(("dp", "expert"), None, None),
        P(),
        P("dp", "expert", None),
        P("dp", "expert", None),
        P(),
        P(None, "expert"),
        P(("dp", "expert"), None),
        P("expert", None, "dp"),
        P("expert", None, "dp"),
        P("expert", None, "dp"),
        P("expert", "dp"),
        P("expert", "dp"),
        P("expert", "dp"),
    )
    out_specs = (P(("dp", "expert"), None), P(("dp", "expert"), None))
    return jax.shard_map(shards, mesh=mesh, in_specs=in_specs, out_specs=out_specs, check_vma=False)
```

```python
from functools import partial

import jax
import jax.numpy as jnp
from jax import lax
from jax.experimental import pallas as pl
from jax.experimental.pallas import tpu as pltpu
from jax.sharding import PartitionSpec as P

D = 2048
LATENT = 512
ROPE = 64
QK_NOPE = 128
TOPK = 6


ROUTE_SCALE = 2.446
NORM_EPS = 1e-06
NEG_FILL = -1e30


def assign_slots(route_rows, experts):
    flat_routes = route_rows.reshape(-1)
    one_hot = (flat_routes[:, None] == jnp.arange(experts, dtype=jnp.int32)[None, :]).astype(
        jnp.int32
    )
    running = jnp.cumsum(one_hot, axis=0)
    slot_rank = jnp.sum(running * one_hot, axis=1) - 1
    return slot_rank.reshape(route_rows.shape)


def dispatch_matrix(route_rows, slot_rows, experts, capacity):
    target = route_rows * capacity + slot_rows
    places = jnp.arange(experts * capacity, dtype=jnp.int32)
    total = jnp.zeros((route_rows.shape[0], experts * capacity), jnp.bfloat16)
    for column in range(route_rows.shape[1]):
        total = total + (target[:, column][:, None] == places[None, :]).astype(jnp.bfloat16)
    return total


MESH_ID = pl.DeviceIdType.MESH


def gather_kernel(nx, nz, shard_ref, out_ref, xs_sem, xr_sem, own_sem, rs_sem, ls_sem, rr_sem):
    d = lax.axis_index("dp")
    e = lax.axis_index("expert")
    x = e // nz
    z = e % nz
    right = x * nz + (z + 1) % nz
    left = x * nz + (z + nz - 1) % nz
    steps_r = nz // 2
    steps_l = nz - 1 - steps_r

    barrier = pltpu.get_barrier_semaphore()
    for k in range(1, nx):
        peer = ((x + k) % nx) * nz + z
        pl.semaphore_signal(barrier, 1, device_id=(d, peer), device_id_type=MESH_ID)
    greeted = nx - 1
    if nz > 1:
        pl.semaphore_signal(barrier, 1, device_id=(d, right), device_id_type=MESH_ID)
        greeted += 1
    if nz > 2:
        pl.semaphore_signal(barrier, 1, device_id=(d, left), device_id_type=MESH_ID)
        greeted += 1
    if greeted:
        pl.semaphore_wait(barrier, greeted)

    own = pltpu.make_async_copy(shard_ref, out_ref.at[z, x], own_sem)
    own.start()
    x_copies = []
    for k in range(1, nx):
        px = (x + k) % nx
        send = pltpu.make_async_remote_copy(
            src_ref=shard_ref,
            dst_ref=out_ref.at[z, x],
            send_sem=xs_sem.at[k],
            recv_sem=xr_sem.at[x],
            device_id=(d, px * nz + z),
            device_id_type=MESH_ID,
        )
        send.start()
        x_copies.append(send)
    own.wait()
    for k in range(1, nx):
        px = (x + k) % nx
        incoming = pltpu.make_async_remote_copy(
            src_ref=shard_ref,
            dst_ref=out_ref.at[z, px],
            send_sem=xs_sem.at[k],
            recv_sem=xr_sem.at[px],
            device_id=(d, px * nz + z),
            device_id_type=MESH_ID,
        )
        incoming.wait_recv()

    def ring_copy(group, sems, step, target):
        return pltpu.make_async_remote_copy(
            src_ref=out_ref.at[group],
            dst_ref=out_ref.at[group],
            send_sem=sems.at[step],
            recv_sem=rr_sem.at[group],
            device_id=(d, target),
            device_id_type=MESH_ID,
        )

    sent = []
    for s in range(max(steps_r, steps_l)):
        if s < steps_r:
            group = (z - s + nz) % nz
            if s > 0:
                ring_copy(group, rs_sem, s, right).wait_recv()
            c = ring_copy(group, rs_sem, s, right)
            c.start()
            sent.append(c)
        if s < steps_l:
            group = (z + s) % nz
            if s > 0:
                ring_copy(group, ls_sem, s, left).wait_recv()
            c = ring_copy(group, ls_sem, s, left)
            c.start()
            sent.append(c)
    if steps_r > 0:
        ring_copy((z - steps_r + nz) % nz, rs_sem, 0, right).wait_recv()
    if steps_l > 0:
        ring_copy((z + steps_l) % nz, ls_sem, 0, left).wait_recv()
    for c in sent:
        c.wait_send()
    for c in x_copies:
        c.wait_send()


def expert_gather(flat, members):
    nz = 16 if members % 16 == 0 else members
    nx = members // nz
    rows, lanes = flat.shape
    steps = max(nz // 2, 1)
    out = pl.pallas_call(
        partial(gather_kernel, nx, nz),
        out_shape=jax.ShapeDtypeStruct((nz, nx, rows, lanes), flat.dtype),
        in_specs=[pl.BlockSpec(memory_space=pltpu.VMEM)],
        out_specs=pl.BlockSpec(memory_space=pltpu.VMEM),
        scratch_shapes=[
            pltpu.SemaphoreType.DMA((max(nx, 1),)),
            pltpu.SemaphoreType.DMA((max(nx, 1),)),
            pltpu.SemaphoreType.DMA(()),
            pltpu.SemaphoreType.DMA((steps,)),
            pltpu.SemaphoreType.DMA((steps,)),
            pltpu.SemaphoreType.DMA((nz,)),
        ],
        compiler_params=pltpu.CompilerParams(collective_id=0, has_side_effects=True),
    )(flat)
    return jnp.swapaxes(out, 0, 1).reshape(members, rows * lanes)


def gather_weights(members, by_kernel, **parts):
    names = list(parts)
    flat = jnp.concatenate([parts[n][0].reshape(-1) for n in names])
    lanes = 128
    total = flat.shape[0]
    padded = -(-total // (lanes * 8)) * lanes * 8
    flat = jnp.pad(flat, (0, padded - total)).reshape(padded // lanes, lanes)
    if by_kernel:
        everyone = expert_gather(flat, members)
    else:
        everyone = lax.all_gather(flat[None], "expert", axis=0, tiled=True)
        everyone = everyone.reshape(members, padded)
    out = {}
    start = 0
    for n in names:
        local, axis = parts[n]
        size = local.size
        piece = everyone[:, start : start + size].reshape((members,) + local.shape)
        piece = jnp.moveaxis(piece, 0, axis)
        shape = list(local.shape)
        shape[axis] *= members
        out[n] = piece.reshape(shape)
        start += size
    return out


def shards(
    pre_query,
    pre_latent,
    pre_resid,
    dec_query,
    dec_latent,
    dec_resid,
    cache_lengths,
    latent_cache,
    sink_logits,
    uv_weight,
    out_weight,
    norm_gain,
    router,
    routes,
    gate_weight,
    up_weight,
    down_weight,
    shared_gate,
    shared_up,
    shared_down,
):
    groups = lax.axis_size("dp")
    members = lax.axis_size("expert")
    pre_rows = pre_query.shape[0]
    rows_dev = pre_rows + 1
    scale_qk = (QK_NOPE + ROPE) ** (-0.5)
    weights = gather_weights(
        members,
        True,
        uv=(uv_weight, 1),
        out=(out_weight, 1),
        shared_gate=(shared_gate, 0),
        shared_up=(shared_up, 0),
        shared_down=(shared_down, 0),
        router=(router, 1),
    )
    pre_scores = (
        jnp.einsum("thc,uc->thu", pre_query, pre_latent, preferred_element_type=jnp.float32)
        * scale_qk
    )
    places = jnp.arange(pre_rows, dtype=jnp.int32)
    allowed = (places[None, :] <= places[:, None])[:, None, :]
    masked = jnp.where(allowed, pre_scores, NEG_FILL)
    pre_max = jnp.maximum(jnp.max(masked, axis=2), sink_logits[None, :])
    exp_terms = jnp.where(allowed, jnp.exp(masked - pre_max[:, :, None]), 0.0)
    denominator = jnp.sum(exp_terms, axis=2) + jnp.exp(sink_logits[None, :] - pre_max)
    numerator = jnp.einsum(
        "thu,ul->thl",
        exp_terms.astype(jnp.bfloat16),
        pre_latent[:, :LATENT],
        preferred_element_type=jnp.float32,
    )
    pre_att = (numerator / denominator[:, :, None]).astype(jnp.bfloat16)
    window = latent_cache.shape[1]
    slot_ids = jnp.arange(window, dtype=jnp.int32)
    newest = cache_lengths - 1
    position = newest[:, None] - jnp.mod(newest[:, None] - slot_ids[None, :], window)
    usable = ((position >= 0) & (position > cache_lengths[:, None] - window))[:, None, :]
    cache_scores = (
        jnp.einsum("rhc,rsc->rhs", dec_query, latent_cache, preferred_element_type=jnp.float32)
        * scale_qk
    )
    own_scores = (
        jnp.einsum("rhc,rc->rh", dec_query, dec_latent, preferred_element_type=jnp.float32)
        * scale_qk
    )
    cache_masked = jnp.where(usable, cache_scores, NEG_FILL)
    top_score = jnp.maximum(
        jnp.maximum(jnp.max(cache_masked, axis=2), own_scores), sink_logits[None, :]
    )
    cache_exp = jnp.where(usable, jnp.exp(cache_masked - top_score[:, :, None]), 0.0)
    own_exp = jnp.exp(own_scores - top_score)
    dec_numer = jnp.einsum(
        "rhs,rsl->rhl",
        cache_exp.astype(jnp.bfloat16),
        latent_cache[:, :, :LATENT],
        preferred_element_type=jnp.float32,
    )
    dec_numer = dec_numer + own_exp.astype(jnp.bfloat16).astype(jnp.float32)[
        :, :, None
    ] * dec_latent[:, None, :LATENT].astype(jnp.float32)
    dec_total = jnp.sum(cache_exp, axis=2) + own_exp + jnp.exp(sink_logits[None, :] - top_score)
    dec_att = (dec_numer / dec_total[:, :, None]).astype(jnp.bfloat16)
    attention = jnp.concatenate([pre_att, dec_att], axis=0)
    spread = lax.all_to_all(attention, "dp", split_axis=1, concat_axis=0, tiled=True)
    uv_full, out_full = weights["uv"], weights["out"]
    head_values = jnp.einsum(
        "thl,hlv->thv", spread, uv_full, preferred_element_type=jnp.float32
    ).astype(jnp.bfloat16)
    head_partial = jnp.einsum(
        "thv,hvd->td", head_values, out_full, preferred_element_type=jnp.float32
    )
    attn_out = lax.psum_scatter(
        head_partial.astype(jnp.bfloat16), "dp", scatter_dimension=0, tiled=True
    ).astype(jnp.float32)
    resid = jnp.concatenate([pre_resid, dec_resid], axis=0)
    hidden = (resid.astype(jnp.float32) + attn_out).astype(jnp.bfloat16)
    hidden_up = lax.optimization_barrier(hidden).astype(jnp.float32)
    mean_square = jnp.mean(hidden_up * hidden_up, axis=1, keepdims=True)
    normed = (
        hidden_up * lax.rsqrt(mean_square + NORM_EPS) * norm_gain.astype(jnp.float32)[None, :]
    ).astype(jnp.bfloat16)
    capacity = max(2, (rows_dev * TOPK + members - 1) // members)
    route_row = routes.astype(jnp.bfloat16).reshape(1, rows_dev * TOPK)
    route_row = jnp.pad(route_row, ((0, 0), (0, D - rows_dev * TOPK)))
    own_slots = assign_slots(routes, members)
    own_matrix = dispatch_matrix(routes, own_slots, members, capacity).reshape(
        rows_dev, members, capacity
    )
    outgoing = jnp.einsum("rxc,rd->xcd", own_matrix, normed, preferred_element_type=jnp.bfloat16)
    arrived = lax.all_to_all(outgoing, "expert", split_axis=0, concat_axis=0, tiled=True)
    shared_ready = (
        weights["shared_gate"],
        weights["shared_up"],
        weights["shared_down"],
        weights["router"],
    )
    expert_rows = lax.all_gather(
        arrived.reshape(members, 1, capacity, D), "dp", axis=1, tiled=True
    )
    expert_rows = expert_rows.reshape(-1, D)
    own_both, _ = lax.optimization_barrier(
        (jnp.concatenate([normed, route_row], axis=0), arrived)
    )
    group_both = lax.all_gather(own_both[None], "dp", axis=0, tiled=True)
    expert_rows, group_both = lax.optimization_barrier((expert_rows, group_both))
    group_tokens = group_both[:, :rows_dev].reshape(groups * rows_dev, D)
    group_routes = (
        group_both[:, rows_dev, : rows_dev * TOPK].astype(jnp.int32).reshape(-1, TOPK)
    )
    routes_by_group = group_routes.reshape(groups, rows_dev, TOPK)
    slots_by_group = jax.vmap(partial(assign_slots, experts=members))(routes_by_group)
    gate_proj = jnp.dot(expert_rows, gate_weight[0], preferred_element_type=jnp.float32)
    up_proj = jnp.dot(expert_rows, up_weight[0], preferred_element_type=jnp.float32)
    expert_act = (jax.nn.silu(gate_proj) * up_proj).astype(jnp.bfloat16)
    shared_gate_full, shared_up_full, shared_down_full, router_full = shared_ready
    shared_tokens, expert_act = lax.optimization_barrier((group_tokens, expert_act))
    shared_act = (
        jax.nn.silu(jnp.dot(shared_tokens, shared_gate_full, preferred_element_type=jnp.float32))
        * jnp.dot(shared_tokens, shared_up_full, preferred_element_type=jnp.float32)
    ).astype(jnp.bfloat16)
    down_local = down_weight[0]
    col_width = down_local.shape[1]
    routed_piece = lax.all_gather(expert_act, "dp", axis=1, tiled=True)
    shared_piece = lax.all_gather(shared_act, "dp", axis=1, tiled=True)
    routed_piece, shared_piece = lax.optimization_barrier((routed_piece, shared_piece))
    routed_cols = jnp.dot(routed_piece, down_local, preferred_element_type=jnp.float32)
    shared_cols = jnp.dot(shared_piece, shared_down_full, preferred_element_type=jnp.float32)
    expert_out = routed_cols.astype(jnp.bfloat16)
    shared_out = shared_cols.astype(jnp.bfloat16)
    returned = lax.all_to_all(
        expert_out.reshape(members, groups * capacity, col_width),
        "expert",
        split_axis=0,
        concat_axis=0,
        tiled=True,
    )
    group_offset = (jnp.arange(groups, dtype=jnp.int32) * capacity)[:, None, None]
    lookup = (routes_by_group * (groups * capacity) + group_offset + slots_by_group).reshape(
        groups * rows_dev, TOPK
    )
    picked = jnp.take(returned.reshape(-1, col_width), lookup, axis=0)
    group_logits = jnp.dot(group_tokens, router_full, preferred_element_type=jnp.float32)
    picked_scores = jax.nn.sigmoid(
        jnp.take_along_axis(group_logits, group_routes.reshape(-1, TOPK), axis=1)
    )
    route_weight = ROUTE_SCALE * picked_scores / jnp.sum(picked_scores, axis=1, keepdims=True)
    moe_cols = shared_out.astype(jnp.float32) + jnp.sum(
        route_weight[:, :, None] * picked.astype(jnp.float32), axis=1
    )
    moe_home = lax.all_to_all(
        moe_cols.reshape(groups, rows_dev, col_width).astype(jnp.bfloat16),
        "dp",
        split_axis=0,
        concat_axis=2,
        tiled=True,
    ).astype(jnp.float32)
    final = (hidden_up + moe_home[0]).astype(jnp.bfloat16)
    return (final[:pre_rows], final[pre_rows:])


def solution(mesh):
    in_specs = (
        P(("dp", "expert"), None, None),
        P(("dp", "expert"), None),
        P(("dp", "expert"), None),
        P(("dp", "expert"), None, None),
        P(("dp", "expert"), None),
        P(("dp", "expert"), None),
        P(("dp", "expert")),
        P(("dp", "expert"), None, None),
        P(),
        P("dp", "expert", None),
        P("dp", "expert", None),
        P(),
        P(None, "expert"),
        P(("dp", "expert"), None),
        P("expert", None, "dp"),
        P("expert", None, "dp"),
        P("expert", None, "dp"),
        P("expert", "dp"),
        P("expert", "dp"),
        P("expert", "dp"),
    )
    out_specs = (P(("dp", "expert"), None), P(("dp", "expert"), None))
    return jax.shard_map(shards, mesh=mesh, in_specs=in_specs, out_specs=out_specs, check_vma=False)
```

```python
from functools import partial

import jax
import jax.numpy as jnp
from jax import lax
from jax.experimental import pallas as pl
from jax.experimental.pallas import tpu as pltpu
from jax.sharding import PartitionSpec as P

D = 2048
LATENT = 512
ROPE = 64
QK_NOPE = 128
TOPK = 6


ROUTE_SCALE = 2.446
NORM_EPS = 1e-06
NEG_FILL = -1e30


def assign_slots(route_rows, experts):
    flat_routes = route_rows.reshape(-1)
    one_hot = (flat_routes[:, None] == jnp.arange(experts, dtype=jnp.int32)[None, :]).astype(
        jnp.int32
    )
    running = jnp.cumsum(one_hot, axis=0)
    slot_rank = jnp.sum(running * one_hot, axis=1) - 1
    return slot_rank.reshape(route_rows.shape)


def dispatch_matrix(route_rows, slot_rows, experts, capacity):
    target = route_rows * capacity + slot_rows
    places = jnp.arange(experts * capacity, dtype=jnp.int32)
    total = jnp.zeros((route_rows.shape[0], experts * capacity), jnp.bfloat16)
    for column in range(route_rows.shape[1]):
        total = total + (target[:, column][:, None] == places[None, :]).astype(jnp.bfloat16)
    return total


MESH_ID = pl.DeviceIdType.MESH


def gather_kernel(nx, nz, shard_ref, out_ref, xs_sem, xr_sem, own_sem, rs_sem, ls_sem, rr_sem):
    d = lax.axis_index("dp")
    e = lax.axis_index("expert")
    x = e // nz
    z = e % nz
    right = x * nz + (z + 1) % nz
    left = x * nz + (z + nz - 1) % nz
    steps_r = nz // 2
    steps_l = nz - 1 - steps_r

    barrier = pltpu.get_barrier_semaphore()
    for k in range(1, nx):
        peer = ((x + k) % nx) * nz + z
        pl.semaphore_signal(barrier, 1, device_id=(d, peer), device_id_type=MESH_ID)
    greeted = nx - 1
    if nz > 1:
        pl.semaphore_signal(barrier, 1, device_id=(d, right), device_id_type=MESH_ID)
        greeted += 1
    if nz > 2:
        pl.semaphore_signal(barrier, 1, device_id=(d, left), device_id_type=MESH_ID)
        greeted += 1
    if greeted:
        pl.semaphore_wait(barrier, greeted)

    own = pltpu.make_async_copy(shard_ref, out_ref.at[z, x], own_sem)
    own.start()
    x_copies = []
    for k in range(1, nx):
        px = (x + k) % nx
        send = pltpu.make_async_remote_copy(
            src_ref=shard_ref,
            dst_ref=out_ref.at[z, x],
            send_sem=xs_sem.at[k],
            recv_sem=xr_sem.at[x],
            device_id=(d, px * nz + z),
            device_id_type=MESH_ID,
        )
        send.start()
        x_copies.append(send)
    own.wait()
    for k in range(1, nx):
        px = (x + k) % nx
        incoming = pltpu.make_async_remote_copy(
            src_ref=shard_ref,
            dst_ref=out_ref.at[z, px],
            send_sem=xs_sem.at[k],
            recv_sem=xr_sem.at[px],
            device_id=(d, px * nz + z),
            device_id_type=MESH_ID,
        )
        incoming.wait_recv()

    def ring_copy(group, sems, step, target):
        return pltpu.make_async_remote_copy(
            src_ref=out_ref.at[group],
            dst_ref=out_ref.at[group],
            send_sem=sems.at[step],
            recv_sem=rr_sem.at[group],
            device_id=(d, target),
            device_id_type=MESH_ID,
        )

    sent = []
    for s in range(max(steps_r, steps_l)):
        if s < steps_r:
            group = (z - s + nz) % nz
            if s > 0:
                ring_copy(group, rs_sem, s, right).wait_recv()
            c = ring_copy(group, rs_sem, s, right)
            c.start()
            sent.append(c)
        if s < steps_l:
            group = (z + s) % nz
            if s > 0:
                ring_copy(group, ls_sem, s, left).wait_recv()
            c = ring_copy(group, ls_sem, s, left)
            c.start()
            sent.append(c)
    if steps_r > 0:
        ring_copy((z - steps_r + nz) % nz, rs_sem, 0, right).wait_recv()
    if steps_l > 0:
        ring_copy((z + steps_l) % nz, ls_sem, 0, left).wait_recv()
    for c in sent:
        c.wait_send()
    for c in x_copies:
        c.wait_send()


def expert_gather(flat, members):
    nz = 16 if members % 16 == 0 else members
    nx = members // nz
    rows, lanes = flat.shape
    steps = max(nz // 2, 1)
    out = pl.pallas_call(
        partial(gather_kernel, nx, nz),
        out_shape=jax.ShapeDtypeStruct((nz, nx, rows, lanes), flat.dtype),
        in_specs=[pl.BlockSpec(memory_space=pltpu.VMEM)],
        out_specs=pl.BlockSpec(memory_space=pltpu.VMEM),
        scratch_shapes=[
            pltpu.SemaphoreType.DMA((max(nx, 1),)),
            pltpu.SemaphoreType.DMA((max(nx, 1),)),
            pltpu.SemaphoreType.DMA(()),
            pltpu.SemaphoreType.DMA((steps,)),
            pltpu.SemaphoreType.DMA((steps,)),
            pltpu.SemaphoreType.DMA((nz,)),
        ],
        compiler_params=pltpu.CompilerParams(collective_id=0, has_side_effects=True),
    )(flat)
    return jnp.swapaxes(out, 0, 1).reshape(members, rows * lanes)


def gather_weights(members, by_kernel, **parts):
    names = list(parts)
    flat = jnp.concatenate([parts[n][0].reshape(-1) for n in names])
    lanes = 128
    total = flat.shape[0]
    padded = -(-total // (lanes * 8)) * lanes * 8
    flat = jnp.pad(flat, (0, padded - total)).reshape(padded // lanes, lanes)
    if by_kernel:
        everyone = expert_gather(flat, members)
    else:
        everyone = lax.all_gather(flat[None], "expert", axis=0, tiled=True)
        everyone = everyone.reshape(members, padded)
    out = {}
    start = 0
    for n in names:
        local, axis = parts[n]
        size = local.size
        piece = everyone[:, start : start + size].reshape((members,) + local.shape)
        piece = jnp.moveaxis(piece, 0, axis)
        shape = list(local.shape)
        shape[axis] *= members
        out[n] = piece.reshape(shape)
        start += size
    return out


def shards(
    pre_query,
    pre_latent,
    pre_resid,
    dec_query,
    dec_latent,
    dec_resid,
    cache_lengths,
    latent_cache,
    sink_logits,
    uv_weight,
    out_weight,
    norm_gain,
    router,
    routes,
    gate_weight,
    up_weight,
    down_weight,
    shared_gate,
    shared_up,
    shared_down,
):
    groups = lax.axis_size("dp")
    members = lax.axis_size("expert")
    pre_rows = pre_query.shape[0]
    rows_dev = pre_rows + 1
    scale_qk = (QK_NOPE + ROPE) ** (-0.5)
    weights = gather_weights(
        members,
        True,
        uv=(uv_weight, 1),
        out=(out_weight, 1),
        shared_gate=(shared_gate, 0),
        shared_up=(shared_up, 0),
        shared_down=(shared_down, 0),
        router=(router, 1),
    )
    pre_scores = (
        jnp.einsum("thc,uc->thu", pre_query, pre_latent, preferred_element_type=jnp.float32)
        * scale_qk
    )
    places = jnp.arange(pre_rows, dtype=jnp.int32)
    allowed = (places[None, :] <= places[:, None])[:, None, :]
    masked = jnp.where(allowed, pre_scores, NEG_FILL)
    pre_max = jnp.maximum(jnp.max(masked, axis=2), sink_logits[None, :])
    exp_terms = jnp.where(allowed, jnp.exp(masked - pre_max[:, :, None]), 0.0)
    denominator = jnp.sum(exp_terms, axis=2) + jnp.exp(sink_logits[None, :] - pre_max)
    numerator = jnp.einsum(
        "thu,ul->thl",
        exp_terms.astype(jnp.bfloat16),
        pre_latent[:, :LATENT],
        preferred_element_type=jnp.float32,
    )
    pre_att = (numerator / denominator[:, :, None]).astype(jnp.bfloat16)
    window = latent_cache.shape[1]
    slot_ids = jnp.arange(window, dtype=jnp.int32)
    newest = cache_lengths - 1
    position = newest[:, None] - jnp.mod(newest[:, None] - slot_ids[None, :], window)
    usable = ((position >= 0) & (position > cache_lengths[:, None] - window))[:, None, :]
    cache_scores = (
        jnp.einsum("rhc,rsc->rhs", dec_query, latent_cache, preferred_element_type=jnp.float32)
        * scale_qk
    )
    own_scores = (
        jnp.einsum("rhc,rc->rh", dec_query, dec_latent, preferred_element_type=jnp.float32)
        * scale_qk
    )
    cache_masked = jnp.where(usable, cache_scores, NEG_FILL)
    top_score = jnp.maximum(
        jnp.maximum(jnp.max(cache_masked, axis=2), own_scores), sink_logits[None, :]
    )
    cache_exp = jnp.where(usable, jnp.exp(cache_masked - top_score[:, :, None]), 0.0)
    own_exp = jnp.exp(own_scores - top_score)
    dec_numer = jnp.einsum(
        "rhs,rsl->rhl",
        cache_exp.astype(jnp.bfloat16),
        latent_cache[:, :, :LATENT],
        preferred_element_type=jnp.float32,
    )
    dec_numer = dec_numer + own_exp.astype(jnp.bfloat16).astype(jnp.float32)[
        :, :, None
    ] * dec_latent[:, None, :LATENT].astype(jnp.float32)
    dec_total = jnp.sum(cache_exp, axis=2) + own_exp + jnp.exp(sink_logits[None, :] - top_score)
    dec_att = (dec_numer / dec_total[:, :, None]).astype(jnp.bfloat16)
    attention = jnp.concatenate([pre_att, dec_att], axis=0)
    spread = lax.all_to_all(attention, "dp", split_axis=1, concat_axis=0, tiled=True)
    uv_full, out_full = weights["uv"], weights["out"]
    head_values = jnp.einsum(
        "thl,hlv->thv", spread, uv_full, preferred_element_type=jnp.float32
    ).astype(jnp.bfloat16)
    head_partial = jnp.einsum(
        "thv,hvd->td", head_values, out_full, preferred_element_type=jnp.float32
    )
    attn_out = lax.psum_scatter(
        head_partial.astype(jnp.bfloat16), "dp", scatter_dimension=0, tiled=True
    ).astype(jnp.float32)
    resid = jnp.concatenate([pre_resid, dec_resid], axis=0)
    hidden = (resid.astype(jnp.float32) + attn_out).astype(jnp.bfloat16)
    hidden_up = lax.optimization_barrier(hidden).astype(jnp.float32)
    mean_square = jnp.mean(hidden_up * hidden_up, axis=1, keepdims=True)
    normed = (
        hidden_up * lax.rsqrt(mean_square + NORM_EPS) * norm_gain.astype(jnp.float32)[None, :]
    ).astype(jnp.bfloat16)
    capacity = max(2, (rows_dev * TOPK + members - 1) // members)
    route_row = routes.astype(jnp.bfloat16).reshape(1, rows_dev * TOPK)
    route_row = jnp.pad(route_row, ((0, 0), (0, D - rows_dev * TOPK)))
    own_slots = assign_slots(routes, members)
    own_matrix = dispatch_matrix(routes, own_slots, members, capacity).reshape(
        rows_dev, members, capacity
    )
    outgoing = jnp.einsum("rxc,rd->xcd", own_matrix, normed, preferred_element_type=jnp.bfloat16)
    arrived = lax.all_to_all(outgoing, "expert", split_axis=0, concat_axis=0, tiled=True)
    shared_ready = (
        weights["shared_gate"],
        weights["shared_up"],
        weights["shared_down"],
        weights["router"],
    )
    expert_rows = lax.all_gather(arrived[None], "dp", axis=0, tiled=True)
    expert_rows = expert_rows.reshape(-1, D)
    own_both, _ = lax.optimization_barrier(
        (jnp.concatenate([normed, route_row], axis=0), arrived)
    )
    group_both = lax.all_gather(own_both[None], "dp", axis=0, tiled=True)
    expert_rows, group_both = lax.optimization_barrier((expert_rows, group_both))
    group_tokens = group_both[:, :rows_dev].reshape(groups * rows_dev, D)
    group_routes = (
        group_both[:, rows_dev, : rows_dev * TOPK].astype(jnp.int32).reshape(-1, TOPK)
    )
    routes_by_group = group_routes.reshape(groups, rows_dev, TOPK)
    slots_by_group = jax.vmap(partial(assign_slots, experts=members))(routes_by_group)
    gate_proj = jnp.dot(expert_rows, gate_weight[0], preferred_element_type=jnp.float32)
    up_proj = jnp.dot(expert_rows, up_weight[0], preferred_element_type=jnp.float32)
    expert_act = (jax.nn.silu(gate_proj) * up_proj).astype(jnp.bfloat16)
    shared_gate_full, shared_up_full, shared_down_full, router_full = shared_ready
    shared_act = (
        jax.nn.silu(jnp.dot(group_tokens, shared_gate_full, preferred_element_type=jnp.float32))
        * jnp.dot(group_tokens, shared_up_full, preferred_element_type=jnp.float32)
    ).astype(jnp.bfloat16)
    down_local = down_weight[0]
    col_width = down_local.shape[1]
    routed_piece = lax.all_gather(expert_act, "dp", axis=1, tiled=True)
    shared_piece = lax.all_gather(shared_act, "dp", axis=1, tiled=True)
    routed_cols = jnp.dot(routed_piece, down_local, preferred_element_type=jnp.float32)
    shared_cols = jnp.dot(shared_piece, shared_down_full, preferred_element_type=jnp.float32)
    expert_out = routed_cols.astype(jnp.bfloat16)
    shared_out = shared_cols.astype(jnp.bfloat16)
    expert_out = jnp.swapaxes(expert_out.reshape(groups, members, capacity, col_width), 0, 1)
    returned = lax.all_to_all(
        expert_out.reshape(members, groups * capacity, col_width),
        "expert",
        split_axis=0,
        concat_axis=0,
        tiled=True,
    )
    group_offset = (jnp.arange(groups, dtype=jnp.int32) * capacity)[:, None, None]
    lookup = (routes_by_group * (groups * capacity) + group_offset + slots_by_group).reshape(
        groups * rows_dev, TOPK
    )
    picked = jnp.take(returned.reshape(-1, col_width), lookup, axis=0)
    group_logits = jnp.dot(group_tokens, router_full, preferred_element_type=jnp.float32)
    picked_scores = jax.nn.sigmoid(
        jnp.take_along_axis(group_logits, group_routes.reshape(-1, TOPK), axis=1)
    )
    route_weight = ROUTE_SCALE * picked_scores / jnp.sum(picked_scores, axis=1, keepdims=True)
    moe_cols = shared_out.astype(jnp.float32) + jnp.sum(
        route_weight[:, :, None] * picked.astype(jnp.float32), axis=1
    )
    moe_home = lax.all_to_all(
        moe_cols.reshape(groups, rows_dev, col_width).astype(jnp.bfloat16),
        "dp",
        split_axis=0,
        concat_axis=2,
        tiled=True,
    ).astype(jnp.float32)
    final = (hidden_up + moe_home[0]).astype(jnp.bfloat16)
    return (final[:pre_rows], final[pre_rows:])


def solution(mesh):
    in_specs = (
        P(("dp", "expert"), None, None),
        P(("dp", "expert"), None),
        P(("dp", "expert"), None),
        P(("dp", "expert"), None, None),
        P(("dp", "expert"), None),
        P(("dp", "expert"), None),
        P(("dp", "expert")),
        P(("dp", "expert"), None, None),
        P(),
        P("dp", "expert", None),
        P("dp", "expert", None),
        P(),
        P(None, "expert"),
        P(("dp", "expert"), None),
        P("expert", None, "dp"),
        P("expert", None, "dp"),
        P("expert", None, "dp"),
        P("expert", "dp"),
        P("expert", "dp"),
        P("expert", "dp"),
    )
    out_specs = (P(("dp", "expert"), None), P(("dp", "expert"), None))
    return jax.shard_map(shards, mesh=mesh, in_specs=in_specs, out_specs=out_specs, check_vma=False)
```

```python
from functools import partial

import jax
import jax.numpy as jnp
from jax import lax
from jax.experimental import pallas as pl
from jax.experimental.pallas import tpu as pltpu
from jax.sharding import PartitionSpec as P

D = 2048
LATENT = 512
ROPE = 64
QK_NOPE = 128
TOPK = 6


ROUTE_SCALE = 2.446
NORM_EPS = 1e-06
NEG_FILL = -1e30


def assign_slots(route_rows, experts):
    flat_routes = route_rows.reshape(-1)
    one_hot = (flat_routes[:, None] == jnp.arange(experts, dtype=jnp.int32)[None, :]).astype(
        jnp.int32
    )
    running = jnp.cumsum(one_hot, axis=0)
    slot_rank = jnp.sum(running * one_hot, axis=1) - 1
    return slot_rank.reshape(route_rows.shape)


def dispatch_matrix(route_rows, slot_rows, experts, capacity):
    target = route_rows * capacity + slot_rows
    places = jnp.arange(experts * capacity, dtype=jnp.int32)
    total = jnp.zeros((route_rows.shape[0], experts * capacity), jnp.bfloat16)
    for column in range(route_rows.shape[1]):
        total = total + (target[:, column][:, None] == places[None, :]).astype(jnp.bfloat16)
    return total


MESH_ID = pl.DeviceIdType.MESH


def gather_kernel(nx, nz, shard_ref, out_ref, xs_sem, xr_sem, own_sem, rs_sem, ls_sem, rr_sem):
    d = lax.axis_index("dp")
    e = lax.axis_index("expert")
    x = e // nz
    z = e % nz
    right = x * nz + (z + 1) % nz
    left = x * nz + (z + nz - 1) % nz
    steps_r = nz // 2
    steps_l = nz - 1 - steps_r

    barrier = pltpu.get_barrier_semaphore()
    for k in range(1, nx):
        peer = ((x + k) % nx) * nz + z
        pl.semaphore_signal(barrier, 1, device_id=(d, peer), device_id_type=MESH_ID)
    greeted = nx - 1
    if nz > 1:
        pl.semaphore_signal(barrier, 1, device_id=(d, right), device_id_type=MESH_ID)
        greeted += 1
    if nz > 2:
        pl.semaphore_signal(barrier, 1, device_id=(d, left), device_id_type=MESH_ID)
        greeted += 1
    if greeted:
        pl.semaphore_wait(barrier, greeted)

    own = pltpu.make_async_copy(shard_ref, out_ref.at[x, z], own_sem)
    own.start()
    x_copies = []
    for k in range(1, nx):
        px = (x + k) % nx
        send = pltpu.make_async_remote_copy(
            src_ref=shard_ref,
            dst_ref=out_ref.at[x, z],
            send_sem=xs_sem.at[k],
            recv_sem=xr_sem.at[x],
            device_id=(d, px * nz + z),
            device_id_type=MESH_ID,
        )
        send.start()
        x_copies.append(send)
    own.wait()
    for k in range(1, nx):
        px = (x + k) % nx
        incoming = pltpu.make_async_remote_copy(
            src_ref=shard_ref,
            dst_ref=out_ref.at[px, z],
            send_sem=xs_sem.at[k],
            recv_sem=xr_sem.at[px],
            device_id=(d, px * nz + z),
            device_id_type=MESH_ID,
        )
        incoming.wait_recv()

    def ring_copy(group, sems, step, target):
        return pltpu.make_async_remote_copy(
            src_ref=out_ref.at[:, group],
            dst_ref=out_ref.at[:, group],
            send_sem=sems.at[step],
            recv_sem=rr_sem.at[group],
            device_id=(d, target),
            device_id_type=MESH_ID,
        )

    sent = []
    for s in range(max(steps_r, steps_l)):
        if s < steps_r:
            group = (z - s + nz) % nz
            if s > 0:
                ring_copy(group, rs_sem, s, right).wait_recv()
            c = ring_copy(group, rs_sem, s, right)
            c.start()
            sent.append(c)
        if s < steps_l:
            group = (z + s) % nz
            if s > 0:
                ring_copy(group, ls_sem, s, left).wait_recv()
            c = ring_copy(group, ls_sem, s, left)
            c.start()
            sent.append(c)
    if steps_r > 0:
        ring_copy((z - steps_r + nz) % nz, rs_sem, 0, right).wait_recv()
    if steps_l > 0:
        ring_copy((z + steps_l) % nz, ls_sem, 0, left).wait_recv()
    for c in sent:
        c.wait_send()
    for c in x_copies:
        c.wait_send()


def expert_gather(flat, members):
    nz = 16 if members % 16 == 0 else members
    nx = members // nz
    rows, lanes = flat.shape
    steps = max(nz // 2, 1)
    out = pl.pallas_call(
        partial(gather_kernel, nx, nz),
        out_shape=jax.ShapeDtypeStruct((nx, nz, rows, lanes), flat.dtype),
        in_specs=[pl.BlockSpec(memory_space=pltpu.VMEM)],
        out_specs=pl.BlockSpec(memory_space=pltpu.VMEM),
        scratch_shapes=[
            pltpu.SemaphoreType.DMA((max(nx, 1),)),
            pltpu.SemaphoreType.DMA((max(nx, 1),)),
            pltpu.SemaphoreType.DMA(()),
            pltpu.SemaphoreType.DMA((steps,)),
            pltpu.SemaphoreType.DMA((steps,)),
            pltpu.SemaphoreType.DMA((nz,)),
        ],
        compiler_params=pltpu.CompilerParams(collective_id=0, has_side_effects=True),
    )(flat)
    return out.reshape(members, rows * lanes)


def gather_weights(members, by_kernel, **parts):
    names = list(parts)
    flat = jnp.concatenate([parts[n][0].reshape(-1) for n in names])
    lanes = 128
    total = flat.shape[0]
    padded = -(-total // (lanes * 8)) * lanes * 8
    flat = jnp.pad(flat, (0, padded - total)).reshape(padded // lanes, lanes)
    if by_kernel:
        everyone = expert_gather(flat, members)
    else:
        everyone = lax.all_gather(flat[None], "expert", axis=0, tiled=True)
        everyone = everyone.reshape(members, padded)
    out = {}
    start = 0
    for n in names:
        local, axis = parts[n]
        size = local.size
        piece = everyone[:, start : start + size].reshape((members,) + local.shape)
        piece = jnp.moveaxis(piece, 0, axis)
        shape = list(local.shape)
        shape[axis] *= members
        out[n] = piece.reshape(shape)
        start += size
    return out


def shards(
    pre_query,
    pre_latent,
    pre_resid,
    dec_query,
    dec_latent,
    dec_resid,
    cache_lengths,
    latent_cache,
    sink_logits,
    uv_weight,
    out_weight,
    norm_gain,
    router,
    routes,
    gate_weight,
    up_weight,
    down_weight,
    shared_gate,
    shared_up,
    shared_down,
):
    groups = lax.axis_size("dp")
    members = lax.axis_size("expert")
    pre_rows = pre_query.shape[0]
    rows_dev = pre_rows + 1
    scale_qk = (QK_NOPE + ROPE) ** (-0.5)
    weights = gather_weights(
        members,
        True,
        uv=(uv_weight, 1),
        out=(out_weight, 1),
        shared_gate=(shared_gate, 0),
        shared_up=(shared_up, 0),
        shared_down=(shared_down, 0),
        router=(router, 1),
    )
    pre_scores = (
        jnp.einsum("thc,uc->thu", pre_query, pre_latent, preferred_element_type=jnp.float32)
        * scale_qk
    )
    places = jnp.arange(pre_rows, dtype=jnp.int32)
    allowed = (places[None, :] <= places[:, None])[:, None, :]
    masked = jnp.where(allowed, pre_scores, NEG_FILL)
    pre_max = jnp.maximum(jnp.max(masked, axis=2), sink_logits[None, :])
    exp_terms = jnp.where(allowed, jnp.exp(masked - pre_max[:, :, None]), 0.0)
    denominator = jnp.sum(exp_terms, axis=2) + jnp.exp(sink_logits[None, :] - pre_max)
    numerator = jnp.einsum(
        "thu,ul->thl",
        exp_terms.astype(jnp.bfloat16),
        pre_latent[:, :LATENT],
        preferred_element_type=jnp.float32,
    )
    pre_att = (numerator / denominator[:, :, None]).astype(jnp.bfloat16)
    window = latent_cache.shape[1]
    slot_ids = jnp.arange(window, dtype=jnp.int32)
    newest = cache_lengths - 1
    position = newest[:, None] - jnp.mod(newest[:, None] - slot_ids[None, :], window)
    usable = ((position >= 0) & (position > cache_lengths[:, None] - window))[:, None, :]
    cache_scores = (
        jnp.einsum("rhc,rsc->rhs", dec_query, latent_cache, preferred_element_type=jnp.float32)
        * scale_qk
    )
    own_scores = (
        jnp.einsum("rhc,rc->rh", dec_query, dec_latent, preferred_element_type=jnp.float32)
        * scale_qk
    )
    cache_masked = jnp.where(usable, cache_scores, NEG_FILL)
    top_score = jnp.maximum(
        jnp.maximum(jnp.max(cache_masked, axis=2), own_scores), sink_logits[None, :]
    )
    cache_exp = jnp.where(usable, jnp.exp(cache_masked - top_score[:, :, None]), 0.0)
    own_exp = jnp.exp(own_scores - top_score)
    dec_numer = jnp.einsum(
        "rhs,rsl->rhl",
        cache_exp.astype(jnp.bfloat16),
        latent_cache[:, :, :LATENT],
        preferred_element_type=jnp.float32,
    )
    dec_numer = dec_numer + own_exp.astype(jnp.bfloat16).astype(jnp.float32)[
        :, :, None
    ] * dec_latent[:, None, :LATENT].astype(jnp.float32)
    dec_total = jnp.sum(cache_exp, axis=2) + own_exp + jnp.exp(sink_logits[None, :] - top_score)
    dec_att = (dec_numer / dec_total[:, :, None]).astype(jnp.bfloat16)
    attention = jnp.concatenate([pre_att, dec_att], axis=0)
    spread = lax.all_to_all(attention, "dp", split_axis=1, concat_axis=0, tiled=True)
    uv_full, out_full = weights["uv"], weights["out"]
    head_values = jnp.einsum(
        "thl,hlv->thv", spread, uv_full, preferred_element_type=jnp.float32
    ).astype(jnp.bfloat16)
    head_partial = jnp.einsum(
        "thv,hvd->td", head_values, out_full, preferred_element_type=jnp.float32
    )
    attn_out = lax.psum_scatter(
        head_partial.astype(jnp.bfloat16), "dp", scatter_dimension=0, tiled=True
    ).astype(jnp.float32)
    resid = jnp.concatenate([pre_resid, dec_resid], axis=0)
    hidden = (resid.astype(jnp.float32) + attn_out).astype(jnp.bfloat16)
    hidden_up = lax.optimization_barrier(hidden).astype(jnp.float32)
    mean_square = jnp.mean(hidden_up * hidden_up, axis=1, keepdims=True)
    normed = (
        hidden_up * lax.rsqrt(mean_square + NORM_EPS) * norm_gain.astype(jnp.float32)[None, :]
    ).astype(jnp.bfloat16)
    capacity = max(2, (rows_dev * TOPK + members - 1) // members)
    route_row = routes.astype(jnp.bfloat16).reshape(1, rows_dev * TOPK)
    route_row = jnp.pad(route_row, ((0, 0), (0, D - rows_dev * TOPK)))
    own_slots = assign_slots(routes, members)
    own_matrix = dispatch_matrix(routes, own_slots, members, capacity).reshape(
        rows_dev, members, capacity
    )
    outgoing = jnp.einsum("rxc,rd->xcd", own_matrix, normed, preferred_element_type=jnp.bfloat16)
    arrived = lax.all_to_all(outgoing, "expert", split_axis=0, concat_axis=0, tiled=True)
    shared_ready = (
        weights["shared_gate"],
        weights["shared_up"],
        weights["shared_down"],
        weights["router"],
    )
    expert_rows = lax.all_gather(
        arrived.reshape(members, 1, capacity, D), "dp", axis=1, tiled=True
    )
    expert_rows = expert_rows.reshape(-1, D)
    own_both, _ = lax.optimization_barrier(
        (jnp.concatenate([normed, route_row], axis=0), arrived)
    )
    group_both = lax.all_gather(own_both[None], "dp", axis=0, tiled=True)
    expert_rows, group_both = lax.optimization_barrier((expert_rows, group_both))
    group_tokens = group_both[:, :rows_dev].reshape(groups * rows_dev, D)
    group_routes = (
        group_both[:, rows_dev, : rows_dev * TOPK].astype(jnp.int32).reshape(-1, TOPK)
    )
    routes_by_group = group_routes.reshape(groups, rows_dev, TOPK)
    slots_by_group = jax.vmap(partial(assign_slots, experts=members))(routes_by_group)
    gate_proj = jnp.dot(expert_rows, gate_weight[0], preferred_element_type=jnp.float32)
    up_proj = jnp.dot(expert_rows, up_weight[0], preferred_element_type=jnp.float32)
    expert_act = (jax.nn.silu(gate_proj) * up_proj).astype(jnp.bfloat16)
    shared_gate_full, shared_up_full, shared_down_full, router_full = shared_ready
    shared_act = (
        jax.nn.silu(jnp.dot(group_tokens, shared_gate_full, preferred_element_type=jnp.float32))
        * jnp.dot(group_tokens, shared_up_full, preferred_element_type=jnp.float32)
    ).astype(jnp.bfloat16)
    down_local = down_weight[0]
    col_width = down_local.shape[1]
    routed_piece = lax.all_gather(expert_act, "dp", axis=1, tiled=True)
    shared_piece = lax.all_gather(shared_act, "dp", axis=1, tiled=True)
    routed_cols = jnp.dot(routed_piece, down_local, preferred_element_type=jnp.float32)
    shared_cols = jnp.dot(shared_piece, shared_down_full, preferred_element_type=jnp.float32)
    expert_out = routed_cols.astype(jnp.bfloat16)
    shared_out = shared_cols.astype(jnp.bfloat16)
    returned = lax.all_to_all(
        expert_out.reshape(members, groups * capacity, col_width),
        "expert",
        split_axis=0,
        concat_axis=0,
        tiled=True,
    )
    group_offset = (jnp.arange(groups, dtype=jnp.int32) * capacity)[:, None, None]
    lookup = (routes_by_group * (groups * capacity) + group_offset + slots_by_group).reshape(
        groups * rows_dev, TOPK
    )
    picked = jnp.take(returned.reshape(-1, col_width), lookup, axis=0)
    group_logits = jnp.dot(group_tokens, router_full, preferred_element_type=jnp.float32)
    picked_scores = jax.nn.sigmoid(
        jnp.take_along_axis(group_logits, group_routes.reshape(-1, TOPK), axis=1)
    )
    route_weight = ROUTE_SCALE * picked_scores / jnp.sum(picked_scores, axis=1, keepdims=True)
    moe_cols = shared_out.astype(jnp.float32) + jnp.sum(
        route_weight[:, :, None] * picked.astype(jnp.float32), axis=1
    )
    moe_home = lax.all_to_all(
        moe_cols.reshape(groups, rows_dev, col_width).astype(jnp.bfloat16),
        "dp",
        split_axis=0,
        concat_axis=2,
        tiled=True,
    ).astype(jnp.float32)
    final = (hidden_up + moe_home[0]).astype(jnp.bfloat16)
    return (final[:pre_rows], final[pre_rows:])


def solution(mesh):
    in_specs = (
        P(("dp", "expert"), None, None),
        P(("dp", "expert"), None),
        P(("dp", "expert"), None),
        P(("dp", "expert"), None, None),
        P(("dp", "expert"), None),
        P(("dp", "expert"), None),
        P(("dp", "expert")),
        P(("dp", "expert"), None, None),
        P(),
        P("dp", "expert", None),
        P("dp", "expert", None),
        P(),
        P(None, "expert"),
        P(("dp", "expert"), None),
        P("expert", None, "dp"),
        P("expert", None, "dp"),
        P("expert", None, "dp"),
        P("expert", "dp"),
        P("expert", "dp"),
        P("expert", "dp"),
    )
    out_specs = (P(("dp", "expert"), None), P(("dp", "expert"), None))
    return jax.shard_map(shards, mesh=mesh, in_specs=in_specs, out_specs=out_specs, check_vma=False)
```
